32 devices in a mesh: dp: 8 (over z, y), seq: 4 (over x, core).
Axes of the slice: x: 2, y: 2, z: 4, core: 2. Of those that a mesh axis runs over, the one named last changes fastest.
Arguments:
- inputs: bfloat16 [16, 1024, 768], P('dp', 'seq'), may hold values from -6 to 6
- lengths: int32 [16], P('dp'), may hold values from 512 to 1024, as said below
- query_weight: bfloat16 [768, 768], P('dp'), may hold values from -0.3125 to 0.3125
- key_weight: bfloat16 [768, 768], P('dp'), may hold values from -0.3125 to 0.3125
- value_weight: bfloat16 [768, 768], P('dp'), may hold values from -0.21875 to 0.21875
- output_weight: bfloat16 [768, 768], P('dp'), may hold values from -0.625 to 0.625
- up_weight: bfloat16 [768, 3072], P('dp'), may hold values from -0.21875 to 0.21875
- down_weight: bfloat16 [3072, 768], P('dp'), may hold values from -0.15625 to 0.15625
- query_bias: bfloat16 [768], P('dp'), may hold values from -3 to 3
- value_bias: bfloat16 [768], P('dp'), may hold values from -3 to 3
- output_bias: bfloat16 [768], P('dp'), may hold values from -3 to 3
- up_bias: bfloat16 [3072], P('dp'), may hold values from -3 to 3
- down_bias: bfloat16 [768], P('dp'), may hold values from -3 to 3
- first_gain: bfloat16 [768], P('dp'), may hold values from 0.5 to 1.5
- first_shift: bfloat16 [768], P('dp'), may hold values from -2 to 2
- second_gain: bfloat16 [768], P('dp'), may hold values from 0.5 to 1.5
- second_shift: bfloat16 [768], P('dp'), may hold values from -2 to 2
- cotangent: bfloat16 [16, 1024, 768], P('dp', 'seq'), may hold values from -6 to 6
Outputs:
- layer_out: bfloat16 [16, 1024, 768], P('dp', 'seq')
- input_grad: bfloat16 [16, 1024, 768], P('dp', 'seq')
- query_weight_grad: float32 [768, 768], P('dp')
- key_weight_grad: float32 [768, 768], P('dp')
- value_weight_grad: float32 [768, 768], P('dp')
- output_weight_grad: float32 [768, 768], P('dp')
- up_weight_grad: float32 [768, 3072], P('dp')
- down_weight_grad: float32 [3072, 768], P('dp')
- query_bias_grad: float32 [768], P('dp')
- value_bias_grad: float32 [768], P('dp')
- output_bias_grad: float32 [768], P('dp')
- up_bias_grad: float32 [3072], P('dp')
- down_bias_grad: float32 [768], P('dp')
- first_gain_grad: float32 [768], P('dp')
- first_shift_grad: float32 [768], P('dp')
- second_gain_grad: float32 [768], P('dp')
- second_shift_grad: float32 [768], P('dp')
The draws below stay inside these ranges and needn't reach their ends.
Inputs may be any that keep to these rules, and one draw needn't show every extreme that they name: `lengths`: the number of real tokens of each sequence; its later positions up to 1024 are padding.
All inputs are finite; a program needn't handle non-finite values.
Results may differ from the reference program's by a relative error of at most 0.015.
Values may be sent and summed in bfloat16 or wider, within the bound.
A program may use at most 192 MiB of HBM per device.

```python
import jax
import jax.numpy as jnp
from jax import lax

D = 768
HEADS = 12
HEAD_DIM = 64
FF = 3072
SEQ_LEN = 1024
SEQS = 16


def draw_lengths(key, part):
    first_key, second_key, third_key = jax.random.split(key, 3)
    drawn_lengths = jax.random.randint(first_key, (SEQS,), SEQ_LEN // 2, SEQ_LEN + 1)
    longest_at = jax.random.randint(second_key, (), 0, SEQS)
    shortest_at = (longest_at + 1 + jax.random.randint(third_key, (), 0, max(SEQS - 1, 1))) % SEQS
    indices = jnp.arange(SEQS)
    drawn_lengths = jnp.where(indices == shortest_at, SEQ_LEN // 2, drawn_lengths)
    drawn_lengths = jnp.where(indices == longest_at, SEQ_LEN, drawn_lengths)
    return drawn_lengths.astype(jnp.int32)


def shard_levels(key, extent, cuts, smallest, largest):
    level, own = 1.0, jax.random.fold_in(key, 6)
    for dim, blocks in cuts:
        steps = jnp.exp(jax.random.uniform(jax.random.fold_in(own, dim), (blocks,), jnp.float32, smallest / len(cuts), largest / len(cuts)))
        level = level * jnp.repeat(steps, extent[dim] // blocks).reshape([-1 if axis == dim else 1 for axis in range(len(extent))])
    return level


def scatter_about(key, shape, width, bound, pieces=(), kind=jnp.bfloat16):
    gain = shard_levels(key, shape, pieces, -0.22, 0.18) if pieces else 1.0
    array = jax.random.normal(key, shape, jnp.float32) * width * gain
    return jnp.minimum(jnp.maximum(array, -bound), bound).astype(kind)


def setup_inputs(seed: int = 0) -> dict:
    seeds = jax.random.split(jax.random.key(seed), 19)
    inputs = scatter_about(seeds[0], (SEQS, SEQ_LEN, D), 1.0, 6.0, ((0, 8), (1, 4)))
    lengths = draw_lengths(jax.random.fold_in(seeds[18], 71), 0)
    query_weight = scatter_about(seeds[2], (D, D), (D // 2) ** -0.5, 0.3125, ((0, 8),))
    key_weight = scatter_about(seeds[3], (D, D), (D // 2) ** -0.5, 0.3125, ((0, 8),))
    value_weight = scatter_about(seeds[4], (D, D), D ** -0.5, 0.21875, ((0, 8),))
    output_weight = scatter_about(seeds[5], (D, D), (D // 8) ** -0.5, 0.625, ((0, 8),))
    up_weight = scatter_about(seeds[6], (D, FF), D ** -0.5, 0.21875, ((0, 8),))
    down_weight = scatter_about(seeds[7], (FF, D), (FF // 2) ** -0.5, 0.15625, ((0, 8),))
    query_bias = scatter_about(seeds[8], (D,), 0.5, 3.0, ((0, 8),))
    value_bias = scatter_about(seeds[9], (D,), 0.5, 3.0, ((0, 8),))
    output_bias = scatter_about(seeds[10], (D,), 0.5, 3.0, ((0, 8),))
    up_bias = scatter_about(seeds[11], (FF,), 0.5, 3.0, ((0, 8),))
    down_bias = scatter_about(seeds[12], (D,), 0.5, 3.0, ((0, 8),))
    first_gain = jnp.clip(1.0 + 0.1 * jax.random.normal(seeds[13], (D,), jnp.float32), 0.5, 1.5).astype(jnp.bfloat16)
    first_shift = scatter_about(seeds[14], (D,), 0.3, 2.0, ((0, 8),))
    second_gain = jnp.clip(1.0 + 0.1 * jax.random.normal(seeds[15], (D,), jnp.float32), 0.5, 1.5).astype(jnp.bfloat16)
    second_shift = scatter_about(seeds[16], (D,), 0.3, 2.0, ((0, 8),))
    cotangent = scatter_about(seeds[17], (SEQS, SEQ_LEN, D), 1.0, 6.0, ((0, 8), (1, 4)))
    return dict(inputs=inputs, lengths=lengths, query_weight=query_weight, key_weight=key_weight, value_weight=value_weight, output_weight=output_weight, up_weight=up_weight, down_weight=down_weight, query_bias=query_bias, value_bias=value_bias, output_bias=output_bias, up_bias=up_bias, down_bias=down_bias, first_gain=first_gain, first_shift=first_shift, second_gain=second_gain, second_shift=second_shift, cotangent=cotangent)


@jax.custom_vjp
def low(v):
    return lax.optimization_barrier(v.astype(jnp.bfloat16)).astype(jnp.float32)

@jax.custom_vjp
def low_back(v):
    return v

def low_keep(v):
    return (low(v), None)

def low_pass(kept, grad):
    return (grad,)

def back_keep(v):
    return (v, None)

def back_low(kept, grad):
    return (low(grad),)
low.defvjp(low_keep, low_pass)
low_back.defvjp(back_keep, back_low)
eps_norm = 1e-05
masked_score = -1000000000.0
highest = lax.Precision.HIGHEST

def layer_norm(hidden, gain_vec, shift_vec):
    row_mean = lax.optimization_barrier(jnp.mean(hidden, axis=-1, keepdims=True))
    centred = hidden - row_mean
    row_var = lax.optimization_barrier(jnp.mean(centred * centred, axis=-1, keepdims=True))
    return centred * lax.rsqrt(row_var + eps_norm) * gain_vec + shift_vec

def forward(params, seq_in, length):
    query_weight, key_weight, value_weight, output_weight, up_weight, down_weight, query_bias, value_bias, output_bias, up_bias, down_bias, first_gain, first_shift, second_gain, second_shift = params
    seq_len = seq_in.shape[0]
    queries = low_back(low(jnp.dot(seq_in, query_weight, precision=highest) + query_bias))
    key_rows = low_back(low(jnp.dot(seq_in, key_weight, precision=highest)))
    value_rows = low_back(low(jnp.dot(seq_in, value_weight, precision=highest) + value_bias))
    head_q = queries.reshape(seq_len, HEADS, HEAD_DIM)
    head_k = key_rows.reshape(seq_len, HEADS, HEAD_DIM)
    head_v = value_rows.reshape(seq_len, HEADS, HEAD_DIM)
    scores = low_back(jnp.einsum('qhd,khd->hqk', head_q, head_k, precision=highest) * HEAD_DIM ** (-0.5))
    key_live = jnp.arange(seq_len) < length
    scores = jnp.where(key_live[None, None, :], scores, masked_score)
    probabilities = low(jax.nn.softmax(scores, axis=-1))
    context = jnp.einsum('hqk,khd->qhd', probabilities, head_v, precision=highest).reshape(seq_len, D)
    context = low_back(low(context))
    attended = low_back(jnp.dot(context, output_weight, precision=highest) + output_bias)
    first_norm = low(layer_norm(seq_in + attended, first_gain, first_shift))
    up_pre = low_back(jnp.dot(first_norm, up_weight, precision=highest) + up_bias)
    hidden_act = low(jax.nn.gelu(up_pre, approximate=False))
    down_out = low_back(jnp.dot(hidden_act, down_weight, precision=highest) + down_bias)
    return layer_norm(first_norm + down_out, second_gain, second_shift)

def reference(inputs, lengths, query_weight, key_weight, value_weight, output_weight, up_weight, down_weight, query_bias, value_bias, output_bias, up_bias, down_bias, first_gain, first_shift, second_gain, second_shift, cotangent):
    params = tuple((param_arr.astype(jnp.float32) for param_arr in (query_weight, key_weight, value_weight, output_weight, up_weight, down_weight, query_bias, value_bias, output_bias, up_bias, down_bias, first_gain, first_shift, second_gain, second_shift)))
    seq_len = inputs.shape[1]

    def one_sequence(running, operands):
        seq_in, seq_cot, length = operands
        live_rows = (jnp.arange(seq_len) < length).astype(jnp.float32)

        def apply_layer(param_set, layer_in):
            return forward(param_set, layer_in, length)
        result, pullback = jax.vjp(apply_layer, params, seq_in.astype(jnp.float32))
        param_grads, seq_grad = pullback(seq_cot.astype(jnp.float32) * live_rows[:, None])
        running = jax.tree.map(lambda total_val, new_val: total_val + new_val, running, param_grads)
        return (running, (result.astype(jnp.bfloat16), seq_grad.astype(jnp.bfloat16)))
    zeros_init = jax.tree.map(jnp.zeros_like, params)
    totals, outputs = lax.scan(one_sequence, zeros_init, (inputs, cotangent, lengths))
    layer_out, input_grad = outputs
    return (layer_out, input_grad, totals[0], totals[1], totals[2], totals[3], totals[4], totals[5], totals[6], totals[7], totals[8], totals[9], totals[10], totals[11], totals[12], totals[13], totals[14])
```

```python
import functools
import jax
import jax.numpy as jnp
from jax import lax
from jax.experimental import pallas as pl
from jax.experimental.pallas import tpu as pltpu
from jax.sharding import PartitionSpec as P

MESH = pl.DeviceIdType.MESH
HEAD_DIM = 64
eps_norm = 1e-05
masked_score = -1000000000.0


def flip(value, bits):
    bit = 1
    while bit <= bits:
        if bits & bit:
            value = value + bit - 2 * bit * lax.rem(lax.div(value, bit), 2)
        bit *= 2
    return value


class Place:
    def __init__(self, dp_size):
        self.dp = lax.axis_index("dp")
        self.seq = lax.axis_index("seq")
        self.depth = dp_size // 2
        self.z = lax.div(self.dp, 2)
        self.y = lax.rem(self.dp, 2)
        self.core = lax.rem(self.seq, 2)
        self.side = lax.div(self.seq, 2)

    def along_z(self, k):
        return flip(self.dp, 2 * k)

    def peers(self):
        result = [(self.along_z(k), self.seq) for k in range(1, self.depth)]
        result.append((flip(self.dp, 1), self.seq))
        result.append((self.dp, flip(self.seq, 1)))
        result.append((self.dp, flip(self.seq, 2)))
        return result

    def greet(self):
        barrier = pltpu.get_barrier_semaphore()
        peers = self.peers()
        for peer in peers:
            pl.semaphore_signal(barrier, inc=1, device_id=peer, device_id_type=MESH)
        pl.semaphore_wait(barrier, len(peers))


class Gather:
    def __init__(self, place, src, dst, rows, columns, to_columns, sems):
        self.place, self.src, self.dst = place, src, dst
        self.columns, self.to_columns = columns, to_columns
        self.first, count = rows
        self.send, self.recv, self.local = sems
        self.depth = place.depth
        unit = count // 6
        self.fetch = (place.core * (3 * unit) + place.side * unit, 2 * unit)
        self.far = (place.core * (3 * unit) + place.side * (2 * unit), unit)
        self.got = (place.core * (3 * unit) + (1 - place.side) * (2 * unit), unit)
        self.half = (place.core * (3 * unit), 3 * unit)

    def view(self, z, y, window):
        rows = pl.ds(pl.multiple_of(self.first + window[0], window[1] if window[1] < 32 else 16), window[1])
        return self.dst.at[z, y, rows, pl.ds(*self.to_columns)]

    def copy(self, src, dst, index, peer):
        return pltpu.make_async_remote_copy(
            src_ref=src, dst_ref=dst, send_sem=self.send.at[index], recv_sem=self.recv.at[index],
            device_id=peer, device_id_type=MESH,
        )

    def mine(self):
        rows = pl.ds(pl.multiple_of(self.first + self.fetch[0], 16), self.fetch[1])
        return self.src.at[rows, pl.ds(*self.columns)]

    def own(self):
        p = self.place
        return pltpu.make_async_copy(self.mine(), self.view(p.z, p.y, self.fetch), self.local)

    def over_z(self, k):
        p = self.place
        return self.copy(self.mine(), self.view(p.z, p.y, self.fetch), k, (p.along_z(k), p.seq))

    def over_y(self):
        p = self.place
        ref = self.view(slice(None), p.y, self.fetch)
        return self.copy(ref, ref, 0, (flip(p.dp, 1), p.seq))

    def over_x(self):
        p, every = self.place, slice(None)
        ref = self.view(every, every, self.far)
        return self.copy(ref, ref, self.depth, (p.dp, flip(p.seq, 2)))

    def across(self):
        p, every = self.place, slice(None)
        ref = self.view(every, every, self.half)
        return self.copy(ref, ref, self.depth + 1, (p.dp, flip(p.seq, 1)))

    def stage_z(self):
        self.own().start()
        for k in range(1, self.depth):
            self.over_z(k).start()

    def stage_y(self):
        self.own().wait()
        for k in range(1, self.depth):
            self.over_z(k).wait_recv()
        self.over_y().start()

    def stage_x(self):
        self.over_y().wait_recv()
        self.over_x().start()

    def stage_core(self):
        self.over_x().wait_recv()
        self.across().start()

    def finish(self):
        for k in range(1, self.depth):
            self.over_z(k).wait_send()
        self.over_y().wait_send()
        self.over_x().wait_send()
        self.across().wait()


def gather_sems(dp_size, units):
    n = dp_size // 2 + 2
    return [pltpu.SemaphoreType.DMA((units, n)), pltpu.SemaphoreType.DMA((units, n)), pltpu.SemaphoreType.DMA((units,))]


class Spread:
    def __init__(self, place, src, dst, sems):
        self.place, self.src, self.dst = place, src, dst
        self.send, self.recv, self.local = sems

    def own(self):
        return pltpu.make_async_copy(self.src, self.dst.at[self.place.z, self.place.y], self.local)

    def over_z(self, k):
        p = self.place
        return pltpu.make_async_remote_copy(
            src_ref=self.src, dst_ref=self.dst.at[p.z, p.y], send_sem=self.send.at[k], recv_sem=self.recv.at[k],
            device_id=(p.along_z(k), p.seq), device_id_type=MESH,
        )

    def over_y(self):
        p = self.place
        ref = self.dst.at[:, p.y]
        return pltpu.make_async_remote_copy(
            src_ref=ref, dst_ref=ref, send_sem=self.send.at[0], recv_sem=self.recv.at[0],
            device_id=(flip(p.dp, 1), p.seq), device_id_type=MESH,
        )

    def start(self):
        self.own().start()
        for k in range(1, self.place.depth):
            self.over_z(k).start()

    def forward(self):
        self.own().wait()
        for k in range(1, self.place.depth):
            self.over_z(k).wait_recv()
        self.over_y().start()

    def finish(self):
        for k in range(1, self.place.depth):
            self.over_z(k).wait_send()
        self.over_y().wait()


def gather_steps(units, window):
    count = len(units)
    steps = [[unit.stage_z for unit in units[:window]]]
    for i in range(count + 4):
        step = []
        if 0 <= i - 4 < count:
            step.append(units[i - 4].stage_core)
        if 0 <= i - 2 < count:
            step.append(units[i - 2].stage_x)
        if i < count:
            step.append(units[i].stage_y)
            if i + window < count:
                step.append(units[i + window].stage_z)
        steps.append(step)
    steps.append([unit.finish for unit in units])
    return steps


class Swap:
    def __init__(self, place, src, dst, send, recv, local):
        side = place.side
        length = src.shape[1]
        own = dst.at[pl.ds(pl.multiple_of(side * length, 8), length)]
        self.here = pltpu.make_async_copy(src.at[side], own, local)
        self.there = pltpu.make_async_remote_copy(
            src_ref=src.at[1 - side], dst_ref=own, send_sem=send, recv_sem=recv,
            device_id=(place.dp, flip(place.seq, 2)), device_id_type=MESH,
        )

    def start(self):
        self.here.start()
        self.there.start()

    def wait(self):
        self.here.wait()
        self.there.wait()


def weight_units(place, srcs, dsts, plan, sems):
    send, recv, local = sems
    return [
        Gather(place, srcs[s], dsts[d], (first, rows), (column, width), (to, width), (send.at[i], recv.at[i], local.at[i]))
        for i, (s, d, first, rows, column, width, to) in enumerate(plan)
    ]


def first_kernel(dp_size, plan, n_src, n_dst, n_rows, window, *refs):
    refs = list(refs)
    srcs, vec, rows_in = refs[:n_src], refs[n_src], refs[n_src + 1:n_src + 1 + n_rows]
    refs = refs[n_src + 1 + n_rows:]
    dsts, vec_out, rows_out = refs[:n_dst], refs[n_dst], refs[n_dst + 1:n_dst + 1 + n_rows]
    send, recv, local, vec_send, vec_recv, swap_sem, vec_local = refs[n_dst + 1 + n_rows:]
    place = Place(dp_size)
    place.greet()
    moves = [Swap(place, a, b, swap_sem.at[i, 0], swap_sem.at[i, 1], swap_sem.at[i, 2]) for i, (a, b) in enumerate(zip(rows_in, rows_out))]
    spread = Spread(place, vec, vec_out, (vec_send, vec_recv, vec_local))
    units = weight_units(place, srcs, dsts, plan, (send, recv, local))
    spread.start()
    for move in moves:
        move.start()
    steps = gather_steps(units, window)
    for call in steps[0]:
        call()
    spread.forward()
    for step in steps[1:]:
        for call in step:
            call()
    spread.finish()
    for move in moves:
        move.wait()


def first_exchange(dp_size, weights, dst_shapes, plan, vec, rows, window=3):
    n_src, n_dst = len(weights), len(dst_shapes)
    anywhere = pl.BlockSpec(memory_space=pl.ANY)
    z = dp_size // 2
    out_shape = [jax.ShapeDtypeStruct((z, 2, *shape), jnp.bfloat16) for shape in dst_shapes]
    out_shape += [jax.ShapeDtypeStruct((z, 2, *vec.shape), vec.dtype)]
    out_shape += [jax.ShapeDtypeStruct((r.shape[0] * r.shape[1], r.shape[2]), r.dtype) for r in rows]
    return pl.pallas_call(
        functools.partial(first_kernel, dp_size, plan, n_src, n_dst, len(rows), window),
        out_shape=out_shape,
        in_specs=[anywhere] * (n_src + 1 + len(rows)),
        out_specs=[anywhere] * (n_dst + 1 + len(rows)),
        scratch_shapes=gather_sems(dp_size, len(plan)) + [pltpu.SemaphoreType.DMA((z,))] * 2 + [pltpu.SemaphoreType.DMA((len(rows), 3)), pltpu.SemaphoreType.DMA],
        compiler_params=pltpu.CompilerParams(collective_id=0, has_side_effects=True),
        name="first_exchange",
    )(*weights, vec, *rows)


class Reduce:
    def __init__(self, place, src, rows, columns, to_columns, out, to_row, bufs, sems):
        self.place, self.src, self.out = place, src, out
        self.columns, self.to_columns, self.to_row = columns, to_columns, to_row
        self.first, count = rows
        self.unit = unit = count // 6
        self.own, self.from_core, self.to_x, self.from_x, self.to_y, self.from_y, self.to_z, self.from_z, self.last, self.got, self.total = bufs
        self.send, self.recv = sems
        self.depth = place.depth
        self.half = place.core * (3 * unit)
        self.sibling_half = (1 - place.core) * (3 * unit)

    def view(self, start):
        rows = pl.ds(pl.multiple_of(self.first + start, self.unit), 3 * self.unit)
        return self.src.at[:, :, rows, pl.ds(*self.columns)]

    def copy(self, src, dst, index, peer):
        return pltpu.make_async_remote_copy(
            src_ref=src, dst_ref=dst, send_sem=self.send.at[index], recv_sem=self.recv.at[index],
            device_id=peer, device_id_type=MESH,
        )

    def load(self):
        return pltpu.make_async_copy(self.view(self.half), self.own, self.send.at[0])

    def core(self):
        p = self.place
        return self.copy(self.view(self.sibling_half), self.from_core, self.depth, (p.dp, flip(p.seq, 1)))

    def x(self):
        p = self.place
        return self.copy(self.to_x, self.from_x, self.depth + 1, (p.dp, flip(p.seq, 2)))

    def y(self):
        p = self.place
        return self.copy(self.to_y, self.from_y, self.depth + 2, (flip(p.dp, 1), p.seq))

    def z(self, k):
        p = self.place
        return self.copy(self.to_z.at[k - 1], self.from_z.at[k - 1], k, (p.along_z(k), p.seq))

    def x_last(self):
        p = self.place
        return self.copy(self.last, self.got, self.depth + 3, (p.dp, flip(p.seq, 2)))

    def place_out(self):
        row = pl.multiple_of(self.to_row + self.half, self.unit)
        return self.out.at[pl.ds(row, 3 * self.unit), pl.ds(*self.to_columns)]

    def put_here(self):
        return pltpu.make_async_copy(self.total, self.place_out(), self.send.at[self.depth + 5])

    def put_there(self):
        p = self.place
        return self.copy(self.total, self.place_out(), self.depth + 4, (p.dp, flip(p.seq, 1)))

    def rows(self, start):
        return pl.ds(pl.multiple_of(start, self.unit), self.unit)

    def stage_core(self):
        self.load().start()
        self.core().start()

    def chip(self, z, y, start):
        rows = self.rows(start)
        return self.own[z, y, rows, :].astype(jnp.float32) + self.from_core[z, y, rows, :].astype(jnp.float32)

    def stage_x(self):
        self.load().wait()
        self.core().wait_recv()
        u, side, y = self.unit, self.place.side, self.place.y
        far = (1 - side) * (2 * u)

        def body(z, carry):
            for yy in range(2):
                self.to_x[z, yy, :, :] = self.chip(z, yy, far).astype(jnp.bfloat16)
            return carry

        lax.fori_loop(0, self.depth, body, 0)
        self.x().start()

    def pair(self, z, y):
        u = self.unit
        solo = self.chip(z, y, self.place.side * (2 * u)) + self.from_x[z, y, :, :].astype(jnp.float32)
        return self.chip(z, y, u), solo

    def stage_y(self):
        self.x().wait_recv()
        u, y = self.unit, self.place.y

        def body(z, carry):
            both, solo = self.pair(z, 1 - y)
            self.to_y[z, pl.ds(0, u), :] = both.astype(jnp.bfloat16)
            self.to_y[z, pl.ds(u, u), :] = solo.astype(jnp.bfloat16)
            return carry

        lax.fori_loop(0, self.depth, body, 0)
        self.y().start()

    def column(self, z):
        u = self.unit
        both, solo = self.pair(z, self.place.y)
        both = both + self.from_y[z, pl.ds(0, u), :].astype(jnp.float32)
        solo = solo + self.from_y[z, pl.ds(u, u), :].astype(jnp.float32)
        return both, solo

    def stage_z(self):
        self.y().wait_recv()
        u = self.unit
        for k in range(1, self.depth):
            both, solo = self.column(flip(self.place.z, k))
            self.to_z[k - 1, pl.ds(0, u), :] = both.astype(jnp.bfloat16)
            self.to_z[k - 1, pl.ds(u, u), :] = solo.astype(jnp.bfloat16)
            self.z(k).start()

    def stage_last(self):
        for k in range(1, self.depth):
            self.z(k).wait_recv()
        u = self.unit
        both, solo = self.column(self.place.z)
        for k in range(1, self.depth):
            both = both + self.from_z[k - 1, pl.ds(0, u), :].astype(jnp.float32)
            solo = solo + self.from_z[k - 1, pl.ds(u, u), :].astype(jnp.float32)
        self.last[pl.ds(0, u), :] = both.astype(jnp.bfloat16)
        self.last[pl.ds(u, u), :] = solo.astype(jnp.bfloat16)
        self.x_last().start()

    def stage_out(self):
        self.x_last().wait_recv()
        u, side = self.unit, self.place.side
        mine, got = self.last[...].astype(jnp.float32), self.got[...].astype(jnp.float32)
        self.total[self.rows(u), :] = mine[:u] + got[:u]
        self.total[self.rows(side * (2 * u)), :] = mine[u:]
        self.total[self.rows((1 - side) * (2 * u)), :] = got[u:]
        self.put_here().start()
        self.put_there().start()

    def finish(self):
        self.core().wait_send()
        self.x().wait_send()
        self.y().wait_send()
        for k in range(1, self.depth):
            self.z(k).wait_send()
        self.x_last().wait_send()
        self.put_here().wait()
        self.put_there().wait()


def reduce_scratch(dp_size, units, rows, width):
    z, u = dp_size // 2, rows // 6
    low = lambda *shape: pltpu.VMEM((units, *shape, width), jnp.bfloat16)
    return [
        low(z, 2, 3 * u), low(z, 2, 3 * u), low(z, 2, u), low(z, 2, u), low(z, 2 * u), low(z, 2 * u),
        low(z - 1, 2 * u), low(z - 1, 2 * u), low(2 * u), low(2 * u), pltpu.VMEM((units, 3 * u, width), jnp.float32),
        pltpu.SemaphoreType.DMA((units, z + 6)), pltpu.SemaphoreType.DMA((units, z + 6)),
    ]


def reduce_units(place, srcs, outs, plan, scratch):
    bufs, send, recv = scratch[:-2], scratch[-2], scratch[-1]
    return [
        Reduce(place, srcs[s], (first, rows), (column, width), (to, width), outs[o], to_row, [b.at[i] for b in bufs], (send.at[i], recv.at[i]))
        for i, (s, o, first, rows, column, width, to_row, to) in enumerate(plan)
    ]


STAGES = ("stage_core", "stage_x", "stage_y", "stage_z", "stage_last", "stage_out", "finish")


def reduce_steps(units, ages=(0, 1, 3, 5, 7, 9, 11)):
    steps = []
    for tick in range(len(units) + ages[-1]):
        step = []
        for stage, age in sorted(zip(STAGES, ages), key=lambda pair: -pair[1]):
            i = tick - age
            if 0 <= i < len(units):
                step.append(getattr(units[i], stage))
        steps.append(step)
    return steps


class SumAll:
    def __init__(self, place, src, out, buf, got, send, recv):
        self.place, self.src, self.out, self.buf, self.got, self.send, self.recv = place, src, out, buf, got, send, recv

    def copy(self, stage, slot, peer):
        return pltpu.make_async_remote_copy(
            src_ref=self.buf.at[stage], dst_ref=self.got.at[slot], send_sem=self.send.at[slot], recv_sem=self.recv.at[slot],
            device_id=peer, device_id_type=MESH,
        )

    def copies(self, stage):
        p = self.place
        if stage < 3:
            peer = [(p.dp, flip(p.seq, 1)), (p.dp, flip(p.seq, 2)), (flip(p.dp, 1), p.seq)][stage]
            return [self.copy(stage, stage, peer)]
        return [self.copy(3, 2 + k, (p.along_z(k), p.seq)) for k in range(1, p.depth)]

    def begin(self):
        self.buf[0] = self.src[...]
        for c in self.copies(0):
            c.start()

    def advance(self, stage):
        for c in self.copies(stage):
            c.wait_recv()
        if stage < 3:
            self.buf[stage + 1] = self.buf[stage] + self.got[stage]
            for c in self.copies(stage + 1):
                c.start()
        else:
            z, n = self.place.z, self.place.depth
            pick = lambda i: i
            total = self.buf[3]
            parts = [self.buf[3]] + [self.got[2 + k] for k in range(1, n)]
            total = (parts[0] + parts[1]) + (parts[2] + parts[3])
            self.out[...] = total

    def finish(self):
        for stage in range(4):
            for c in self.copies(stage):
                c.wait_send()


def last_kernel(dp_size, plan, n_src, n_out, n_rows, *refs):
    refs = list(refs)
    srcs, vec, rows_in = refs[:n_src], refs[n_src], refs[n_src + 1:n_src + 1 + n_rows]
    refs = refs[n_src + 1 + n_rows:]
    outs, vec_out, rows_out = refs[:n_out], refs[n_out], refs[n_out + 1:n_out + 1 + n_rows]
    scratch = refs[n_out + 1 + n_rows:]
    place = Place(dp_size)
    place.greet()
    small = SumAll(place, vec, vec_out, *scratch[13:17])
    sem = scratch[17]
    moves = [SwapBack(place, a, b, sem.at[i, 0], sem.at[i, 1], sem.at[i, 2]) for i, (a, b) in enumerate(zip(rows_in, rows_out))]
    small.begin()
    for move in moves:
        move.start()
    steps = reduce_steps(reduce_units(place, srcs, outs, plan, scratch[:13]))
    for i, step in enumerate(steps):
        for call in step:
            call()
        if i < 4:
            small.advance(i)
    small.finish()
    for move in moves:
        move.wait()


def last_exchange(dp_size, grads, out_shapes, plan, vec, rows, rows_shape):
    n_src, n_out = len(grads), len(out_shapes)
    anywhere = pl.BlockSpec(memory_space=pl.ANY)
    vmem = pl.BlockSpec(memory_space=pltpu.VMEM)
    z = dp_size // 2
    count, width = plan[0][3], plan[0][5]
    n_rows = len(rows)
    return pl.pallas_call(
        functools.partial(last_kernel, dp_size, plan, n_src, n_out, n_rows),
        out_shape=[jax.ShapeDtypeStruct(s, jnp.float32) for s in out_shapes] + [jax.ShapeDtypeStruct(vec.shape, vec.dtype)]
        + [jax.ShapeDtypeStruct(rows_shape, r.dtype) for r in rows],
        in_specs=[anywhere] * n_src + [vmem] + [anywhere] * n_rows,
        out_specs=[anywhere] * n_out + [vmem] + [anywhere] * n_rows,
        scratch_shapes=reduce_scratch(dp_size, len(plan), count, width) + [
            pltpu.VMEM((4, *vec.shape), jnp.float32), pltpu.VMEM((z + 2, *vec.shape), jnp.float32),
            pltpu.SemaphoreType.DMA((z + 2,)), pltpu.SemaphoreType.DMA((z + 2,)), pltpu.SemaphoreType.DMA((n_rows, 3)),
        ],
        compiler_params=pltpu.CompilerParams(collective_id=3, has_side_effects=True, vmem_limit_bytes=60 << 20),
        name="last_exchange",
    )(*grads, vec, *rows)


def halves(width):
    lane = lax.broadcasted_iota(jnp.int32, (1, width), 1)
    return lane


def key_extra(extra_ref, length, core, rows, first_pos):
    block = rows // 4
    row = lax.broadcasted_iota(jnp.int32, (rows, 128), 0)
    lane = lax.broadcasted_iota(jnp.int32, (rows, 128), 1)
    part = row // block
    owner = jnp.where(part < 2, core, 1 - core)
    position = row - part * block + (owner + 2 * lax.rem(part, 2)) * block
    dead = jnp.where(position < length, 0.0, masked_score)
    for parity in range(2):
        base = HEAD_DIM * (1 - parity)
        at = lane - base
        value = jnp.where(at == 0, dead, jnp.where((at > 0) & (at < 4), -1.0, 0.0))
        extra_ref[parity, :, :] = value.astype(jnp.bfloat16)


def split3(value):
    high = value.astype(jnp.bfloat16).astype(jnp.float32)
    rest = value - high
    mid = rest.astype(jnp.bfloat16).astype(jnp.float32)
    return high, mid, rest - mid


def nt(a, b):
    return lax.dot_general(a, b, (((1,), (1,)), ((), ())), preferred_element_type=jnp.float32)


def nn(a, b):
    return jnp.dot(a, b, preferred_element_type=jnp.float32)


def greet_sibling(peer):
    barrier = pltpu.get_barrier_semaphore()
    pl.semaphore_signal(barrier, inc=1, device_id=peer, device_id_type=MESH)
    pl.semaphore_wait(barrier, 1)


def forward_kernel(tile, length_ref, qkv_ref, ctx_ref, lse_ref, other_ref, extra_ref, send, recv):
    seq = lax.axis_index("seq")
    core, side = lax.rem(seq, 2), lax.div(seq, 2)
    peer = (lax.axis_index("dp"), flip(seq, 1))
    rows, width = ctx_ref.shape
    greet_sibling(peer)
    swap = pltpu.make_async_remote_copy(
        src_ref=qkv_ref.at[:, pl.ds(width, 2 * width)], dst_ref=other_ref, send_sem=send, recv_sem=recv,
        device_id=peer, device_id_type=MESH,
    )
    swap.start()
    length = jnp.where(side == 0, length_ref[0], length_ref[1])
    key_extra(extra_ref, length, core, 2 * rows, 0)
    swap.wait()
    lane = lax.broadcasted_iota(jnp.int32, (1, 128), 1)
    lse_ref[...] = jnp.zeros_like(lse_ref)
    slabs = width // 128

    def slab(j, carry):
        at = pl.multiple_of(j * 128, 128)
        cols = lambda base: pl.ds(pl.multiple_of(base + j * 128, 128), 128)
        keys = jnp.concatenate([qkv_ref[:, cols(width)], other_ref[:, cols(0)]], axis=0)
        values = jnp.concatenate([qkv_ref[:, cols(2 * width)], other_ref[:, cols(width)]], axis=0)
        queries = qkv_ref[:, cols(0)]
        outs = []
        stats = []
        for parity in range(2):
            mine = (lane < HEAD_DIM) if parity == 0 else (lane >= HEAD_DIM)
            mark = jnp.where(lane == HEAD_DIM * (1 - parity), 1.0, 0.0).astype(jnp.bfloat16)
            k_h = jnp.where(mine, keys, extra_ref[parity])
            v_h = jnp.where(mine, values, jnp.ones_like(values))
            q_h = jnp.where(mine, queries * jnp.bfloat16(HEAD_DIM ** -0.5), mark)
            pieces, tops = [], []
            for t in range(rows // tile):
                scores = nt(q_h[t * tile:(t + 1) * tile], k_h)
                top = jnp.max(scores, axis=-1, keepdims=True)
                weight = jnp.exp(scores - top).astype(jnp.bfloat16)
                pieces.append(nn(weight, v_h))
                tops.append(top)
            out = jnp.concatenate(pieces, axis=0)
            top = jnp.concatenate(tops, axis=0)
            other = HEAD_DIM * (1 - parity)
            total = out[:, other:other + 1]
            outs.append(out / total)
            stats.append(top + jnp.log(total))
        ctx_ref[:, cols(0)] = jnp.where(lane < HEAD_DIM, outs[0], outs[1]).astype(jnp.bfloat16)
        lse_ref[...] = jnp.where(lane == 2 * j, stats[0], jnp.where(lane == 2 * j + 1, stats[1], lse_ref[...]))
        return carry

    lax.fori_loop(0, slabs, slab, 0)


def attend_forward(lengths, qkv):
    rows, width = qkv.shape[0], qkv.shape[1] // 3
    vmem = pl.BlockSpec(memory_space=pltpu.VMEM)
    return pl.pallas_call(
        functools.partial(forward_kernel, min(256, rows)),
        out_shape=[
            jax.ShapeDtypeStruct((rows, width), jnp.bfloat16),
            jax.ShapeDtypeStruct((rows, 128), jnp.float32),
            jax.ShapeDtypeStruct((rows, 2 * width), jnp.bfloat16),
        ],
        in_specs=[pl.BlockSpec(memory_space=pltpu.SMEM), vmem],
        out_specs=[vmem] * 3,
        scratch_shapes=[pltpu.VMEM((2, 2 * rows, 128), jnp.bfloat16), pltpu.SemaphoreType.DMA, pltpu.SemaphoreType.DMA],
        compiler_params=pltpu.CompilerParams(collective_id=1, has_side_effects=True, vmem_limit_bytes=48 << 20),
        name="attend_forward",
    )(lengths, qkv)


def backward_kernel(block, length_ref, qkv_ref, other_ref, ctx_ref, grad_ref, lse_ref, out_ref,
                    extra_ref, k_ref, v_ref, q_ref, g_ref, kt_ref, dq_ref, dk_ref, dv_ref, got_ref, send, recv):
    seq = lax.axis_index("seq")
    core, side = lax.rem(seq, 2), lax.div(seq, 2)
    peer = (lax.axis_index("dp"), flip(seq, 1))
    rows, width = ctx_ref.shape
    slabs = width // 128
    greet_sibling(peer)
    length = jnp.where(side == 0, length_ref[0], length_ref[1])
    key_extra(extra_ref, length, core, 2 * rows, 0)
    lane = lax.broadcasted_iota(jnp.int32, (1, 128), 1)
    sub = lax.broadcasted_iota(jnp.int32, (128, 1), 0)

    def give(j, which):
        src = (dk_ref if which == 0 else dv_ref).at[j, pl.ds(rows, rows)]
        return pltpu.make_async_remote_copy(
            src_ref=src, dst_ref=got_ref.at[j, which], send_sem=send.at[j, which], recv_sem=recv.at[j, which],
            device_id=peer, device_id_type=MESH,
        )

    def slab(j, carry):
        cols = lambda base: pl.ds(pl.multiple_of(base + j * 128, 128), 128)
        keys = jnp.concatenate([qkv_ref[:, cols(width)], other_ref[:, cols(0)]], axis=0)
        values = jnp.concatenate([qkv_ref[:, cols(2 * width)], other_ref[:, cols(width)]], axis=0)
        queries = qkv_ref[:, cols(0)] * jnp.bfloat16(HEAD_DIM ** -0.5)
        grads = grad_ref[:, cols(0)]
        along = grads.astype(jnp.float32) * ctx_ref[:, cols(0)].astype(jnp.float32)
        lse = lse_ref[...]
        for parity in range(2):
            mine = (lane < HEAD_DIM) if parity == 0 else (lane >= HEAD_DIM)
            at = lane - HEAD_DIM * (1 - parity)
            delta = jnp.sum(jnp.where(mine, along, 0.0), axis=-1, keepdims=True)
            stat = jnp.sum(jnp.where(lane == 2 * j + parity, lse, 0.0), axis=-1, keepdims=True)
            s0, s1, s2 = split3(stat)
            d0, d1, d2 = split3(delta)
            low = jnp.bfloat16
            q_more = jnp.where(at == 0, 1.0, jnp.where(at == 1, s0, jnp.where(at == 2, s1, jnp.where(at == 3, s2, 0.0)))).astype(low)
            g_more = jnp.where(at == 1, d0, jnp.where(at == 2, d1, jnp.where(at == 3, d2, 0.0))).astype(low)
            k_h = jnp.where(mine, keys, extra_ref[parity])
            k_ref[parity] = k_h
            v_ref[parity] = jnp.where(mine, values, extra_ref[parity])
            q_ref[parity] = jnp.where(mine, queries, q_more)
            g_ref[parity] = jnp.where(mine, grads, g_more)
            kt_ref[parity] = jnp.where((sub < HEAD_DIM) if parity == 0 else (sub >= HEAD_DIM), keys.T, jnp.zeros((128, 2 * rows), low))
        dq_ref[...] = jnp.zeros_like(dq_ref)

        def part(b, carry):
            span = pl.ds(pl.multiple_of(b * block, block), block)
            made = []
            for parity in range(2):
                q_h, g_h = q_ref[parity], g_ref[parity]
                prob = jnp.exp(nt(k_ref[parity, span, :], q_h))
                slope = nt(v_ref[parity, span, :], g_h)
                ds = (prob * slope).astype(jnp.bfloat16)
                dv = nn(prob.astype(jnp.bfloat16), g_h)
                dk = nn(ds, q_h)
                dq_ref[...] += nn(kt_ref[parity, :, span], ds)
                made.append((dk, dv))
            dk_ref[j, span, :] = jnp.where(lane < HEAD_DIM, made[0][0], made[1][0])
            dv_ref[j, span, :] = jnp.where(lane < HEAD_DIM, made[0][1], made[1][1])
            return carry

        lax.fori_loop(0, 2 * rows // block, part, 0)
        out_ref[:, cols(0)] = (dq_ref[...].T * (HEAD_DIM ** -0.5)).astype(jnp.bfloat16)
        give(j, 0).start()
        give(j, 1).start()
        return carry

    lax.fori_loop(0, slabs, slab, 0)

    def take(j, carry):
        for which in range(2):
            give(j, which).wait()
            mine = (dk_ref if which == 0 else dv_ref)[j, pl.ds(0, rows), :]
            at = pl.ds(pl.multiple_of((1 + which) * width + j * 128, 128), 128)
            out_ref[:, at] = (mine + got_ref[j, which]).astype(jnp.bfloat16)
        return carry

    lax.fori_loop(0, slabs, take, 0)


def attend_backward(lengths, qkv, other, ctx, grad, lse):
    rows, width = ctx.shape
    slabs = width // 128
    vmem = pl.BlockSpec(memory_space=pltpu.VMEM)
    low = lambda *shape: pltpu.VMEM(shape, jnp.bfloat16)
    full = lambda *shape: pltpu.VMEM(shape, jnp.float32)
    return pl.pallas_call(
        functools.partial(backward_kernel, min(256, rows)),
        out_shape=jax.ShapeDtypeStruct(qkv.shape, jnp.bfloat16),
        in_specs=[pl.BlockSpec(memory_space=pltpu.SMEM)] + [vmem] * 5,
        out_specs=vmem,
        scratch_shapes=[
            low(2, 2 * rows, 128), low(2, 2 * rows, 128), low(2, 2 * rows, 128), low(2, rows, 128), low(2, rows, 128),
            low(2, 128, 2 * rows), full(128, rows), full(slabs, 2 * rows, 128), full(slabs, 2 * rows, 128),
            full(slabs, 2, rows, 128), pltpu.SemaphoreType.DMA((slabs, 2)), pltpu.SemaphoreType.DMA((slabs, 2)),
        ],
        compiler_params=pltpu.CompilerParams(collective_id=2, has_side_effects=True, vmem_limit_bytes=56 << 20),
        name="attend_backward",
    )(lengths, qkv, other, ctx, grad, lse)


class SwapBack:
    def __init__(self, place, src, dst, send, recv, local):
        side, length = place.side, dst.shape[1]
        block = lambda i: src.at[pl.ds(pl.multiple_of(i * length, length), length)]
        self.here = pltpu.make_async_copy(block(side), dst.at[side], local)
        self.there = pltpu.make_async_remote_copy(
            src_ref=block(1 - side), dst_ref=dst.at[side], send_sem=send, recv_sem=recv,
            device_id=(place.dp, flip(place.seq, 2)), device_id_type=MESH,
        )

    def start(self):
        self.here.start()
        self.there.start()

    def wait(self):
        self.here.wait()
        self.there.wait()


def matmul(a, b):
    return jnp.dot(a, b, preferred_element_type=jnp.float32)


def inner_rows(a, b):
    return lax.dot_general(a, b, (((0,), (0,)), ((), ())), preferred_element_type=jnp.float32)


def times_transposed(a, b):
    return lax.dot_general(a, b, (((1,), (1,)), ((), ())), preferred_element_type=jnp.float32)


def swap_rows(rows):
    side = lax.div(lax.axis_index("seq"), 2)
    size = lax.axis_size("seq")
    got = lax.ppermute(lax.dynamic_index_in_dim(rows, 1 - side, 0, False), "seq", [(i, i ^ 2) for i in range(size)])
    kept = lax.dynamic_index_in_dim(rows, side, 0, False)
    first = jnp.where(side == 0, kept, got)
    second = jnp.where(side == 0, got, kept)
    return jnp.concatenate([first, second], axis=0)


def swap_rows_back(rows):
    side = lax.div(lax.axis_index("seq"), 2)
    size = lax.axis_size("seq")
    blocks = rows.reshape(2, rows.shape[0] // 2, rows.shape[1])
    got = lax.ppermute(lax.dynamic_index_in_dim(blocks, 1 - side, 0, False), "seq", [(i, i ^ 2) for i in range(size)])
    kept = lax.dynamic_index_in_dim(blocks, side, 0, False)
    return jnp.stack([jnp.where(side == 0, kept, got), jnp.where(side == 0, got, kept)])


def pack_vectors(narrow, wide):
    rows = jnp.stack([v.astype(jnp.float32) for v in narrow])
    rows = jnp.pad(rows, ((0, 0), (0, 128 - rows.shape[1])))
    more = wide.astype(jnp.float32).reshape(-1, 128)
    both = jnp.concatenate([rows, more], axis=0)
    return jnp.pad(both, ((0, 16 - both.shape[0]), (0, 0)))


def norm_stats(hidden):
    row_mean = jnp.mean(hidden, axis=-1, keepdims=True)
    centred = hidden - row_mean
    row_var = jnp.mean(centred * centred, axis=-1, keepdims=True)
    scale = lax.rsqrt(row_var + eps_norm)
    return centred * scale, scale


def norm_backward(grad, gain, unit, scale):
    e = grad * gain
    first = jnp.mean(e, axis=-1, keepdims=True)
    second = jnp.mean(e * unit, axis=-1, keepdims=True)
    return scale * (e - first - unit * second)


def col_sum(value):
    return jnp.sum(value, axis=0)


def local(
    inputs, lengths, query_weight, key_weight, value_weight, output_weight, up_weight, down_weight,
    query_bias, value_bias, output_bias, up_bias, down_bias, first_gain, first_shift, second_gain, second_shift, cotangent,
):
    dp_size = lax.axis_size("dp")
    groups, length, width = inputs.shape
    shard = query_weight.shape[0]
    fast = dp_size == 8 and shard == 96 and groups == 2
    rows = groups * length
    seq = lax.axis_index("seq")
    core, side = lax.rem(seq, 2), lax.div(seq, 2)
    narrow = [query_bias, value_bias, output_bias, down_bias, first_gain, first_shift, second_gain, second_shift]
    hidden_width = up_weight.shape[1]
    if fast:
        u = shard
        plan = [(i, 0, 0, u, 0, width, width * i) for i in range(3)] + [(3, 1, 0, u, 0, width, 0)]
        plan += [(4, 2, 0, u, width * j, width, width * j) for j in range(hidden_width // width)]
        plan += [(5, 3, u * j, u, 0, width, 0) for j in range(down_weight.shape[0] // u)]
        weights = [query_weight, key_weight, value_weight, output_weight, up_weight, down_weight]
        shapes = [(u, 3 * width), (u, width), (u, hidden_width), (down_weight.shape[0], width)]
        qkv_w, out_w, up_w, down_w, vec, flat_in, flat_cot = first_exchange(
            dp_size, weights, shapes, plan, pack_vectors(narrow, up_bias), (inputs, cotangent)
        )
        qkv_w, out_w = qkv_w.reshape(width, 3 * width), out_w.reshape(width, width)
        up_w, down_w = up_w.reshape(width, hidden_width), down_w.reshape(hidden_width, width)
        vec = vec.reshape(dp_size, 16, 128)
        flat_vec = vec[:, :8, :shard].transpose(1, 0, 2).reshape(8, width)
        bias_up = vec[:, 8:8 + up_bias.shape[0] // 128].reshape(hidden_width)
    else:
        gather = lambda a: lax.all_gather(a, "dp", axis=0, tiled=True)
        qkv_w = gather(jnp.concatenate([query_weight, key_weight, value_weight], axis=1))
        out_w, up_w, down_w = gather(output_weight), gather(up_weight), gather(down_weight)
        flat_vec = jnp.stack([gather(v.astype(jnp.float32)) for v in narrow])
        bias_up = gather(up_bias.astype(jnp.float32))
        flat_in, flat_cot = swap_rows(inputs), swap_rows(cotangent)
    bias_q, bias_v, bias_out, bias_down, gain_1, shift_1, gain_2, shift_2 = [flat_vec[i] for i in range(8)]
    bias_qkv = jnp.concatenate([bias_q, jnp.zeros_like(bias_q), bias_v])

    qkv = (matmul(flat_in, qkv_w) + bias_qkv).astype(jnp.bfloat16)
    context, lse, other = attend_forward(lengths, qkv)
    first_sum = flat_in.astype(jnp.float32) + (matmul(context, out_w) + bias_out)
    unit_1, scale_1 = norm_stats(first_sum)
    first_norm = (unit_1 * gain_1 + shift_1).astype(jnp.bfloat16)
    up_pre = matmul(first_norm, up_w) + bias_up
    below = 0.5 + 0.5 * lax.erf(up_pre * (0.5 ** 0.5))
    hidden_act = (up_pre * below).astype(jnp.bfloat16)
    slope = (below + up_pre * jnp.exp(-0.5 * up_pre * up_pre) * 0.3989422804014327).astype(jnp.bfloat16)
    down_out = matmul(hidden_act, down_w) + bias_down
    second_sum = first_norm.astype(jnp.float32) + down_out
    unit_2, scale_2 = norm_stats(second_sum)
    layer_rows = (unit_2 * gain_2 + shift_2).astype(jnp.bfloat16)

    row = jnp.arange(rows)
    position = lax.rem(row, length) + (core + 2 * lax.div(row, length)) * length
    live = (position < lengths[side]).astype(jnp.float32)
    grad_out = flat_cot.astype(jnp.float32) * live[:, None]
    second_gain_grad, second_shift_grad = col_sum(grad_out * unit_2), col_sum(grad_out)
    second_sum_grad = norm_backward(grad_out, gain_2, unit_2, scale_2)
    down_low = second_sum_grad.astype(jnp.bfloat16)
    low = jnp.bfloat16
    down_w_grad = inner_rows(hidden_act, down_low).astype(low)
    down_bias_grad = col_sum(down_low.astype(jnp.float32))
    up_low = (times_transposed(down_low, down_w) * slope.astype(jnp.float32)).astype(low)
    up_w_grad = inner_rows(first_norm, up_low).astype(low)
    up_bias_grad = col_sum(up_low.astype(jnp.float32))
    norm_grad = second_sum_grad + times_transposed(up_low, up_w)
    first_gain_grad, first_shift_grad = col_sum(norm_grad * unit_1), col_sum(norm_grad)
    first_sum_grad = norm_backward(norm_grad, gain_1, unit_1, scale_1)
    attended_low = first_sum_grad.astype(low)
    out_w_grad = inner_rows(context, attended_low).astype(low)
    out_bias_grad = col_sum(attended_low.astype(jnp.float32))
    context_grad = times_transposed(attended_low, out_w).astype(low)

    qkv_low = attend_backward(lengths, qkv, other, context, context_grad, lse)
    qkv_w_grad = inner_rows(flat_in, qkv_low).astype(low)
    qkv_bias_grad = col_sum(qkv_low.astype(jnp.float32))
    input_rows = (first_sum_grad + times_transposed(qkv_low, qkv_w)).astype(low)

    small = jnp.concatenate([
        jnp.stack([qkv_bias_grad[:width], qkv_bias_grad[2 * width:], out_bias_grad, down_bias_grad, first_gain_grad,
                   first_shift_grad, second_gain_grad, second_shift_grad]),
        up_bias_grad.reshape(-1, width),
    ], axis=0)
    me = lax.axis_index("dp")
    if fast:
        plan = [(3, 5, u * j, u, 0, width, u * j, 0) for j in range(down_weight.shape[0] // u)]
        plan += [(2, 4, 0, u, width * j, width, 0, width * j) for j in range(hidden_width // width)]
        plan += [(1, 3, 0, u, 0, width, 0, 0)] + [(0, i, 0, u, width * i, width, 0, 0) for i in range(3)]
        shapes = [(u, width)] * 4 + [up_weight.shape, down_weight.shape]
        grads = [g.reshape(dp_size // 2, 2, -1, g.shape[1]) for g in (qkv_w_grad, out_w_grad, up_w_grad, down_w_grad)]
        small = jnp.pad(small, ((0, 16 - small.shape[0]), (0, 0)))
        *weight_grads, small, layer_out, input_grad = last_exchange(
            dp_size, grads, shapes, plan, small, (layer_rows, input_rows), (groups, length, width)
        )
    else:
        scatter = lambda a: lax.psum(lax.psum_scatter(a.astype(jnp.float32), "dp", scatter_dimension=0, tiled=True), "seq")
        qkv_g = scatter(qkv_w_grad)
        weight_grads = [qkv_g[:, :width], qkv_g[:, width:2 * width], qkv_g[:, 2 * width:]]
        weight_grads += [scatter(out_w_grad), scatter(up_w_grad), scatter(down_w_grad)]
        small = lax.psum(small, ("dp", "seq"))
        layer_out, input_grad = swap_rows_back(layer_rows), swap_rows_back(input_rows)
    part = query_bias.shape[0]
    mine = lax.dynamic_slice(small, (0, me * part), (8, part))
    up_part = up_bias.shape[0]
    up_mine = lax.dynamic_slice(small[8:8 + hidden_width // width].reshape(hidden_width), (me * up_part,), (up_part,))
    return (layer_out, input_grad, *weight_grads, mine[0], mine[1], mine[2], up_mine, *[mine[i] for i in range(3, 8)])


def solution(mesh):
    rows, matrix, vector = P("dp", "seq", None), P("dp", None), P("dp")
    return jax.shard_map(
        local,
        mesh=mesh,
        in_specs=(rows, vector, *[matrix] * 6, *[vector] * 9, rows),
        out_specs=(rows, rows, *[matrix] * 6, *[vector] * 9),
        check_vma=False,
    )
```

```python
import collections
import functools
import jax
import jax.numpy as jnp
from jax import lax
from jax.experimental import pallas as pl
from jax.experimental.pallas import tpu as pltpu
from jax.sharding import PartitionSpec as P

MESH = pl.DeviceIdType.MESH
HEAD_DIM = 64
eps_norm = 1e-05
masked_score = -1000000000.0


def flip(value, bits):
    bit = 1
    while bit <= bits:
        if bits & bit:
            value = value + bit - 2 * bit * lax.rem(lax.div(value, bit), 2)
        bit *= 2
    return value


class Place:
    def __init__(self, dp_size):
        self.dp = lax.axis_index("dp")
        self.seq = lax.axis_index("seq")
        self.depth = dp_size // 2
        self.z = lax.div(self.dp, 2)
        self.y = lax.rem(self.dp, 2)
        self.core = lax.rem(self.seq, 2)
        self.side = lax.div(self.seq, 2)

    def along_z(self, k):
        return flip(self.dp, 2 * k)

    def peers(self):
        result = [(self.along_z(k), self.seq) for k in range(1, self.depth)]
        result.append((flip(self.dp, 1), self.seq))
        result.append((self.dp, flip(self.seq, 1)))
        result.append((self.dp, flip(self.seq, 2)))
        return result

    def greet(self):
        barrier = pltpu.get_barrier_semaphore()
        peers = self.peers()
        for peer in peers:
            pl.semaphore_signal(barrier, inc=1, device_id=peer, device_id_type=MESH)
        pl.semaphore_wait(barrier, len(peers))


class Gather:
    def __init__(self, place, src, dst, rows, columns, to_columns, split, sems):
        self.place, self.src, self.dst = place, src, dst
        self.columns, self.to_columns, self.split = columns, to_columns, split
        self.first, count = rows
        self.send, self.recv, self.local = sems
        self.depth = place.depth
        self.unit = unit = count // 6
        half = place.core * (3 * unit)
        self.half = (half, 3 * unit)
        self.fetch = (half + place.side * unit, 2 * unit) if split else self.half
        self.far = (half + place.side * (2 * unit), unit)

    def view(self, z, y, window):
        rows = pl.ds(pl.multiple_of(self.first + window[0], self.unit), window[1])
        return self.dst.at[z, y, rows, pl.ds(*self.to_columns)]

    def copy(self, src, dst, index, peer):
        return pltpu.make_async_remote_copy(
            src_ref=src, dst_ref=dst, send_sem=self.send.at[index], recv_sem=self.recv.at[index],
            device_id=peer, device_id_type=MESH,
        )

    def mine(self):
        rows = pl.ds(pl.multiple_of(self.first + self.fetch[0], self.unit), self.fetch[1])
        return self.src.at[rows, pl.ds(*self.columns)]

    def own(self):
        p = self.place
        return pltpu.make_async_copy(self.mine(), self.view(p.z, p.y, self.fetch), self.local)

    def over_z(self, k):
        p = self.place
        return self.copy(self.mine(), self.view(p.z, p.y, self.fetch), k, (p.along_z(k), p.seq))

    def over_y(self):
        p = self.place
        ref = self.view(slice(None), p.y, self.fetch)
        return self.copy(ref, ref, 0, (flip(p.dp, 1), p.seq))

    def over_x(self):
        p, every = self.place, slice(None)
        ref = self.view(every, every, self.far)
        return self.copy(ref, ref, self.depth, (p.dp, flip(p.seq, 2)))

    def across(self):
        p, every = self.place, slice(None)
        ref = self.view(every, every, self.half)
        return self.copy(ref, ref, self.depth + 1, (p.dp, flip(p.seq, 1)))

    def stage_z(self):
        self.own().start()
        for k in range(1, self.depth):
            self.over_z(k).start()

    def stage_y(self):
        self.own().wait()
        for k in range(1, self.depth):
            self.over_z(k).wait_recv()
        self.over_y().start()

    def stage_x(self):
        self.over_y().wait_recv()
        if self.split:
            self.over_x().start()
        else:
            self.across().start()

    def stage_core(self):
        if self.split:
            self.over_x().wait_recv()
            self.across().start()

    def arrive(self):
        self.across().wait_recv()

    def finish(self):
        for k in range(1, self.depth):
            self.over_z(k).wait_send()
        self.over_y().wait_send()
        if self.split:
            self.over_x().wait_send()
        self.across().wait_send()


def gather_sems(dp_size, units):
    n = dp_size // 2 + 2
    return [pltpu.SemaphoreType.DMA((units, n)), pltpu.SemaphoreType.DMA((units, n)), pltpu.SemaphoreType.DMA((units,))]


class Spread:
    def __init__(self, place, src, dst, sems):
        self.place, self.src, self.dst = place, src, dst
        self.send, self.recv, self.local = sems

    def own(self):
        return pltpu.make_async_copy(self.src, self.dst.at[self.place.z, self.place.y], self.local)

    def over_z(self, k):
        p = self.place
        return pltpu.make_async_remote_copy(
            src_ref=self.src, dst_ref=self.dst.at[p.z, p.y], send_sem=self.send.at[k], recv_sem=self.recv.at[k],
            device_id=(p.along_z(k), p.seq), device_id_type=MESH,
        )

    def over_y(self):
        p = self.place
        ref = self.dst.at[:, p.y]
        return pltpu.make_async_remote_copy(
            src_ref=ref, dst_ref=ref, send_sem=self.send.at[0], recv_sem=self.recv.at[0],
            device_id=(flip(p.dp, 1), p.seq), device_id_type=MESH,
        )

    def start(self):
        self.own().start()
        for k in range(1, self.place.depth):
            self.over_z(k).start()

    def forward(self):
        self.own().wait()
        for k in range(1, self.place.depth):
            self.over_z(k).wait_recv()
        self.over_y().start()

    def finish(self):
        for k in range(1, self.place.depth):
            self.over_z(k).wait_send()
        self.over_y().wait()


def gather_steps(units, window):
    count = len(units)
    steps = [[unit.stage_z for unit in units[:window]]]
    for i in range(count + 2):
        step = []
        if 0 <= i - 2 < count:
            step.append(units[i - 2].stage_core)
        if 0 <= i - 1 < count:
            step.append(units[i - 1].stage_x)
        if i < count:
            step.append(units[i].stage_y)
            if i + window < count:
                step.append(units[i + window].stage_z)
        steps.append(step)
    return steps


def weight_units(place, srcs, dsts, plan, sems):
    send, recv, local = sems
    return [
        Gather(place, srcs[s], dsts[d], (first, rows), (column, width), (to, width), split, (send.at[i], recv.at[i], local.at[i]))
        for i, (s, d, first, rows, column, width, to, split) in enumerate(plan)
    ]


class Swap:
    def __init__(self, place, src, dst, send, recv, local):
        side = place.side
        length = src.shape[1]
        own = dst.at[pl.ds(pl.multiple_of(side * length, 8), length)]
        self.here = pltpu.make_async_copy(src.at[side], own, local)
        self.there = pltpu.make_async_remote_copy(
            src_ref=src.at[1 - side], dst_ref=own, send_sem=send, recv_sem=recv,
            device_id=(place.dp, flip(place.seq, 2)), device_id_type=MESH,
        )

    def start(self):
        self.here.start()
        self.there.start()

    def wait(self):
        self.here.wait()
        self.there.wait()


class SwapBack:
    def __init__(self, place, src, dst, send, recv, local):
        side, length = place.side, dst.shape[1]
        block = lambda i: src.at[pl.ds(pl.multiple_of(i * length, length), length)]
        self.here = pltpu.make_async_copy(block(side), dst.at[side], local)
        self.there = pltpu.make_async_remote_copy(
            src_ref=block(1 - side), dst_ref=dst.at[side], send_sem=send, recv_sem=recv,
            device_id=(place.dp, flip(place.seq, 2)), device_id_type=MESH,
        )

    def start(self):
        self.here.start()
        self.there.start()

    def wait(self):
        self.here.wait()
        self.there.wait()


class Reduce:
    def __init__(self, place, src, rows, columns, to_columns, out, to_row, split, own, bufs, sems):
        self.place, self.src, self.out, self.split = place, src, out, split
        self.columns, self.to_columns, self.to_row = columns, to_columns, to_row
        self.first, count = rows
        self.unit = unit = count // 6
        self.from_core, self.from_x, self.from_y, self.from_z, self.got, self.total = bufs
        self.send, self.recv = sems
        self.depth = place.depth
        self.half = place.core * (3 * unit)
        self.sibling_half = (1 - place.core) * (3 * unit)
        self.keep = (place.side * unit, 2 * unit) if split else (0, 3 * unit)
        self.loads = own is not None
        self.own = own if self.loads else self.view(self.half)

    def view(self, start):
        rows = pl.ds(pl.multiple_of(self.first + start, self.unit), 3 * self.unit)
        return self.src.at[:, :, rows, pl.ds(*self.columns)]

    def rows(self, window):
        return pl.ds(pl.multiple_of(window[0], self.unit), window[1])

    def copy(self, src, dst, index, peer):
        return pltpu.make_async_remote_copy(
            src_ref=src, dst_ref=dst, send_sem=self.send.at[index], recv_sem=self.recv.at[index],
            device_id=peer, device_id_type=MESH,
        )

    def load(self):
        return pltpu.make_async_copy(self.view(self.half), self.own, self.send.at[0])

    def core(self):
        p = self.place
        return self.copy(self.view(self.sibling_half), self.from_core, self.depth, (p.dp, flip(p.seq, 1)))

    def far(self):
        return ((1 - self.place.side) * (2 * self.unit), self.unit)

    def x(self):
        p = self.place
        return self.copy(self.own.at[:, :, self.rows(self.far())], self.from_x, self.depth + 1, (p.dp, flip(p.seq, 2)))

    def y(self):
        p = self.place
        src = self.own.at[:, 1 - p.y, self.rows(self.keep)]
        return self.copy(src, self.from_y.at[:, pl.ds(0, self.keep[1])], self.depth + 2, (flip(p.dp, 1), p.seq))

    def z(self, k):
        p = self.place
        src = self.own.at[flip(p.z, k), p.y, self.rows(self.keep)]
        return self.copy(src, self.from_z.at[k - 1, pl.ds(0, self.keep[1])], k, (p.along_z(k), p.seq))

    def x_last(self):
        p = self.place
        src = self.own.at[p.z, p.y, self.rows(self.keep)]
        return self.copy(src, self.got.at[pl.ds(0, self.keep[1])], self.depth + 3, (p.dp, flip(p.seq, 2)))

    def place_out(self):
        row = pl.multiple_of(self.to_row + self.half, self.unit)
        return self.out.at[pl.ds(row, 3 * self.unit), pl.ds(*self.to_columns)]

    def put_here(self):
        return pltpu.make_async_copy(self.total, self.place_out(), self.send.at[self.depth + 5])

    def put_there(self):
        p = self.place
        return self.copy(self.total, self.place_out(), self.depth + 4, (p.dp, flip(p.seq, 1)))

    def chip(self, z, y, window):
        rows = self.rows(window)
        return self.own[z, y, rows, :].astype(jnp.float32) + self.from_core[z, y, rows, :].astype(jnp.float32)

    def pieces(self, z, y):
        u, side = self.unit, self.place.side
        if not self.split:
            return [((i * u, u), (i * u, u), self.chip(z, y, (i * u, u))) for i in range(3)]
        solo = (side * (2 * u), u)
        gained = self.chip(z, y, solo) + self.from_x[z, y, :, :].astype(jnp.float32)
        return [((u, u), ((1 - side) * u, u), self.chip(z, y, (u, u))), (solo, (side * u, u), gained)]

    def stage_core(self):
        if self.loads:
            self.load().start()
        self.core().start()

    def stage_x(self):
        if self.loads:
            self.load().wait()
        self.core().wait_recv()
        if not self.split:
            return
        rows = self.rows(self.far())

        def body(z, carry):
            for y in range(2):
                self.own[z, y, rows, :] = self.chip(z, y, self.far()).astype(jnp.bfloat16)
            return carry

        lax.fori_loop(0, self.depth, body, 0)
        self.x().start()

    def stage_y(self):
        if self.split:
            self.x().wait_recv()
        y = 1 - self.place.y

        def body(z, carry):
            for at, _, value in self.pieces(z, y):
                self.own[z, y, self.rows(at), :] = value.astype(jnp.bfloat16)
            return carry

        lax.fori_loop(0, self.depth, body, 0)
        self.y().start()

    def column(self, z):
        return [
            (at, kept, value + self.from_y[z, self.rows(kept), :].astype(jnp.float32))
            for at, kept, value in self.pieces(z, self.place.y)
        ]

    def stage_z(self):
        self.y().wait_recv()
        for k in range(1, self.depth):
            z = flip(self.place.z, k)
            for at, _, value in self.column(z):
                self.own[z, self.place.y, self.rows(at), :] = value.astype(jnp.bfloat16)
            self.z(k).start()

    def stage_last(self):
        for k in range(1, self.depth):
            self.z(k).wait_recv()
        p = self.place
        for at, kept, value in self.column(p.z):
            for k in range(1, self.depth):
                value = value + self.from_z[k - 1, self.rows(kept), :].astype(jnp.float32)
            self.own[p.z, p.y, self.rows(at), :] = value.astype(jnp.bfloat16)
        self.x_last().start()

    def stage_out(self):
        self.x_last().wait_recv()
        p, u = self.place, self.unit
        mine = lambda at: self.own[p.z, p.y, self.rows(at), :].astype(jnp.float32)
        got = lambda at: self.got[self.rows(at), :].astype(jnp.float32)
        if self.split:
            side = p.side
            self.total[self.rows((u, u)), :] = mine((u, u)) + got((side * u, u))
            self.total[self.rows((side * (2 * u), u)), :] = mine((side * (2 * u), u))
            self.total[self.rows((2 * u - side * (2 * u), u)), :] = got(((1 - side) * u, u))
        else:
            whole = (0, 3 * u)
            self.total[...] = mine(whole) + got(whole)
        self.put_here().start()
        self.put_there().start()

    def finish(self):
        self.core().wait_send()
        if self.split:
            self.x().wait_send()
        self.y().wait_send()
        for k in range(1, self.depth):
            self.z(k).wait_send()
        self.x_last().wait_send()
        self.put_here().wait()
        self.put_there().wait()


def reduce_scratch(dp_size, units, loads, rows, width):
    z, u = dp_size // 2, rows // 6
    low = lambda count, *shape: pltpu.VMEM((count, *shape, width), jnp.bfloat16)
    return [
        low(loads, z, 2, 3 * u), low(units, z, 2, 3 * u), low(units, z, 2, u), low(units, z, 3 * u), low(units, z - 1, 3 * u),
        low(units, 3 * u), pltpu.VMEM((units, 3 * u, width), jnp.float32),
        pltpu.SemaphoreType.DMA((units, z + 6)), pltpu.SemaphoreType.DMA((units, z + 6)),
    ]


def reduce_units(place, srcs, outs, plan, loads, scratch):
    own, bufs, send, recv = scratch[0], scratch[1:-2], scratch[-2], scratch[-1]
    return [
        Reduce(place, srcs[s], (first, rows), (column, width), (to, width), outs[o], to_row, split,
               own.at[i] if i < loads else None, [b.at[i] for b in bufs], (send.at[i], recv.at[i]))
        for i, (s, o, first, rows, column, width, to_row, to, split) in enumerate(plan)
    ]


STAGES = ("stage_core", "stage_x", "stage_y", "stage_z", "stage_last", "stage_out", "finish")


def reduce_steps(units):
    first, steps = -3, collections.defaultdict(list)
    for i, unit in enumerate(units):
        lag = 2 if unit.split else 0
        ages = (-3 if unit.loads else -1, 0, lag, lag + 2, lag + 4, lag + 6, lag + 7)
        for stage, age in zip(STAGES, ages):
            steps[i + age].append((-age, getattr(unit, stage)))
    ticks = range(first, max(steps) + 1)
    return [[call for _, call in sorted(steps[tick], key=lambda pair: pair[0])] for tick in ticks], first


class SumAll:
    def __init__(self, place, src, out, buf, got, send, recv):
        self.place, self.src, self.out, self.buf, self.got, self.send, self.recv = place, src, out, buf, got, send, recv

    def copy(self, stage, slot, peer):
        return pltpu.make_async_remote_copy(
            src_ref=self.buf.at[stage], dst_ref=self.got.at[slot], send_sem=self.send.at[slot], recv_sem=self.recv.at[slot],
            device_id=peer, device_id_type=MESH,
        )

    def copies(self, stage):
        p = self.place
        if stage < 3:
            peer = [(p.dp, flip(p.seq, 1)), (p.dp, flip(p.seq, 2)), (flip(p.dp, 1), p.seq)][stage]
            return [self.copy(stage, stage, peer)]
        return [self.copy(3, 2 + k, (p.along_z(k), p.seq)) for k in range(1, p.depth)]

    def begin(self):
        self.buf[0] = self.src[...]
        for c in self.copies(0):
            c.start()

    def advance(self, stage):
        for c in self.copies(stage):
            c.wait_recv()
        if stage < 3:
            self.buf[stage + 1] = self.buf[stage] + self.got[stage]
            for c in self.copies(stage + 1):
                c.start()
        else:
            z, n = self.place.z, self.place.depth
            pick = lambda i: i
            total = self.buf[3]
            parts = [self.buf[3]] + [self.got[2 + k] for k in range(1, n)]
            total = (parts[0] + parts[1]) + (parts[2] + parts[3])
            self.out[...] = total

    def finish(self):
        for stage in range(4):
            for c in self.copies(stage):
                c.wait_send()


def halves(width):
    lane = lax.broadcasted_iota(jnp.int32, (1, width), 1)
    return lane


def key_extra(extra_ref, length, core, rows, first_pos):
    block = rows // 4
    row = lax.broadcasted_iota(jnp.int32, (rows, 128), 0)
    lane = lax.broadcasted_iota(jnp.int32, (rows, 128), 1)
    part = row // block
    owner = jnp.where(part < 2, core, 1 - core)
    position = row - part * block + (owner + 2 * lax.rem(part, 2)) * block
    dead = jnp.where(position < length, 0.0, masked_score)
    for parity in range(2):
        base = HEAD_DIM * (1 - parity)
        at = lane - base
        value = jnp.where(at == 0, dead, jnp.where((at > 0) & (at < 4), -1.0, 0.0))
        extra_ref[parity, :, :] = value.astype(jnp.bfloat16)


def split3(value):
    high = value.astype(jnp.bfloat16).astype(jnp.float32)
    rest = value - high
    mid = rest.astype(jnp.bfloat16).astype(jnp.float32)
    return high, mid, rest - mid


def nt(a, b):
    return lax.dot_general(a, b, (((1,), (1,)), ((), ())), preferred_element_type=jnp.float32)


def nn(a, b):
    return jnp.dot(a, b, preferred_element_type=jnp.float32)


def greet_sibling(peer):
    barrier = pltpu.get_barrier_semaphore()
    pl.semaphore_signal(barrier, inc=1, device_id=peer, device_id_type=MESH)
    pl.semaphore_wait(barrier, 1)


def forward_slab(j, tile, qkv_ref, other_ref, extra_ref, ctx_ref, lse_ref):
    rows, width = ctx_ref.shape
    lane = lax.broadcasted_iota(jnp.int32, (1, 128), 1)
    cols = lambda base: pl.ds(base + 128 * j if isinstance(j, int) else pl.multiple_of(base + 128 * j, 128), 128)
    keys = jnp.concatenate([qkv_ref[:, cols(width)], other_ref[:, cols(0)]], axis=0)
    values = jnp.concatenate([qkv_ref[:, cols(2 * width)], other_ref[:, cols(width)]], axis=0)
    queries = qkv_ref[:, cols(0)]
    outs, stats = [], []
    for parity in range(2):
        mine = (lane < HEAD_DIM) if parity == 0 else (lane >= HEAD_DIM)
        mark = jnp.where(lane == HEAD_DIM * (1 - parity), 1.0, 0.0).astype(jnp.bfloat16)
        k_h = jnp.where(mine, keys, extra_ref[parity])
        v_h = jnp.where(mine, values, jnp.ones_like(values))
        q_h = jnp.where(mine, queries * jnp.bfloat16(HEAD_DIM ** -0.5), mark)
        pieces, tops = [], []
        for t in range(rows // tile):
            scores = nt(q_h[t * tile:(t + 1) * tile], k_h)
            top = jnp.max(scores, axis=-1, keepdims=True)
            pieces.append(nn(jnp.exp(scores - top).astype(jnp.bfloat16), v_h))
            tops.append(top)
        out, top = jnp.concatenate(pieces, axis=0), jnp.concatenate(tops, axis=0)
        other = HEAD_DIM * (1 - parity)
        total = out[:, other:other + 1]
        outs.append(out / total)
        stats.append(top + jnp.log(total))
    ctx_ref[:, cols(0)] = jnp.where(lane < HEAD_DIM, outs[0], outs[1]).astype(jnp.bfloat16)
    lse_ref[...] = jnp.where(lane == 2 * j, stats[0], jnp.where(lane == 2 * j + 1, stats[1], lse_ref[...]))


def backward_slab(j, block, ins, work, dk_ref, dv_ref, out_ref):
    qkv_ref, other_ref, ctx_ref, grad_ref, lse_ref = ins
    extra_ref, k_ref, v_ref, q_ref, g_ref, kt_ref, dq_ref = work
    rows, width = ctx_ref.shape
    low = jnp.bfloat16
    lane = lax.broadcasted_iota(jnp.int32, (1, 128), 1)
    sub = lax.broadcasted_iota(jnp.int32, (128, 1), 0)
    cols = lambda base: pl.ds(base + 128 * j if isinstance(j, int) else pl.multiple_of(base + 128 * j, 128), 128)
    keys = jnp.concatenate([qkv_ref[:, cols(width)], other_ref[:, cols(0)]], axis=0)
    values = jnp.concatenate([qkv_ref[:, cols(2 * width)], other_ref[:, cols(width)]], axis=0)
    queries = qkv_ref[:, cols(0)] * jnp.bfloat16(HEAD_DIM ** -0.5)
    grads = grad_ref[:, cols(0)]
    along = grads.astype(jnp.float32) * ctx_ref[:, cols(0)].astype(jnp.float32)
    lse = lse_ref[...]
    for parity in range(2):
        mine = (lane < HEAD_DIM) if parity == 0 else (lane >= HEAD_DIM)
        at = lane - HEAD_DIM * (1 - parity)
        delta = jnp.sum(jnp.where(mine, along, 0.0), axis=-1, keepdims=True)
        stat = jnp.sum(jnp.where(lane == 2 * j + parity, lse, 0.0), axis=-1, keepdims=True)
        s0, s1, s2 = split3(stat)
        d0, d1, d2 = split3(delta)
        q_more = jnp.where(at == 0, 1.0, jnp.where(at == 1, s0, jnp.where(at == 2, s1, jnp.where(at == 3, s2, 0.0)))).astype(low)
        g_more = jnp.where(at == 1, d0, jnp.where(at == 2, d1, jnp.where(at == 3, d2, 0.0))).astype(low)
        k_ref[parity] = jnp.where(mine, keys, extra_ref[parity])
        v_ref[parity] = jnp.where(mine, values, extra_ref[parity])
        q_ref[parity] = jnp.where(mine, queries, q_more)
        g_ref[parity] = jnp.where(mine, grads, g_more)
        kt_ref[parity] = jnp.where((sub < HEAD_DIM) if parity == 0 else (sub >= HEAD_DIM), keys.T, jnp.zeros((128, 2 * rows), low))
    dq_ref[...] = jnp.zeros_like(dq_ref)

    def part(b, carry):
        span = pl.ds(pl.multiple_of(b * block, block), block)
        made = []
        for parity in range(2):
            q_h, g_h = q_ref[parity], g_ref[parity]
            prob = jnp.exp(nt(k_ref[parity, span, :], q_h))
            slope = nt(v_ref[parity, span, :], g_h)
            ds = (prob * slope).astype(low)
            dv = nn(prob.astype(low), g_h)
            dk = nn(ds, q_h)
            dq_ref[...] += nn(kt_ref[parity, :, span], ds)
            made.append((dk, dv))
        dk_ref[span, :] = jnp.where(lane < HEAD_DIM, made[0][0], made[1][0])
        dv_ref[span, :] = jnp.where(lane < HEAD_DIM, made[0][1], made[1][1])
        return carry

    lax.fori_loop(0, 2 * rows // block, part, 0)
    out_ref[:, cols(0)] = (dq_ref[...].T * (HEAD_DIM ** -0.5)).astype(low)


def backward_work(rows):
    low = lambda *shape: pltpu.VMEM(shape, jnp.bfloat16)
    return [
        low(2, 2 * rows, 128), low(2, 2 * rows, 128), low(2, 2 * rows, 128), low(2, rows, 128), low(2, rows, 128),
        low(2, 128, 2 * rows), pltpu.VMEM((128, rows), jnp.float32),
    ]


class Give:
    def __init__(self, peer, dk_ref, dv_ref, got_ref, out_ref, rows, width, sems):
        self.peer, self.pair, self.got_ref, self.out_ref = peer, (dk_ref, dv_ref), got_ref, out_ref
        self.rows, self.width, (self.send, self.recv) = rows, width, sems

    def copy(self, j, which):
        return pltpu.make_async_remote_copy(
            src_ref=self.pair[which].at[j % 2, pl.ds(self.rows, self.rows)], dst_ref=self.got_ref.at[j, which],
            send_sem=self.send.at[j, which], recv_sem=self.recv.at[j, which], device_id=self.peer, device_id_type=MESH,
        )

    def start(self, j):
        for which in range(2):
            self.copy(j, which).start()

    def take(self, j):
        for which in range(2):
            self.copy(j, which).wait()
            total = self.pair[which][j % 2, pl.ds(0, self.rows), :] + self.got_ref[j, which]
            self.out_ref[:, pl.ds((1 + which) * self.width + j * 128, 128)] = total.astype(jnp.bfloat16)


def forward_kernel(tile, length_ref, qkv_ref, ctx_ref, lse_ref, other_ref, extra_ref, send, recv):
    seq = lax.axis_index("seq")
    core, side = lax.rem(seq, 2), lax.div(seq, 2)
    peer = (lax.axis_index("dp"), flip(seq, 1))
    rows, width = ctx_ref.shape
    greet_sibling(peer)
    swap = pltpu.make_async_remote_copy(
        src_ref=qkv_ref.at[:, pl.ds(width, 2 * width)], dst_ref=other_ref, send_sem=send, recv_sem=recv,
        device_id=peer, device_id_type=MESH,
    )
    swap.start()
    key_extra(extra_ref, jnp.where(side == 0, length_ref[0], length_ref[1]), core, 2 * rows, 0)
    swap.wait()
    lse_ref[...] = jnp.zeros_like(lse_ref)

    def slab(j, carry):
        forward_slab(j, tile, qkv_ref, other_ref, extra_ref, ctx_ref, lse_ref)
        return carry

    lax.fori_loop(0, width // 128, slab, 0)


def attend_forward(lengths, qkv):
    rows, width = qkv.shape[0], qkv.shape[1] // 3
    vmem = pl.BlockSpec(memory_space=pltpu.VMEM)
    return pl.pallas_call(
        functools.partial(forward_kernel, min(256, rows)),
        out_shape=[
            jax.ShapeDtypeStruct((rows, width), jnp.bfloat16),
            jax.ShapeDtypeStruct((rows, 128), jnp.float32),
            jax.ShapeDtypeStruct((rows, 2 * width), jnp.bfloat16),
        ],
        in_specs=[pl.BlockSpec(memory_space=pltpu.SMEM), vmem],
        out_specs=[vmem] * 3,
        scratch_shapes=[pltpu.VMEM((2, 2 * rows, 128), jnp.bfloat16), pltpu.SemaphoreType.DMA, pltpu.SemaphoreType.DMA],
        compiler_params=pltpu.CompilerParams(collective_id=1, has_side_effects=True, vmem_limit_bytes=48 << 20),
        name="attend_forward",
    )(lengths, qkv)


def backward_kernel(block, length_ref, *refs):
    ins, out_ref, work, (dk_ref, dv_ref, got_ref, send, recv) = refs[:5], refs[5], refs[6:13], refs[13:]
    seq = lax.axis_index("seq")
    core, side = lax.rem(seq, 2), lax.div(seq, 2)
    peer = (lax.axis_index("dp"), flip(seq, 1))
    rows, width = ins[2].shape
    greet_sibling(peer)
    key_extra(work[0], jnp.where(side == 0, length_ref[0], length_ref[1]), core, 2 * rows, 0)
    give = Give(peer, dk_ref, dv_ref, got_ref, out_ref, rows, width, (send, recv))
    for j in range(width // 128):
        if j >= 2:
            give.take(j - 2)
        backward_slab(j, block, ins, work, dk_ref.at[j % 2], dv_ref.at[j % 2], out_ref)
        give.start(j)
    for j in range(width // 128 - 2, width // 128):
        give.take(j)


def attend_backward(lengths, qkv, other, ctx, grad, lse):
    rows, width = ctx.shape
    slabs = width // 128
    vmem = pl.BlockSpec(memory_space=pltpu.VMEM)
    return pl.pallas_call(
        functools.partial(backward_kernel, min(256, rows)),
        out_shape=jax.ShapeDtypeStruct(qkv.shape, jnp.bfloat16),
        in_specs=[pl.BlockSpec(memory_space=pltpu.SMEM)] + [vmem] * 5,
        out_specs=vmem,
        scratch_shapes=backward_work(rows) + give_scratch(rows, slabs),
        compiler_params=pltpu.CompilerParams(collective_id=2, has_side_effects=True, vmem_limit_bytes=56 << 20),
        name="attend_backward",
    )(lengths, qkv, other, ctx, grad, lse)


def give_scratch(rows, slabs):
    full = lambda *shape: pltpu.VMEM(shape, jnp.float32)
    return [
        full(2, 2 * rows, 128), full(2, 2 * rows, 128), full(slabs, 2, rows, 128),
        pltpu.SemaphoreType.DMA((slabs, 2)), pltpu.SemaphoreType.DMA((slabs, 2)),
    ]


def encode_kernel(dp_size, plan, window, tile, length_ref, *refs):
    srcs, vec, rows_in, cot_in = refs[:6], refs[6], refs[7], refs[8]
    dsts, flat_vec, bias_up, rows_out, cot_out, qkv_ref, ctx_ref, lse_ref, other_ref = refs[9:13], *refs[13:21]
    (send, recv, local, vec_buf, vec_send, vec_recv, vec_local, swap_sem, w_buf, x_buf, load_sem,
     extra_ref, kv_send, kv_recv) = refs[21:]
    place = Place(dp_size)
    rows, width = ctx_ref.shape
    place.greet()
    moves = [Swap(place, a, b, swap_sem.at[i, 0], swap_sem.at[i, 1], swap_sem.at[i, 2])
             for i, (a, b) in enumerate(((rows_in, rows_out), (cot_in, cot_out)))]
    spread = Spread(place, vec, vec_buf, (vec_send, vec_recv, vec_local))
    units = weight_units(place, srcs, dsts, plan, (send, recv, local))
    steps = gather_steps(units, window)

    def run(i):
        for call in steps[i]:
            call()

    spread.start()
    moves[0].start()
    run(0)
    spread.forward()
    run(1)
    key_extra(extra_ref, jnp.where(place.side == 0, length_ref[0], length_ref[1]), place.core, 2 * rows, 0)
    lse_ref[...] = jnp.zeros_like(lse_ref)
    run(2)
    spread.finish()
    lane = lax.broadcasted_iota(jnp.int32, (8, 128), 1)
    total = jnp.zeros((8, width), jnp.float32)
    share = width // dp_size
    for owner in range(dp_size):
        piece = jnp.where(lane < share, vec_buf[owner // 2, owner % 2, 0:8, :], 0.0)
        padded = jnp.concatenate([piece, jnp.zeros((8, width - 128), jnp.float32)], axis=1)
        total = total + (pltpu.roll(padded, owner * share, 1) if owner else padded)
    flat_vec[...] = total
    wide = bias_up.shape[1] // dp_size // 128
    for owner in range(dp_size):
        for i in range(wide):
            bias_up[:, pl.ds((owner * wide + i) * 128, 128)] = vec_buf[owner // 2, owner % 2, 8 + i:9 + i, :]
    run(3)
    moves[0].wait()
    load_x = pltpu.make_async_copy(rows_out, x_buf, load_sem.at[3])
    load_x.start()
    loads = [pltpu.make_async_copy(dsts[0].at[:, :, :, pl.ds(p[6], width)], w_buf.at[:, :, :, pl.ds(p[6], width)], load_sem.at[i])
             for i, p in enumerate(plan[:3])]
    units[0].arrive()
    loads[0].start()
    run(4)
    for i in range(1, 3):
        units[i].arrive()
        loads[i].start()
    load_x.wait()
    step = 256

    def project(first, count):
        def body(t, carry):
            cols = pl.ds(pl.multiple_of(first + t * step, step), step)
            weight = w_buf[:, :, :, cols].reshape(width, step)
            qkv_ref[:, cols] = nn(x_buf[...], weight).astype(jnp.bfloat16)
            return carry

        lax.fori_loop(0, count, body, 0)

    def project_bias(first, row):
        def body(t, carry):
            cols = pl.ds(pl.multiple_of(first + t * step, step), step)
            bias = flat_vec[row:row + 1, pl.ds(pl.multiple_of(t * step, step), step)]
            weight = w_buf[:, :, :, cols].reshape(width, step)
            qkv_ref[:, cols] = (nn(x_buf[...], weight) + bias).astype(jnp.bfloat16)
            return carry

        lax.fori_loop(0, width // step, body, 0)

    loads[0].wait()
    project(width, width // step)
    loads[1].wait()
    project_bias(2 * width, 1)
    swap = pltpu.make_async_remote_copy(
        src_ref=qkv_ref.at[:, pl.ds(width, 2 * width)], dst_ref=other_ref, send_sem=kv_send, recv_sem=kv_recv,
        device_id=(place.dp, flip(place.seq, 1)), device_id_type=MESH,
    )
    swap.start()
    loads[2].wait()
    project_bias(0, 0)
    run(5)
    swap.wait()
    slabs = width // 128
    for j in range(slabs):
        forward_slab(j, tile, qkv_ref, other_ref, extra_ref, ctx_ref, lse_ref)
        if 6 + j < len(steps):
            run(6 + j)
        if j == 1:
            moves[1].start()
    for i in range(6 + slabs, len(steps)):
        run(i)
    for unit in units[3:]:
        unit.arrive()
    for unit in units:
        unit.finish()
    moves[1].wait()


def encode(dp_size, lengths, weights, dst_shapes, plan, vec, rows_in, cotangent, window=3):
    groups, length, width = rows_in.shape
    rows, z, slots = groups * length, dp_size // 2, dp_size // 2
    anywhere, vmem = pl.BlockSpec(memory_space=pl.ANY), pl.BlockSpec(memory_space=pltpu.VMEM)
    low = lambda *shape: jax.ShapeDtypeStruct(shape, jnp.bfloat16)
    full = lambda *shape: jax.ShapeDtypeStruct(shape, jnp.float32)
    dma = pltpu.SemaphoreType.DMA
    hidden = dst_shapes[2][1]
    return pl.pallas_call(
        functools.partial(encode_kernel, dp_size, plan, window, min(256, rows)),
        out_shape=[low(z, 2, *shape) for shape in dst_shapes] + [
            full(8, width), full(1, hidden), low(rows, width), low(rows, width), low(rows, 3 * width), low(rows, width),
            full(rows, 128), low(rows, 2 * width),
        ],
        in_specs=[pl.BlockSpec(memory_space=pltpu.SMEM)] + [anywhere] * 9,
        out_specs=[anywhere] * 4 + [vmem, vmem, anywhere, anywhere, vmem, vmem, vmem, vmem],
        scratch_shapes=gather_sems(dp_size, len(plan)) + [
            pltpu.VMEM((z, 2, *vec.shape), jnp.float32), dma((slots,)), dma((slots,)), dma, dma((2, 3)),
            pltpu.VMEM((z, 2, *dst_shapes[0]), jnp.bfloat16), pltpu.VMEM((rows, width), jnp.bfloat16), dma((4,)),
            pltpu.VMEM((2, 2 * rows, 128), jnp.bfloat16), dma, dma,
        ],
        compiler_params=pltpu.CompilerParams(collective_id=0, has_side_effects=True, vmem_limit_bytes=56 << 20),
        name="encode",
    )(lengths, *weights, vec, rows_in, cotangent)


def decode_kernel(dp_size, plan, loads, block, length_ref, *refs):
    ins, x_ref, w_ref, base_ref, small_in, parts, layer_in = refs[:5], *refs[5:9], refs[9:12], refs[12]
    outs, small_out, layer_out, input_out = refs[13:19], *refs[19:22]
    scratch = refs[22:]
    work, (dk_ref, dv_ref, got_ref, give_send, give_recv) = scratch[:7], scratch[7:12]
    d_ref, grad_ref, xt_ref, rows_ref, small_ref = scratch[12:17]
    reduce_refs, small_scratch, swap_sem = scratch[17:26], scratch[26:30], scratch[30]
    place = Place(dp_size)
    rows, width = ins[2].shape
    slabs = width // 128
    place.greet()
    give = Give((place.dp, flip(place.seq, 1)), dk_ref, dv_ref, got_ref, d_ref, rows, width, (give_send, give_recv))
    moves = [SwapBack(place, a, b, swap_sem.at[i, 0], swap_sem.at[i, 1], swap_sem.at[i, 2])
             for i, (a, b) in enumerate(((layer_in, layer_out), (rows_ref, input_out)))]
    units = reduce_units(place, (*parts, grad_ref), outs, plan, loads, reduce_refs)
    small = SumAll(place, small_ref, small_out, *small_scratch)
    steps, first = reduce_steps(units)

    def run(tick):
        for call in steps[tick - first]:
            call()

    moves[0].start()
    for tick in range(first, 0):
        run(tick)
    key_extra(work[0], jnp.where(place.side == 0, length_ref[0], length_ref[1]), place.core, 2 * rows, 0)
    for j in range(slabs):
        if j >= 2:
            give.take(j - 2)
        run(j)
        backward_slab(j, block, ins, work, dk_ref.at[j % 2], dv_ref.at[j % 2], d_ref)
        give.start(j)
    xt_ref[...] = x_ref[...].T
    run(slabs)
    for j in range(slabs - 2, slabs):
        give.take(j)
    step = 256

    def weight_part(t, carry):
        cols = pl.ds(pl.multiple_of(t * step, step), step)
        value = nn(xt_ref[...], d_ref[:, cols]).astype(jnp.bfloat16)
        grad_ref[:, :, :, cols] = value.reshape(*grad_ref.shape[:3], step)
        return carry

    lax.fori_loop(0, 3 * width // step, weight_part, 0)
    small_ref[...] = small_in[...]
    small_ref[0:1, :] = jnp.sum(d_ref[:, pl.ds(0, width)].astype(jnp.float32), axis=0, keepdims=True)
    small_ref[1:2, :] = jnp.sum(d_ref[:, pl.ds(2 * width, width)].astype(jnp.float32), axis=0, keepdims=True)
    small.begin()
    run(slabs + 1)

    def input_part(t, carry):
        cols = pl.ds(pl.multiple_of(t * step, step), step)
        value = base_ref[:, cols] + nt(d_ref[...], w_ref[cols, :])
        rows_ref[:, cols] = value.astype(jnp.bfloat16)
        return carry

    lax.fori_loop(0, width // step, input_part, 0)
    moves[1].start()
    last = first + len(steps)
    for i, tick in enumerate(range(slabs + 2, last)):
        run(tick)
        if i < 4:
            small.advance(i)
    small.finish()
    for move in moves:
        move.wait()


def decode(dp_size, lengths, ins, x, qkv_w, base, small, parts, layer_rows, out_shapes, plan, rows_shape):
    rows, width = x.shape
    z, loads = dp_size // 2, sum(1 for p in plan if p[0] < len(parts))
    slabs, dma = width // 128, pltpu.SemaphoreType.DMA
    anywhere, vmem = pl.BlockSpec(memory_space=pl.ANY), pl.BlockSpec(memory_space=pltpu.VMEM)
    low = lambda *shape: pltpu.VMEM(shape, jnp.bfloat16)
    full = lambda *shape: pltpu.VMEM(shape, jnp.float32)
    return pl.pallas_call(
        functools.partial(decode_kernel, dp_size, plan, loads, min(256, rows)),
        out_shape=[jax.ShapeDtypeStruct(s, jnp.float32) for s in out_shapes] + [jax.ShapeDtypeStruct(small.shape, small.dtype)]
        + [jax.ShapeDtypeStruct(rows_shape, jnp.bfloat16)] * 2,
        in_specs=[pl.BlockSpec(memory_space=pltpu.SMEM)] + [vmem] * 9 + [anywhere] * 4,
        out_specs=[anywhere] * 6 + [vmem, anywhere, anywhere],
        scratch_shapes=backward_work(rows) + give_scratch(rows, slabs) + [
            low(rows, 3 * width), low(z, 2, plan[0][3], 3 * width), low(width, rows), low(rows, width), full(*small.shape),
        ] + reduce_scratch(dp_size, len(plan), loads, plan[0][3], width) + [
            full(4, *small.shape), full(z + 2, *small.shape), dma((z + 2,)), dma((z + 2,)), dma((2, 3)),
        ],
        compiler_params=pltpu.CompilerParams(collective_id=3, has_side_effects=True, vmem_limit_bytes=61 << 20),
        name="decode",
    )(lengths, *ins, x, qkv_w, base, small, *parts, layer_rows)


def matmul(a, b):
    return jnp.dot(a, b, preferred_element_type=jnp.float32)


def inner_rows(a, b):
    return lax.dot_general(a, b, (((0,), (0,)), ((), ())), preferred_element_type=jnp.float32)


def times_transposed(a, b):
    return lax.dot_general(a, b, (((1,), (1,)), ((), ())), preferred_element_type=jnp.float32)


def swap_rows(rows):
    side = lax.div(lax.axis_index("seq"), 2)
    size = lax.axis_size("seq")
    got = lax.ppermute(lax.dynamic_index_in_dim(rows, 1 - side, 0, False), "seq", [(i, i ^ 2) for i in range(size)])
    kept = lax.dynamic_index_in_dim(rows, side, 0, False)
    first = jnp.where(side == 0, kept, got)
    second = jnp.where(side == 0, got, kept)
    return jnp.concatenate([first, second], axis=0)


def swap_rows_back(rows):
    side = lax.div(lax.axis_index("seq"), 2)
    size = lax.axis_size("seq")
    blocks = rows.reshape(2, rows.shape[0] // 2, rows.shape[1])
    got = lax.ppermute(lax.dynamic_index_in_dim(blocks, 1 - side, 0, False), "seq", [(i, i ^ 2) for i in range(size)])
    kept = lax.dynamic_index_in_dim(blocks, side, 0, False)
    return jnp.stack([jnp.where(side == 0, kept, got), jnp.where(side == 0, got, kept)])


def pack_vectors(narrow, wide):
    rows = jnp.stack([v.astype(jnp.float32) for v in narrow])
    rows = jnp.pad(rows, ((0, 0), (0, 128 - rows.shape[1])))
    more = wide.astype(jnp.float32).reshape(-1, 128)
    both = jnp.concatenate([rows, more], axis=0)
    return jnp.pad(both, ((0, 16 - both.shape[0]), (0, 0)))


def norm_stats(hidden):
    row_mean = jnp.mean(hidden, axis=-1, keepdims=True)
    centred = hidden - row_mean
    row_var = jnp.mean(centred * centred, axis=-1, keepdims=True)
    scale = lax.rsqrt(row_var + eps_norm)
    return centred * scale, scale


def norm_backward(grad, gain, unit, scale):
    e = grad * gain
    first = jnp.mean(e, axis=-1, keepdims=True)
    second = jnp.mean(e * unit, axis=-1, keepdims=True)
    return scale * (e - first - unit * second)


def col_sum(value):
    return jnp.sum(value, axis=0)


def local(
    inputs, lengths, query_weight, key_weight, value_weight, output_weight, up_weight, down_weight,
    query_bias, value_bias, output_bias, up_bias, down_bias, first_gain, first_shift, second_gain, second_shift, cotangent,
):
    dp_size = lax.axis_size("dp")
    groups, length, width = inputs.shape
    shard = query_weight.shape[0]
    fast = dp_size == 8 and shard == 96 and groups == 2
    rows = groups * length
    seq = lax.axis_index("seq")
    core, side = lax.rem(seq, 2), lax.div(seq, 2)
    narrow = [query_bias, value_bias, output_bias, down_bias, first_gain, first_shift, second_gain, second_shift]
    hidden_width = up_weight.shape[1]
    if fast:
        u = shard
        plan = [(i, 0, 0, u, 0, width, width * i, False) for i in (1, 2, 0)] + [(3, 1, 0, u, 0, width, 0, True)]
        plan += [(4, 2, 0, u, width * j, width, width * j, True) for j in range(hidden_width // width)]
        plan += [(5, 3, u * j, u, 0, width, 0, True) for j in range(down_weight.shape[0] // u)]
        weights = [query_weight, key_weight, value_weight, output_weight, up_weight, down_weight]
        shapes = [(u, 3 * width), (u, width), (u, hidden_width), (down_weight.shape[0], width)]
        qkv_w, out_w, up_w, down_w, flat_vec, bias_up, flat_in, flat_cot, qkv, context, lse, other = encode(
            dp_size, lengths, weights, shapes, plan, pack_vectors(narrow, up_bias), inputs, cotangent
        )
        qkv_w, out_w = qkv_w.reshape(width, 3 * width), out_w.reshape(width, width)
        up_w, down_w, bias_up = up_w.reshape(width, hidden_width), down_w.reshape(hidden_width, width), bias_up[0]
    else:
        gather = lambda a: lax.all_gather(a, "dp", axis=0, tiled=True)
        qkv_w = gather(jnp.concatenate([query_weight, key_weight, value_weight], axis=1))
        out_w, up_w, down_w = gather(output_weight), gather(up_weight), gather(down_weight)
        flat_vec = jnp.stack([gather(v.astype(jnp.float32)) for v in narrow])
        bias_up = gather(up_bias.astype(jnp.float32))
        flat_in, flat_cot = swap_rows(inputs), swap_rows(cotangent)
    bias_q, bias_v, bias_out, bias_down, gain_1, shift_1, gain_2, shift_2 = [flat_vec[i] for i in range(8)]
    if not fast:
        bias_qkv = jnp.concatenate([bias_q, jnp.zeros_like(bias_q), bias_v])
        qkv = (matmul(flat_in, qkv_w) + bias_qkv).astype(jnp.bfloat16)
        context, lse, other = attend_forward(lengths, qkv)
    first_sum = flat_in.astype(jnp.float32) + (matmul(context, out_w) + bias_out)
    unit_1, scale_1 = norm_stats(first_sum)
    first_norm = (unit_1 * gain_1 + shift_1).astype(jnp.bfloat16)
    up_pre = matmul(first_norm, up_w) + bias_up
    below = 0.5 + 0.5 * lax.erf(up_pre * (0.5 ** 0.5))
    hidden_act = (up_pre * below).astype(jnp.bfloat16)
    slope = (below + up_pre * jnp.exp(-0.5 * up_pre * up_pre) * 0.3989422804014327).astype(jnp.bfloat16)
    down_out = matmul(hidden_act, down_w) + bias_down
    second_sum = first_norm.astype(jnp.float32) + down_out
    unit_2, scale_2 = norm_stats(second_sum)
    layer_rows = (unit_2 * gain_2 + shift_2).astype(jnp.bfloat16)

    row = jnp.arange(rows)
    position = lax.rem(row, length) + (core + 2 * lax.div(row, length)) * length
    live = (position < lengths[side]).astype(jnp.float32)
    grad_out = flat_cot.astype(jnp.float32) * live[:, None]
    second_gain_grad, second_shift_grad = col_sum(grad_out * unit_2), col_sum(grad_out)
    second_sum_grad = norm_backward(grad_out, gain_2, unit_2, scale_2)
    down_low = second_sum_grad.astype(jnp.bfloat16)
    low = jnp.bfloat16
    down_w_grad = inner_rows(hidden_act, down_low).astype(low)
    down_bias_grad = col_sum(down_low.astype(jnp.float32))
    up_low = (times_transposed(down_low, down_w) * slope.astype(jnp.float32)).astype(low)
    up_w_grad = inner_rows(first_norm, up_low).astype(low)
    up_bias_grad = col_sum(up_low.astype(jnp.float32))
    norm_grad = second_sum_grad + times_transposed(up_low, up_w)
    first_gain_grad, first_shift_grad = col_sum(norm_grad * unit_1), col_sum(norm_grad)
    first_sum_grad = norm_backward(norm_grad, gain_1, unit_1, scale_1)
    attended_low = first_sum_grad.astype(low)
    out_w_grad = inner_rows(context, attended_low).astype(low)
    out_bias_grad = col_sum(attended_low.astype(jnp.float32))
    context_grad = times_transposed(attended_low, out_w).astype(low)

    if not fast:
        qkv_low = attend_backward(lengths, qkv, other, context, context_grad, lse)
        qkv_w_grad = inner_rows(flat_in, qkv_low)
        qkv_bias_grad = col_sum(qkv_low.astype(jnp.float32))
        input_rows = (first_sum_grad + times_transposed(qkv_low, qkv_w)).astype(low)
    else:
        qkv_bias_grad = jnp.zeros((3 * width,), jnp.float32)

    small = jnp.concatenate([
        jnp.stack([qkv_bias_grad[:width], qkv_bias_grad[2 * width:], out_bias_grad, down_bias_grad, first_gain_grad,
                   first_shift_grad, second_gain_grad, second_shift_grad]),
        up_bias_grad.reshape(-1, width),
    ], axis=0)
    me = lax.axis_index("dp")
    if fast:
        plan = [(0, 5, u * j, u, 0, width, u * j, 0, j > 0) for j in range(down_weight.shape[0] // u)]
        plan += [(1, 4, 0, u, width * j, width, 0, width * j, True) for j in range(hidden_width // width)]
        plan += [(2, 3, 0, u, 0, width, 0, 0, True)] + [(3, i, 0, u, width * i, width, 0, 0, False) for i in range(3)]
        shapes = [(u, width)] * 4 + [up_weight.shape, down_weight.shape]
        parts = [g.reshape(dp_size // 2, 2, -1, g.shape[1]) for g in (down_w_grad, up_w_grad, out_w_grad)]
        small = jnp.pad(small, ((0, 16 - small.shape[0]), (0, 0)))
        *weight_grads, small, layer_out, input_grad = decode(
            dp_size, lengths, (qkv, other, context, context_grad, lse), flat_in, qkv_w, first_sum_grad, small, parts,
            layer_rows, shapes, plan, (groups, length, width)
        )
    else:
        scatter = lambda a: lax.psum(lax.psum_scatter(a.astype(jnp.float32), "dp", scatter_dimension=0, tiled=True), "seq")
        qkv_g = scatter(qkv_w_grad)
        weight_grads = [qkv_g[:, :width], qkv_g[:, width:2 * width], qkv_g[:, 2 * width:]]
        weight_grads += [scatter(out_w_grad), scatter(up_w_grad), scatter(down_w_grad)]
        small = lax.psum(small, ("dp", "seq"))
        layer_out, input_grad = swap_rows_back(layer_rows), swap_rows_back(input_rows)
    part = query_bias.shape[0]
    mine = lax.dynamic_slice(small, (0, me * part), (8, part))
    up_part = up_bias.shape[0]
    up_mine = lax.dynamic_slice(small[8:8 + hidden_width // width].reshape(hidden_width), (me * up_part,), (up_part,))
    return (layer_out, input_grad, *weight_grads, mine[0], mine[1], mine[2], up_mine, *[mine[i] for i in range(3, 8)])


def solution(mesh):
    rows, matrix, vector = P("dp", "seq", None), P("dp", None), P("dp")
    return jax.shard_map(
        local,
        mesh=mesh,
        in_specs=(rows, vector, *[matrix] * 6, *[vector] * 9, rows),
        out_specs=(rows, rows, *[matrix] * 6, *[vector] * 9),
        check_vma=False,
    )
```

```python
import collections
import functools
import jax
import jax.numpy as jnp
from jax import lax
from jax.experimental import pallas as pl
from jax.experimental.pallas import tpu as pltpu
from jax.sharding import PartitionSpec as P

MESH = pl.DeviceIdType.MESH
HEAD_DIM = 64
eps_norm = 1e-05
masked_score = -1000000000.0


def flip(value, bits):
    bit = 1
    while bit <= bits:
        if bits & bit:
            value = value + bit - 2 * bit * lax.rem(lax.div(value, bit), 2)
        bit *= 2
    return value


class Place:
    def __init__(self, dp_size):
        self.dp = lax.axis_index("dp")
        self.seq = lax.axis_index("seq")
        self.depth = dp_size // 2
        self.z = lax.div(self.dp, 2)
        self.y = lax.rem(self.dp, 2)
        self.core = lax.rem(self.seq, 2)
        self.side = lax.div(self.seq, 2)

    def along_z(self, k):
        return flip(self.dp, 2 * k)

    def peers(self):
        result = [(self.along_z(k), self.seq) for k in range(1, self.depth)]
        result.append((flip(self.dp, 1), self.seq))
        result.append((self.dp, flip(self.seq, 1)))
        result.append((self.dp, flip(self.seq, 2)))
        return result

    def greet(self):
        barrier = pltpu.get_barrier_semaphore()
        peers = self.peers()
        for peer in peers:
            pl.semaphore_signal(barrier, inc=1, device_id=peer, device_id_type=MESH)
        pl.semaphore_wait(barrier, len(peers))


class Gather:
    def __init__(self, place, src, dst, rows, columns, to_columns, split, sems):
        self.place, self.src, self.dst = place, src, dst
        self.columns, self.to_columns, self.split = columns, to_columns, split
        self.first, count = rows
        self.send, self.recv, self.local = sems
        self.depth = place.depth
        self.unit = unit = count // 6
        half = place.core * (3 * unit)
        self.half = (half, 3 * unit)
        self.fetch = (half + place.side * unit, 2 * unit) if split else self.half
        self.far = (half + place.side * (2 * unit), unit)

    def view(self, z, y, window):
        rows = pl.ds(pl.multiple_of(self.first + window[0], self.unit), window[1])
        return self.dst.at[z, y, rows, pl.ds(*self.to_columns)]

    def copy(self, src, dst, index, peer):
        return pltpu.make_async_remote_copy(
            src_ref=src, dst_ref=dst, send_sem=self.send.at[index], recv_sem=self.recv.at[index],
            device_id=peer, device_id_type=MESH,
        )

    def mine(self):
        rows = pl.ds(pl.multiple_of(self.first + self.fetch[0], self.unit), self.fetch[1])
        return self.src.at[rows, pl.ds(*self.columns)]

    def own(self):
        p = self.place
        return pltpu.make_async_copy(self.mine(), self.view(p.z, p.y, self.fetch), self.local)

    def over_z(self, k):
        p = self.place
        return self.copy(self.mine(), self.view(p.z, p.y, self.fetch), k, (p.along_z(k), p.seq))

    def over_y(self):
        p = self.place
        ref = self.view(slice(None), p.y, self.fetch)
        return self.copy(ref, ref, 0, (flip(p.dp, 1), p.seq))

    def over_x(self):
        p, every = self.place, slice(None)
        ref = self.view(every, every, self.far)
        return self.copy(ref, ref, self.depth, (p.dp, flip(p.seq, 2)))

    def across(self):
        p, every = self.place, slice(None)
        ref = self.view(every, every, self.half)
        return self.copy(ref, ref, self.depth + 1, (p.dp, flip(p.seq, 1)))

    def stage_z(self):
        self.own().start()
        for k in range(1, self.depth):
            self.over_z(k).start()

    def stage_y(self):
        self.own().wait()
        for k in range(1, self.depth):
            self.over_z(k).wait_recv()
        self.over_y().start()

    def stage_x(self):
        self.over_y().wait_recv()
        if self.split:
            self.over_x().start()
        else:
            self.across().start()

    def stage_core(self):
        if self.split:
            self.over_x().wait_recv()
            self.across().start()

    def arrive(self):
        self.across().wait_recv()

    def finish(self):
        for k in range(1, self.depth):
            self.over_z(k).wait_send()
        self.over_y().wait_send()
        if self.split:
            self.over_x().wait_send()
        self.across().wait_send()


def gather_sems(dp_size, units):
    n = dp_size // 2 + 2
    return [pltpu.SemaphoreType.DMA((units, n)), pltpu.SemaphoreType.DMA((units, n)), pltpu.SemaphoreType.DMA((units,))]


class Spread:
    def __init__(self, place, src, dst, sems):
        self.place, self.src, self.dst = place, src, dst
        self.send, self.recv, self.local = sems

    def own(self):
        return pltpu.make_async_copy(self.src, self.dst.at[self.place.z, self.place.y], self.local)

    def over_z(self, k):
        p = self.place
        return pltpu.make_async_remote_copy(
            src_ref=self.src, dst_ref=self.dst.at[p.z, p.y], send_sem=self.send.at[k], recv_sem=self.recv.at[k],
            device_id=(p.along_z(k), p.seq), device_id_type=MESH,
        )

    def over_y(self):
        p = self.place
        ref = self.dst.at[:, p.y]
        return pltpu.make_async_remote_copy(
            src_ref=ref, dst_ref=ref, send_sem=self.send.at[0], recv_sem=self.recv.at[0],
            device_id=(flip(p.dp, 1), p.seq), device_id_type=MESH,
        )

    def start(self):
        self.own().start()
        for k in range(1, self.place.depth):
            self.over_z(k).start()

    def forward(self):
        self.own().wait()
        for k in range(1, self.place.depth):
            self.over_z(k).wait_recv()
        self.over_y().start()

    def finish(self):
        for k in range(1, self.place.depth):
            self.over_z(k).wait_send()
        self.over_y().wait()


def gather_steps(units, window):
    count = len(units)
    steps = [[unit.stage_z for unit in units[:window]]]
    for i in range(count + 4):
        step = []
        if i < count:
            step.append(units[i].stage_y)
            if i + window < count:
                step.append(units[i + window].stage_z)
        if 0 <= i - 2 < count:
            step.append(units[i - 2].stage_x)
        if 0 <= i - 4 < count:
            step.append(units[i - 4].stage_core)
        steps.append(step)
    return steps


def weight_units(place, srcs, dsts, plan, sems):
    send, recv, local = sems
    return [
        Gather(place, srcs[s], dsts[d], (first, rows), (column, width), (to, width), split, (send.at[i], recv.at[i], local.at[i]))
        for i, (s, d, first, rows, column, width, to, split) in enumerate(plan)
    ]


class Swap:
    def __init__(self, place, src, dst, send, recv, local):
        side = place.side
        length = src.shape[1]
        own = dst.at[pl.ds(pl.multiple_of(side * length, 8), length)]
        self.here = pltpu.make_async_copy(src.at[side], own, local)
        self.there = pltpu.make_async_remote_copy(
            src_ref=src.at[1 - side], dst_ref=own, send_sem=send, recv_sem=recv,
            device_id=(place.dp, flip(place.seq, 2)), device_id_type=MESH,
        )

    def start(self):
        self.here.start()
        self.there.start()

    def wait(self):
        self.here.wait()
        self.there.wait()


class SwapBack:
    def __init__(self, place, src, dst, send, recv, local):
        side, length = place.side, dst.shape[1]
        block = lambda i: src.at[pl.ds(pl.multiple_of(i * length, length), length)]
        self.here = pltpu.make_async_copy(block(side), dst.at[side], local)
        self.there = pltpu.make_async_remote_copy(
            src_ref=block(1 - side), dst_ref=dst.at[side], send_sem=send, recv_sem=recv,
            device_id=(place.dp, flip(place.seq, 2)), device_id_type=MESH,
        )

    def start(self):
        self.here.start()
        self.there.start()

    def wait(self):
        self.here.wait()
        self.there.wait()


class Reduce:
    def __init__(self, place, src, rows, columns, to_columns, out, to_row, split, own, bufs, sems):
        self.place, self.src, self.out, self.split = place, src, out, split
        self.columns, self.to_columns, self.to_row = columns, to_columns, to_row
        self.first, count = rows
        self.unit = unit = count // 6
        self.from_core, self.from_x, self.from_y, self.from_z, self.got, self.total = bufs
        self.send, self.recv = sems
        self.depth = place.depth
        self.half = place.core * (3 * unit)
        self.sibling_half = (1 - place.core) * (3 * unit)
        self.keep = (place.side * unit, 2 * unit) if split else (0, 3 * unit)
        self.loads = own is not None
        self.own = own if self.loads else self.view(self.half)

    def view(self, start):
        rows = pl.ds(pl.multiple_of(self.first + start, self.unit), 3 * self.unit)
        return self.src.at[:, :, rows, pl.ds(*self.columns)]

    def rows(self, window):
        return pl.ds(pl.multiple_of(window[0], self.unit), window[1])

    def copy(self, src, dst, index, peer):
        return pltpu.make_async_remote_copy(
            src_ref=src, dst_ref=dst, send_sem=self.send.at[index], recv_sem=self.recv.at[index],
            device_id=peer, device_id_type=MESH,
        )

    def load(self):
        return pltpu.make_async_copy(self.view(self.half), self.own, self.send.at[0])

    def core(self):
        p = self.place
        return self.copy(self.view(self.sibling_half), self.from_core, self.depth, (p.dp, flip(p.seq, 1)))

    def far(self):
        return ((1 - self.place.side) * (2 * self.unit), self.unit)

    def x(self):
        p = self.place
        return self.copy(self.own.at[:, :, self.rows(self.far())], self.from_x, self.depth + 1, (p.dp, flip(p.seq, 2)))

    def y(self):
        p = self.place
        src = self.own.at[:, 1 - p.y, self.rows(self.keep)]
        return self.copy(src, self.from_y.at[:, pl.ds(0, self.keep[1])], self.depth + 2, (flip(p.dp, 1), p.seq))

    def z(self, k):
        p = self.place
        src = self.own.at[flip(p.z, k), p.y, self.rows(self.keep)]
        return self.copy(src, self.from_z.at[k - 1, pl.ds(0, self.keep[1])], k, (p.along_z(k), p.seq))

    def x_last(self):
        p = self.place
        src = self.own.at[p.z, p.y, self.rows(self.keep)]
        return self.copy(src, self.got.at[pl.ds(0, self.keep[1])], self.depth + 3, (p.dp, flip(p.seq, 2)))

    def place_out(self):
        row = pl.multiple_of(self.to_row + self.half, self.unit)
        return self.out.at[pl.ds(row, 3 * self.unit), pl.ds(*self.to_columns)]

    def put_here(self):
        return pltpu.make_async_copy(self.total, self.place_out(), self.send.at[self.depth + 5])

    def put_there(self):
        p = self.place
        return self.copy(self.total, self.place_out(), self.depth + 4, (p.dp, flip(p.seq, 1)))

    def chip(self, z, y, window):
        rows = self.rows(window)
        return self.own[z, y, rows, :].astype(jnp.float32) + self.from_core[z, y, rows, :].astype(jnp.float32)

    def pieces(self, z, y):
        u, side = self.unit, self.place.side
        if not self.split:
            return [((i * u, u), (i * u, u), self.chip(z, y, (i * u, u))) for i in range(3)]
        solo = (side * (2 * u), u)
        gained = self.chip(z, y, solo) + self.from_x[z, y, :, :].astype(jnp.float32)
        return [((u, u), ((1 - side) * u, u), self.chip(z, y, (u, u))), (solo, (side * u, u), gained)]

    def stage_core(self):
        if self.loads:
            self.load().start()
        self.core().start()

    def stage_x(self):
        if self.loads:
            self.load().wait()
        self.core().wait_recv()
        if not self.split:
            return
        rows = self.rows(self.far())

        def body(z, carry):
            for y in range(2):
                self.own[z, y, rows, :] = self.chip(z, y, self.far()).astype(jnp.bfloat16)
            return carry

        lax.fori_loop(0, self.depth, body, 0)
        self.x().start()

    def stage_y(self):
        if self.split:
            self.x().wait_recv()
        y = 1 - self.place.y

        def body(z, carry):
            for at, _, value in self.pieces(z, y):
                self.own[z, y, self.rows(at), :] = value.astype(jnp.bfloat16)
            return carry

        lax.fori_loop(0, self.depth, body, 0)
        self.y().start()

    def column(self, z):
        return [
            (at, kept, value + self.from_y[z, self.rows(kept), :].astype(jnp.float32))
            for at, kept, value in self.pieces(z, self.place.y)
        ]

    def stage_z(self):
        self.y().wait_recv()
        for k in range(1, self.depth):
            z = flip(self.place.z, k)
            for at, _, value in self.column(z):
                self.own[z, self.place.y, self.rows(at), :] = value.astype(jnp.bfloat16)
            self.z(k).start()

    def stage_last(self):
        for k in range(1, self.depth):
            self.z(k).wait_recv()
        p = self.place
        for at, kept, value in self.column(p.z):
            for k in range(1, self.depth):
                value = value + self.from_z[k - 1, self.rows(kept), :].astype(jnp.float32)
            self.own[p.z, p.y, self.rows(at), :] = value.astype(jnp.bfloat16)
        self.x_last().start()

    def stage_out(self):
        self.x_last().wait_recv()
        p, u = self.place, self.unit
        mine = lambda at: self.own[p.z, p.y, self.rows(at), :].astype(jnp.float32)
        got = lambda at: self.got[self.rows(at), :].astype(jnp.float32)
        if self.split:
            side = p.side
            self.total[self.rows((u, u)), :] = mine((u, u)) + got((side * u, u))
            self.total[self.rows((side * (2 * u), u)), :] = mine((side * (2 * u), u))
            self.total[self.rows((2 * u - side * (2 * u), u)), :] = got(((1 - side) * u, u))
        else:
            whole = (0, 3 * u)
            self.total[...] = mine(whole) + got(whole)
        self.put_here().start()
        self.put_there().start()

    def finish(self):
        self.core().wait_send()
        if self.split:
            self.x().wait_send()
        self.y().wait_send()
        for k in range(1, self.depth):
            self.z(k).wait_send()
        self.x_last().wait_send()
        self.put_here().wait()
        self.put_there().wait()


def reduce_scratch(dp_size, units, loads, rows, width):
    z, u = dp_size // 2, rows // 6
    low = lambda count, *shape: pltpu.VMEM((count, *shape, width), jnp.bfloat16)
    return [
        low(loads, z, 2, 3 * u), low(units, z, 2, 3 * u), low(units, z, 2, u), low(units, z, 3 * u), low(units, z - 1, 3 * u),
        low(units, 3 * u), pltpu.VMEM((units, 3 * u, width), jnp.float32),
        pltpu.SemaphoreType.DMA((units, z + 6)), pltpu.SemaphoreType.DMA((units, z + 6)),
    ]


def reduce_units(place, srcs, outs, plan, loads, scratch):
    own, bufs, send, recv = scratch[0], scratch[1:-2], scratch[-2], scratch[-1]
    return [
        Reduce(place, srcs[s], (first, rows), (column, width), (to, width), outs[o], to_row, split,
               own.at[i] if i < loads else None, [b.at[i] for b in bufs], (send.at[i], recv.at[i]))
        for i, (s, o, first, rows, column, width, to_row, to, split) in enumerate(plan)
    ]


STAGES = ("stage_core", "stage_x", "stage_y", "stage_z", "stage_last", "stage_out", "finish")


def reduce_steps(units):
    first, steps = -3, collections.defaultdict(list)
    for i, unit in enumerate(units):
        lag = 2 if unit.split else 0
        ages = (-3 if unit.loads else -1, 0, lag, lag + 2, lag + 4, lag + 6, lag + 8)
        for stage, age in zip(STAGES, ages):
            steps[i + age].append((-age, getattr(unit, stage)))
    ticks = range(first, max(steps) + 1)
    return [[call for _, call in sorted(steps[tick], key=lambda pair: pair[0])] for tick in ticks], first


class SumAll:
    def __init__(self, place, src, out, buf, got, send, recv):
        self.place, self.src, self.out, self.buf, self.got, self.send, self.recv = place, src, out, buf, got, send, recv

    def copy(self, stage, slot, peer):
        return pltpu.make_async_remote_copy(
            src_ref=self.buf.at[stage], dst_ref=self.got.at[slot], send_sem=self.send.at[slot], recv_sem=self.recv.at[slot],
            device_id=peer, device_id_type=MESH,
        )

    def copies(self, stage):
        p = self.place
        if stage < 3:
            peer = [(p.dp, flip(p.seq, 1)), (p.dp, flip(p.seq, 2)), (flip(p.dp, 1), p.seq)][stage]
            return [self.copy(stage, stage, peer)]
        return [self.copy(3, 2 + k, (p.along_z(k), p.seq)) for k in range(1, p.depth)]

    def begin(self):
        self.buf[0] = self.src[...]
        for c in self.copies(0):
            c.start()

    def advance(self, stage):
        for c in self.copies(stage):
            c.wait_recv()
        if stage < 3:
            self.buf[stage + 1] = self.buf[stage] + self.got[stage]
            for c in self.copies(stage + 1):
                c.start()
        else:
            z, n = self.place.z, self.place.depth
            pick = lambda i: i
            total = self.buf[3]
            parts = [self.buf[3]] + [self.got[2 + k] for k in range(1, n)]
            total = (parts[0] + parts[1]) + (parts[2] + parts[3])
            self.out[...] = total

    def finish(self):
        for stage in range(4):
            for c in self.copies(stage):
                c.wait_send()


def halves(width):
    lane = lax.broadcasted_iota(jnp.int32, (1, width), 1)
    return lane


def key_extra(extra_ref, length, core, rows, first_pos):
    block = rows // 4
    row = lax.broadcasted_iota(jnp.int32, (rows, 128), 0)
    lane = lax.broadcasted_iota(jnp.int32, (rows, 128), 1)
    part = row // block
    owner = jnp.where(part < 2, core, 1 - core)
    position = row - part * block + (owner + 2 * lax.rem(part, 2)) * block
    dead = jnp.where(position < length, 0.0, masked_score)
    for parity in range(2):
        base = HEAD_DIM * (1 - parity)
        at = lane - base
        value = jnp.where(at == 0, dead, jnp.where((at > 0) & (at < 4), -1.0, 0.0))
        extra_ref[parity, :, :] = value.astype(jnp.bfloat16)


def split3(value):
    high = value.astype(jnp.bfloat16).astype(jnp.float32)
    rest = value - high
    mid = rest.astype(jnp.bfloat16).astype(jnp.float32)
    return high, mid, rest - mid


def nt(a, b):
    return lax.dot_general(a, b, (((1,), (1,)), ((), ())), preferred_element_type=jnp.float32)


def nn(a, b):
    return jnp.dot(a, b, preferred_element_type=jnp.float32)


def greet_sibling(peer):
    barrier = pltpu.get_barrier_semaphore()
    pl.semaphore_signal(barrier, inc=1, device_id=peer, device_id_type=MESH)
    pl.semaphore_wait(barrier, 1)


def forward_slab(j, tile, qkv_ref, other_ref, extra_ref, ctx_ref, lse_ref, between=None):
    rows, width = ctx_ref.shape
    lane = lax.broadcasted_iota(jnp.int32, (1, 128), 1)
    cols = lambda base: pl.ds(base + 128 * j if isinstance(j, int) else pl.multiple_of(base + 128 * j, 128), 128)
    keys = jnp.concatenate([qkv_ref[:, cols(width)], other_ref[:, cols(0)]], axis=0)
    values = jnp.concatenate([qkv_ref[:, cols(2 * width)], other_ref[:, cols(width)]], axis=0)
    queries = qkv_ref[:, cols(0)]
    outs, stats = [], []
    for parity in range(2):
        mine = (lane < HEAD_DIM) if parity == 0 else (lane >= HEAD_DIM)
        mark = jnp.where(lane == HEAD_DIM * (1 - parity), 1.0, 0.0).astype(jnp.bfloat16)
        k_h = jnp.where(mine, keys, extra_ref[parity])
        v_h = jnp.where(mine, values, jnp.ones_like(values))
        q_h = jnp.where(mine, queries * jnp.bfloat16(HEAD_DIM ** -0.5), mark)
        pieces, tops = [], []
        for t in range(rows // tile):
            scores = nt(q_h[t * tile:(t + 1) * tile], k_h)
            top = jnp.max(scores, axis=-1, keepdims=True)
            pieces.append(nn(jnp.exp(scores - top).astype(jnp.bfloat16), v_h))
            tops.append(top)
        out, top = jnp.concatenate(pieces, axis=0), jnp.concatenate(tops, axis=0)
        other = HEAD_DIM * (1 - parity)
        total = out[:, other:other + 1]
        outs.append(out / total)
        stats.append(top + jnp.log(total))
        if between is not None:
            between()
    ctx_ref[:, cols(0)] = jnp.where(lane < HEAD_DIM, outs[0], outs[1]).astype(jnp.bfloat16)
    lse_ref[...] = jnp.where(lane == 2 * j, stats[0], jnp.where(lane == 2 * j + 1, stats[1], lse_ref[...]))


def backward_slab(j, block, ins, work, dk_ref, dv_ref, out_ref, between=None):
    qkv_ref, other_ref, ctx_ref, grad_ref, lse_ref = ins
    extra_ref, k_ref, v_ref, q_ref, g_ref, kt_ref, dq_ref = work
    rows, width = ctx_ref.shape
    low = jnp.bfloat16
    lane = lax.broadcasted_iota(jnp.int32, (1, 128), 1)
    sub = lax.broadcasted_iota(jnp.int32, (128, 1), 0)
    cols = lambda base: pl.ds(base + 128 * j if isinstance(j, int) else pl.multiple_of(base + 128 * j, 128), 128)
    keys = jnp.concatenate([qkv_ref[:, cols(width)], other_ref[:, cols(0)]], axis=0)
    values = jnp.concatenate([qkv_ref[:, cols(2 * width)], other_ref[:, cols(width)]], axis=0)
    queries = qkv_ref[:, cols(0)] * jnp.bfloat16(HEAD_DIM ** -0.5)
    grads = grad_ref[:, cols(0)]
    along = grads.astype(jnp.float32) * ctx_ref[:, cols(0)].astype(jnp.float32)
    lse = lse_ref[...]
    for parity in range(2):
        mine = (lane < HEAD_DIM) if parity == 0 else (lane >= HEAD_DIM)
        at = lane - HEAD_DIM * (1 - parity)
        delta = jnp.sum(jnp.where(mine, along, 0.0), axis=-1, keepdims=True)
        stat = jnp.sum(jnp.where(lane == 2 * j + parity, lse, 0.0), axis=-1, keepdims=True)
        s0, s1, s2 = split3(stat)
        d0, d1, d2 = split3(delta)
        q_more = jnp.where(at == 0, 1.0, jnp.where(at == 1, s0, jnp.where(at == 2, s1, jnp.where(at == 3, s2, 0.0)))).astype(low)
        g_more = jnp.where(at == 1, d0, jnp.where(at == 2, d1, jnp.where(at == 3, d2, 0.0))).astype(low)
        k_ref[parity] = jnp.where(mine, keys, extra_ref[parity])
        v_ref[parity] = jnp.where(mine, values, extra_ref[parity])
        q_ref[parity] = jnp.where(mine, queries, q_more)
        g_ref[parity] = jnp.where(mine, grads, g_more)
        kt_ref[parity] = jnp.where((sub < HEAD_DIM) if parity == 0 else (sub >= HEAD_DIM), keys.T, jnp.zeros((128, 2 * rows), low))
    dq_ref[...] = jnp.zeros_like(dq_ref)

    def part(b, carry):
        span = pl.ds(pl.multiple_of(b * block, block), block)
        made = []
        for parity in range(2):
            q_h, g_h = q_ref[parity], g_ref[parity]
            prob = jnp.exp(nt(k_ref[parity, span, :], q_h))
            slope = nt(v_ref[parity, span, :], g_h)
            ds = (prob * slope).astype(low)
            dv = nn(prob.astype(low), g_h)
            dk = nn(ds, q_h)
            dq_ref[...] += nn(kt_ref[parity, :, span], ds)
            made.append((dk, dv))
        dk_ref[span, :] = jnp.where(lane < HEAD_DIM, made[0][0], made[1][0])
        dv_ref[span, :] = jnp.where(lane < HEAD_DIM, made[0][1], made[1][1])
        return carry

    count, cuts = 2 * rows // block, (0, 1, 3, 4) if between is not None else (0, 4)
    for low_cut, high_cut in zip(cuts, cuts[1:]):
        if low_cut:
            between()
        lax.fori_loop(low_cut * count // 4, high_cut * count // 4, part, 0)
    out_ref[:, cols(0)] = (dq_ref[...].T * (HEAD_DIM ** -0.5)).astype(low)


def backward_work(rows):
    low = lambda *shape: pltpu.VMEM(shape, jnp.bfloat16)
    return [
        low(2, 2 * rows, 128), low(2, 2 * rows, 128), low(2, 2 * rows, 128), low(2, rows, 128), low(2, rows, 128),
        low(2, 128, 2 * rows), pltpu.VMEM((128, rows), jnp.float32),
    ]


class Give:
    def __init__(self, peer, dk_ref, dv_ref, got_ref, out_ref, rows, width, sems):
        self.peer, self.pair, self.got_ref, self.out_ref = peer, (dk_ref, dv_ref), got_ref, out_ref
        self.rows, self.width, (self.send, self.recv) = rows, width, sems

    def copy(self, j, which):
        return pltpu.make_async_remote_copy(
            src_ref=self.pair[which].at[j % 2, pl.ds(self.rows, self.rows)], dst_ref=self.got_ref.at[j, which],
            send_sem=self.send.at[j, which], recv_sem=self.recv.at[j, which], device_id=self.peer, device_id_type=MESH,
        )

    def start(self, j):
        for which in range(2):
            self.copy(j, which).start()

    def take(self, j):
        for which in range(2):
            self.copy(j, which).wait()
            total = self.pair[which][j % 2, pl.ds(0, self.rows), :] + self.got_ref[j, which]
            self.out_ref[:, pl.ds((1 + which) * self.width + j * 128, 128)] = total.astype(jnp.bfloat16)


def forward_kernel(tile, length_ref, qkv_ref, ctx_ref, lse_ref, other_ref, extra_ref, send, recv):
    seq = lax.axis_index("seq")
    core, side = lax.rem(seq, 2), lax.div(seq, 2)
    peer = (lax.axis_index("dp"), flip(seq, 1))
    rows, width = ctx_ref.shape
    greet_sibling(peer)
    swap = pltpu.make_async_remote_copy(
        src_ref=qkv_ref.at[:, pl.ds(width, 2 * width)], dst_ref=other_ref, send_sem=send, recv_sem=recv,
        device_id=peer, device_id_type=MESH,
    )
    swap.start()
    key_extra(extra_ref, jnp.where(side == 0, length_ref[0], length_ref[1]), core, 2 * rows, 0)
    swap.wait()
    lse_ref[...] = jnp.zeros_like(lse_ref)

    def slab(j, carry):
        forward_slab(j, tile, qkv_ref, other_ref, extra_ref, ctx_ref, lse_ref)
        return carry

    lax.fori_loop(0, width // 128, slab, 0)


def attend_forward(lengths, qkv):
    rows, width = qkv.shape[0], qkv.shape[1] // 3
    vmem = pl.BlockSpec(memory_space=pltpu.VMEM)
    return pl.pallas_call(
        functools.partial(forward_kernel, min(256, rows)),
        out_shape=[
            jax.ShapeDtypeStruct((rows, width), jnp.bfloat16),
            jax.ShapeDtypeStruct((rows, 128), jnp.float32),
            jax.ShapeDtypeStruct((rows, 2 * width), jnp.bfloat16),
        ],
        in_specs=[pl.BlockSpec(memory_space=pltpu.SMEM), vmem],
        out_specs=[vmem] * 3,
        scratch_shapes=[pltpu.VMEM((2, 2 * rows, 128), jnp.bfloat16), pltpu.SemaphoreType.DMA, pltpu.SemaphoreType.DMA],
        compiler_params=pltpu.CompilerParams(collective_id=1, has_side_effects=True, vmem_limit_bytes=48 << 20),
        name="attend_forward",
    )(lengths, qkv)


def backward_kernel(block, length_ref, *refs):
    ins, out_ref, work, (dk_ref, dv_ref, got_ref, send, recv) = refs[:5], refs[5], refs[6:13], refs[13:]
    seq = lax.axis_index("seq")
    core, side = lax.rem(seq, 2), lax.div(seq, 2)
    peer = (lax.axis_index("dp"), flip(seq, 1))
    rows, width = ins[2].shape
    greet_sibling(peer)
    key_extra(work[0], jnp.where(side == 0, length_ref[0], length_ref[1]), core, 2 * rows, 0)
    give = Give(peer, dk_ref, dv_ref, got_ref, out_ref, rows, width, (send, recv))
    for j in range(width // 128):
        if j >= 2:
            give.take(j - 2)
        backward_slab(j, block, ins, work, dk_ref.at[j % 2], dv_ref.at[j % 2], out_ref)
        give.start(j)
    for j in range(width // 128 - 2, width // 128):
        give.take(j)


def attend_backward(lengths, qkv, other, ctx, grad, lse):
    rows, width = ctx.shape
    slabs = width // 128
    vmem = pl.BlockSpec(memory_space=pltpu.VMEM)
    return pl.pallas_call(
        functools.partial(backward_kernel, min(256, rows)),
        out_shape=jax.ShapeDtypeStruct(qkv.shape, jnp.bfloat16),
        in_specs=[pl.BlockSpec(memory_space=pltpu.SMEM)] + [vmem] * 5,
        out_specs=vmem,
        scratch_shapes=backward_work(rows) + give_scratch(rows, slabs),
        compiler_params=pltpu.CompilerParams(collective_id=2, has_side_effects=True, vmem_limit_bytes=56 << 20),
        name="attend_backward",
    )(lengths, qkv, other, ctx, grad, lse)


def give_scratch(rows, slabs):
    full = lambda *shape: pltpu.VMEM(shape, jnp.float32)
    return [
        full(2, 2 * rows, 128), full(2, 2 * rows, 128), full(slabs, 2, rows, 128),
        pltpu.SemaphoreType.DMA((slabs, 2)), pltpu.SemaphoreType.DMA((slabs, 2)),
    ]


def encode_kernel(dp_size, plan, window, tile, length_ref, *refs):
    srcs, vec, rows_in, cot_in = refs[:6], refs[6], refs[7], refs[8]
    weights_out, flat_vec, bias_up, rows_out, cot_out, qkv_ref, ctx_ref, lse_ref, other_ref = refs[9:13], *refs[13:21]
    (send, recv, local, vec_buf, vec_send, vec_recv, vec_local, swap_sem, *bufs, x_buf, cot_buf, out_sem,
     extra_ref, kv_send, kv_recv) = refs[21:]
    w_buf = bufs[0]
    place = Place(dp_size)
    rows, width = ctx_ref.shape
    place.greet()
    moves = [Swap(place, a, b, swap_sem.at[i, 0], swap_sem.at[i, 1], swap_sem.at[i, 2])
             for i, (a, b) in enumerate(((rows_in, x_buf), (cot_in, cot_buf)))]
    spread = Spread(place, vec, vec_buf, (vec_send, vec_recv, vec_local))
    units = weight_units(place, srcs, bufs, plan, (send, recv, local))
    steps = gather_steps(units, window)
    puts = [pltpu.make_async_copy(a, b, out_sem.at[i])
            for i, (a, b) in enumerate(zip((*bufs, x_buf, cot_buf), (*weights_out, rows_out, cot_out)))]
    clock = iter(steps)

    def run(count=1):
        for _ in range(count):
            for call in next(clock, ()):
                call()

    spread.start()
    moves[0].start()
    run()
    spread.forward()
    run()
    key_extra(extra_ref, jnp.where(place.side == 0, length_ref[0], length_ref[1]), place.core, 2 * rows, 0)
    lse_ref[...] = jnp.zeros_like(lse_ref)
    run()
    spread.finish()
    lane = lax.broadcasted_iota(jnp.int32, (8, 128), 1)
    total = jnp.zeros((8, width), jnp.float32)
    share = width // dp_size
    for owner in range(dp_size):
        piece = jnp.where(lane < share, vec_buf[owner // 2, owner % 2, 0:8, :], 0.0)
        padded = jnp.concatenate([piece, jnp.zeros((8, width - 128), jnp.float32)], axis=1)
        total = total + (pltpu.roll(padded, owner * share, 1) if owner else padded)
    flat_vec[...] = total
    wide = bias_up.shape[1] // dp_size // 128
    for owner in range(dp_size):
        for i in range(wide):
            bias_up[:, pl.ds((owner * wide + i) * 128, 128)] = vec_buf[owner // 2, owner % 2, 8 + i:9 + i, :]
    run(9)
    moves[0].wait()
    puts[4].start()

    def fetch(first):
        for i in range(first, first + 2):
            units[i].arrive()

    step = 256

    def project(first, count):
        def body(t, carry):
            cols = pl.ds(pl.multiple_of(first + t * step, step), step)
            weight = w_buf[:, :, :, cols].reshape(width, step)
            qkv_ref[:, cols] = nn(x_buf[...], weight).astype(jnp.bfloat16)
            return carry

        lax.fori_loop(0, count, body, 0)

    def project_bias(first, row):
        def body(t, carry):
            cols = pl.ds(pl.multiple_of(first + t * step, step), step)
            bias = flat_vec[row:row + 1, pl.ds(pl.multiple_of(t * step, step), step)]
            weight = w_buf[:, :, :, cols].reshape(width, step)
            qkv_ref[:, cols] = (nn(x_buf[...], weight) + bias).astype(jnp.bfloat16)
            return carry

        lax.fori_loop(0, width // step, body, 0)

    fetch(0)
    project(width, width // step)
    run()
    fetch(2)
    project_bias(2 * width, 1)
    swap = pltpu.make_async_remote_copy(
        src_ref=qkv_ref.at[:, pl.ds(width, 2 * width)], dst_ref=other_ref, send_sem=kv_send, recv_sem=kv_recv,
        device_id=(place.dp, flip(place.seq, 1)), device_id_type=MESH,
    )
    swap.start()
    run()
    fetch(4)
    project_bias(0, 0)
    run()
    swap.wait()
    for j in range(width // 128):
        forward_slab(j, tile, qkv_ref, other_ref, extra_ref, ctx_ref, lse_ref, run)
        if j == 1:
            moves[1].start()
    puts[0].start()
    run(len(steps))
    for i in range(1, 4):
        for unit, cut in zip(units, plan):
            if cut[1] == i:
                unit.arrive()
        puts[i].start()
    moves[1].wait()
    puts[5].start()
    for unit in units:
        unit.finish()
    for put in puts:
        put.wait()


def encode(dp_size, lengths, weights, dst_shapes, plan, vec, rows_in, cotangent, window=3):
    groups, length, width = rows_in.shape
    rows, z, slots = groups * length, dp_size // 2, dp_size // 2
    anywhere, vmem = pl.BlockSpec(memory_space=pl.ANY), pl.BlockSpec(memory_space=pltpu.VMEM)
    low = lambda *shape: jax.ShapeDtypeStruct(shape, jnp.bfloat16)
    full = lambda *shape: jax.ShapeDtypeStruct(shape, jnp.float32)
    dma = pltpu.SemaphoreType.DMA
    hidden = dst_shapes[2][1]
    return pl.pallas_call(
        functools.partial(encode_kernel, dp_size, plan, window, min(256, rows)),
        out_shape=[low(z, 2, *shape) for shape in dst_shapes] + [
            full(8, width), full(1, hidden), low(rows, width), low(rows, width), low(rows, 3 * width), low(rows, width),
            full(rows, 128), low(rows, 2 * width),
        ],
        in_specs=[pl.BlockSpec(memory_space=pltpu.SMEM)] + [anywhere] * 9,
        out_specs=[anywhere] * 4 + [vmem, vmem, anywhere, anywhere, vmem, vmem, vmem, vmem],
        scratch_shapes=gather_sems(dp_size, len(plan)) + [
            pltpu.VMEM((z, 2, *vec.shape), jnp.float32), dma((slots,)), dma((slots,)), dma, dma((2, 3)),
            *[pltpu.VMEM((z, 2, *shape), jnp.bfloat16) for shape in dst_shapes],
            pltpu.VMEM((rows, width), jnp.bfloat16), pltpu.VMEM((rows, width), jnp.bfloat16), dma((6,)),
            pltpu.VMEM((2, 2 * rows, 128), jnp.bfloat16), dma, dma,
        ],
        compiler_params=pltpu.CompilerParams(collective_id=0, has_side_effects=True, vmem_limit_bytes=56 << 20),
        name="encode",
    )(lengths, *weights, vec, rows_in, cotangent)


def decode_kernel(dp_size, plan, loads, block, length_ref, *refs):
    ins, late, small_in, parts, layer_in = refs[:5], refs[5:8], refs[8], refs[9:12], refs[12]
    outs, vec_outs, layer_out, input_out = refs[13:19], refs[19:28], *refs[28:30]
    scratch = refs[30:]
    work, (dk_ref, dv_ref, got_ref, give_send, give_recv) = scratch[:7], scratch[7:12]
    d_ref, grad_ref, xt_ref, rows_ref, small_ref = scratch[12:17]
    reduce_refs, small_scratch, swap_sem, small_out = scratch[17:26], scratch[26:30], scratch[30], scratch[31]
    x_ref, w_ref, base_ref, load_sem = scratch[32:]
    loads_in = [pltpu.make_async_copy(a, b, load_sem.at[i]) for i, (a, b) in enumerate(zip(late, (x_ref, w_ref, base_ref)))]
    place = Place(dp_size)
    rows, width = ins[2].shape
    slabs = width // 128
    place.greet()
    give = Give((place.dp, flip(place.seq, 1)), dk_ref, dv_ref, got_ref, d_ref, rows, width, (give_send, give_recv))
    moves = [SwapBack(place, a, b, swap_sem.at[i, 0], swap_sem.at[i, 1], swap_sem.at[i, 2])
             for i, (a, b) in enumerate(((layer_in, layer_out), (rows_ref, input_out)))]
    units = reduce_units(place, (*parts, grad_ref), outs, plan, loads, reduce_refs)
    small = SumAll(place, small_ref, small_out, *small_scratch)
    steps, first = reduce_steps(units)

    def run(tick):
        for call in steps[tick - first]:
            call()

    clock = iter(range(first, first + len(steps)))

    def tick(count=1):
        for _ in range(count):
            run(next(clock))

    moves[0].start()
    for load in loads_in:
        load.start()
    tick(-first)
    key_extra(work[0], jnp.where(place.side == 0, length_ref[0], length_ref[1]), place.core, 2 * rows, 0)
    for j in range(slabs):
        if j >= 2:
            give.take(j - 2)
        if j < slabs - 1:
            tick()
        backward_slab(j, block, ins, work, dk_ref.at[j % 2], dv_ref.at[j % 2], d_ref, tick if j < slabs - 1 else None)
        give.start(j)
    for load in loads_in:
        load.wait()
    xt_ref[...] = x_ref[...].T
    tick()
    for j in range(slabs - 2, slabs):
        give.take(j)
    step = 256

    def weight_part(t, carry):
        cols = pl.ds(pl.multiple_of(t * step, step), step)
        value = nn(xt_ref[...], d_ref[:, cols]).astype(jnp.bfloat16)
        grad_ref[:, :, :, cols] = value.reshape(*grad_ref.shape[:3], step)
        return carry

    parts_of = 3 * width // step
    lax.fori_loop(0, parts_of // 2, weight_part, 0)
    tick()
    lax.fori_loop(parts_of // 2, parts_of, weight_part, 0)
    small_ref[...] = small_in[...]
    small_ref[0:1, :] = jnp.sum(d_ref[:, pl.ds(0, width)].astype(jnp.float32), axis=0, keepdims=True)
    small_ref[1:2, :] = jnp.sum(d_ref[:, pl.ds(2 * width, width)].astype(jnp.float32), axis=0, keepdims=True)
    small.begin()
    tick()

    def input_part(t, carry):
        cols = pl.ds(pl.multiple_of(t * step, step), step)
        value = base_ref[:, cols] + nt(d_ref[...], w_ref[cols, :])
        rows_ref[:, cols] = value.astype(jnp.bfloat16)
        return carry

    lax.fori_loop(0, width // step, input_part, 0)
    moves[1].start()
    for i, now in enumerate(clock):
        run(now)
        if i % 2 and i < 8:
            small.advance(i // 2)
    small.finish()
    share = width // dp_size
    turned = pltpu.roll(small_out[0:8, :], lax.rem(width - place.dp * share, width), 1)
    for i in range(8):
        vec_outs[i][...] = turned[i:i + 1, 0:share]
    wide = small_out[pl.ds(8 + place.z, 1), :]
    vec_outs[8][...] = jnp.where(place.y == 0, wide[:, :width // 2], wide[:, width // 2:])
    for move in moves:
        move.wait()


def decode(dp_size, lengths, ins, x, qkv_w, base, small, parts, layer_rows, out_shapes, plan, rows_shape):
    rows, width = x.shape
    z, loads = dp_size // 2, sum(1 for p in plan if p[0] < len(parts))
    slabs, dma = width // 128, pltpu.SemaphoreType.DMA
    anywhere, vmem = pl.BlockSpec(memory_space=pl.ANY), pl.BlockSpec(memory_space=pltpu.VMEM)
    low = lambda *shape: pltpu.VMEM(shape, jnp.bfloat16)
    full = lambda *shape: pltpu.VMEM(shape, jnp.float32)
    return pl.pallas_call(
        functools.partial(decode_kernel, dp_size, plan, loads, min(256, rows)),
        out_shape=[jax.ShapeDtypeStruct(s, jnp.float32) for s in out_shapes] + [jax.ShapeDtypeStruct((1, width // dp_size), jnp.float32)] * 8
        + [jax.ShapeDtypeStruct((1, width // 2), jnp.float32)] + [jax.ShapeDtypeStruct(rows_shape, jnp.bfloat16)] * 2,
        in_specs=[pl.BlockSpec(memory_space=pltpu.SMEM)] + [vmem] * 5 + [anywhere] * 3 + [vmem] + [anywhere] * 3 + [vmem],
        out_specs=[anywhere] * 6 + [vmem] * 9 + [anywhere] * 2,
        scratch_shapes=backward_work(rows) + give_scratch(rows, slabs) + [
            low(rows, 3 * width), low(z, 2, plan[0][3], 3 * width), low(width, rows), low(rows, width), full(*small.shape),
        ] + reduce_scratch(dp_size, len(plan), loads, plan[0][3], plan[0][5]) + [
            full(4, *small.shape), full(z + 2, *small.shape), dma((z + 2,)), dma((z + 2,)), dma((2, 3)), full(*small.shape),
            low(rows, width), low(width, 3 * width), full(rows, width), dma((3,)),
        ],
        compiler_params=pltpu.CompilerParams(collective_id=3, has_side_effects=True, vmem_limit_bytes=61 << 20),
        name="decode",
    )(lengths, *ins, x, qkv_w, base, small, *parts, layer_rows)


def settle_kernel(count, *refs):
    srcs, dsts, bufs, sem = refs[:count], refs[count:2 * count], refs[2 * count:3 * count], refs[3 * count]
    gets = [pltpu.make_async_copy(a, b, sem.at[0, i]) for i, (a, b) in enumerate(zip(srcs, bufs))]
    puts = [pltpu.make_async_copy(a.at[0] if len(a.shape) > len(b.shape) else a, b, sem.at[1, i])
            for i, (a, b) in enumerate(zip(bufs, dsts))]
    for get in gets:
        get.start()
    for get, put in zip(gets, puts):
        get.wait()
        put.start()
    for put in puts:
        put.wait()


def settle(arrays):
    count = len(arrays)
    anywhere = pl.BlockSpec(memory_space=pl.ANY)
    shape = lambda a: a.shape[1:] if a.shape[0] == 1 else a.shape
    return pl.pallas_call(
        functools.partial(settle_kernel, count),
        out_shape=[jax.ShapeDtypeStruct(shape(a), a.dtype) for a in arrays],
        in_specs=[anywhere] * count,
        out_specs=[anywhere] * count,
        scratch_shapes=[pltpu.VMEM(a.shape, a.dtype) for a in arrays] + [pltpu.SemaphoreType.DMA((2, count))],
        compiler_params=pltpu.CompilerParams(vmem_limit_bytes=61 << 20),
        name="settle",
    )(*arrays)


def matmul(a, b):
    return jnp.dot(a, b, preferred_element_type=jnp.float32)


def inner_rows(a, b):
    return lax.dot_general(a, b, (((0,), (0,)), ((), ())), preferred_element_type=jnp.float32)


def times_transposed(a, b):
    return lax.dot_general(a, b, (((1,), (1,)), ((), ())), preferred_element_type=jnp.float32)


def swap_rows(rows):
    side = lax.div(lax.axis_index("seq"), 2)
    size = lax.axis_size("seq")
    got = lax.ppermute(lax.dynamic_index_in_dim(rows, 1 - side, 0, False), "seq", [(i, i ^ 2) for i in range(size)])
    kept = lax.dynamic_index_in_dim(rows, side, 0, False)
    first = jnp.where(side == 0, kept, got)
    second = jnp.where(side == 0, got, kept)
    return jnp.concatenate([first, second], axis=0)


def swap_rows_back(rows):
    side = lax.div(lax.axis_index("seq"), 2)
    size = lax.axis_size("seq")
    blocks = rows.reshape(2, rows.shape[0] // 2, rows.shape[1])
    got = lax.ppermute(lax.dynamic_index_in_dim(blocks, 1 - side, 0, False), "seq", [(i, i ^ 2) for i in range(size)])
    kept = lax.dynamic_index_in_dim(blocks, side, 0, False)
    return jnp.stack([jnp.where(side == 0, kept, got), jnp.where(side == 0, got, kept)])


def pack_vectors(narrow, wide):
    rows = jnp.stack([v.astype(jnp.float32) for v in narrow])
    rows = jnp.pad(rows, ((0, 0), (0, 128 - rows.shape[1])))
    more = wide.astype(jnp.float32).reshape(-1, 128)
    both = jnp.concatenate([rows, more], axis=0)
    return jnp.pad(both, ((0, 16 - both.shape[0]), (0, 0)))


def norm_stats(hidden):
    row_mean = jnp.mean(hidden, axis=-1, keepdims=True)
    centred = hidden - row_mean
    row_var = jnp.mean(centred * centred, axis=-1, keepdims=True)
    scale = lax.rsqrt(row_var + eps_norm)
    return centred * scale, scale


def norm_backward(grad, gain, unit, scale):
    e = grad * gain
    first = jnp.mean(e, axis=-1, keepdims=True)
    second = jnp.mean(e * unit, axis=-1, keepdims=True)
    return scale * (e - first - unit * second)


def col_sum(value):
    return jnp.sum(value, axis=0)


def local(
    inputs, lengths, query_weight, key_weight, value_weight, output_weight, up_weight, down_weight,
    query_bias, value_bias, output_bias, up_bias, down_bias, first_gain, first_shift, second_gain, second_shift, cotangent,
):
    dp_size = lax.axis_size("dp")
    groups, length, width = inputs.shape
    shard = query_weight.shape[0]
    fast = dp_size == 8 and shard == 96 and groups == 2
    rows = groups * length
    seq = lax.axis_index("seq")
    core, side = lax.rem(seq, 2), lax.div(seq, 2)
    narrow = [query_bias, value_bias, output_bias, down_bias, first_gain, first_shift, second_gain, second_shift]
    hidden_width = up_weight.shape[1]
    if fast:
        u = shard
        half = width // 2
        cuts = [(i, 0, 0, 0, width * i) for i in (1, 2, 0)] + [(3, 1, 0, 0, 0)]
        cuts += [(4, 2, 0, width * j, width * j) for j in range(hidden_width // width)]
        cuts += [(5, 3, u * j, 0, 0) for j in range(down_weight.shape[0] // u)]
        plan = [(s, d, row, u, col + half * h, half, to + half * h) for s, d, row, col, to in cuts for h in range(2)]
        plan = [(*p, i < len(plan) - 6) for i, p in enumerate(plan)]
        weights = [query_weight, key_weight, value_weight, output_weight, up_weight, down_weight]
        shapes = [(u, 3 * width), (u, width), (u, hidden_width), (down_weight.shape[0], width)]
        qkv_w, out_w, up_w, down_w, flat_vec, bias_up, flat_in, flat_cot, qkv, context, lse, other = encode(
            dp_size, lengths, weights, shapes, plan, pack_vectors(narrow, up_bias), inputs, cotangent
        )
        qkv_w, out_w = qkv_w.reshape(width, 3 * width), out_w.reshape(width, width)
        up_w, down_w, bias_up = up_w.reshape(width, hidden_width), down_w.reshape(hidden_width, width), bias_up[0]
    else:
        gather = lambda a: lax.all_gather(a, "dp", axis=0, tiled=True)
        qkv_w = gather(jnp.concatenate([query_weight, key_weight, value_weight], axis=1))
        out_w, up_w, down_w = gather(output_weight), gather(up_weight), gather(down_weight)
        flat_vec = jnp.stack([gather(v.astype(jnp.float32)) for v in narrow])
        bias_up = gather(up_bias.astype(jnp.float32))
        flat_in, flat_cot = swap_rows(inputs), swap_rows(cotangent)
    bias_q, bias_v, bias_out, bias_down, gain_1, shift_1, gain_2, shift_2 = [flat_vec[i] for i in range(8)]
    if not fast:
        bias_qkv = jnp.concatenate([bias_q, jnp.zeros_like(bias_q), bias_v])
        qkv = (matmul(flat_in, qkv_w) + bias_qkv).astype(jnp.bfloat16)
        context, lse, other = attend_forward(lengths, qkv)
    first_sum = flat_in.astype(jnp.float32) + (matmul(context, out_w) + bias_out)
    unit_1, scale_1 = norm_stats(first_sum)
    first_norm = (unit_1 * gain_1 + shift_1).astype(jnp.bfloat16)
    up_pre = matmul(first_norm, up_w) + bias_up
    below = 0.5 + 0.5 * lax.erf(up_pre * (0.5 ** 0.5))
    hidden_act = (up_pre * below).astype(jnp.bfloat16)
    slope = (below + up_pre * jnp.exp(-0.5 * up_pre * up_pre) * 0.3989422804014327).astype(jnp.bfloat16)
    down_out = matmul(hidden_act, down_w) + bias_down
    second_sum = first_norm.astype(jnp.float32) + down_out
    unit_2, scale_2 = norm_stats(second_sum)
    layer_rows = (unit_2 * gain_2 + shift_2).astype(jnp.bfloat16)

    row = jnp.arange(rows)
    position = lax.rem(row, length) + (core + 2 * lax.div(row, length)) * length
    live = (position < lengths[side]).astype(jnp.float32)
    grad_out = flat_cot.astype(jnp.float32) * live[:, None]
    second_gain_grad, second_shift_grad = col_sum(grad_out * unit_2), col_sum(grad_out)
    second_sum_grad = norm_backward(grad_out, gain_2, unit_2, scale_2)
    down_low = second_sum_grad.astype(jnp.bfloat16)
    low = jnp.bfloat16
    down_w_grad = inner_rows(hidden_act, down_low).astype(low)
    down_bias_grad = col_sum(down_low.astype(jnp.float32))
    up_low = (times_transposed(down_low, down_w) * slope.astype(jnp.float32)).astype(low)
    up_w_grad = inner_rows(first_norm, up_low).astype(low)
    up_bias_grad = col_sum(up_low.astype(jnp.float32))
    norm_grad = second_sum_grad + times_transposed(up_low, up_w)
    first_gain_grad, first_shift_grad = col_sum(norm_grad * unit_1), col_sum(norm_grad)
    first_sum_grad = norm_backward(norm_grad, gain_1, unit_1, scale_1)
    attended_low = first_sum_grad.astype(low)
    out_w_grad = inner_rows(context, attended_low).astype(low)
    out_bias_grad = col_sum(attended_low.astype(jnp.float32))
    context_grad = times_transposed(attended_low, out_w).astype(low)

    if not fast:
        qkv_low = attend_backward(lengths, qkv, other, context, context_grad, lse)
        qkv_w_grad = inner_rows(flat_in, qkv_low)
        qkv_bias_grad = col_sum(qkv_low.astype(jnp.float32))
        input_rows = (first_sum_grad + times_transposed(qkv_low, qkv_w)).astype(low)
    else:
        qkv_bias_grad = jnp.zeros((3 * width,), jnp.float32)

    small = jnp.concatenate([
        jnp.stack([qkv_bias_grad[:width], qkv_bias_grad[2 * width:], out_bias_grad, down_bias_grad, first_gain_grad,
                   first_shift_grad, second_gain_grad, second_shift_grad]),
        up_bias_grad.reshape(-1, width),
    ], axis=0)
    me = lax.axis_index("dp")
    if fast:
        cuts = [(0, 5, u * j, 0, u * j, 0) for j in range(down_weight.shape[0] // u)]
        cuts += [(1, 4, 0, width * j, 0, width * j) for j in range(hidden_width // width)]
        cuts += [(2, 3, 0, 0, 0, 0)] + [(3, i, 0, width * i, 0, 0) for i in range(3)]
        plan = [(s, o, row, u, col + half * h, half, to_row, to + half * h) for s, o, row, col, to_row, to in cuts for h in range(2)]
        plan = [(*p, 2 <= i < len(plan) - 8) for i, p in enumerate(plan)]
        shapes = [(u, width)] * 4 + [up_weight.shape, down_weight.shape]
        parts = [g.reshape(dp_size // 2, 2, -1, g.shape[1]) for g in (down_w_grad, up_w_grad, out_w_grad)]
        small = jnp.pad(small, ((0, 16 - small.shape[0]), (0, 0)))
        *mine, layer_out, input_grad = decode(
            dp_size, lengths, (qkv, other, context, context_grad, lse), flat_in, qkv_w, first_sum_grad, small, parts,
            layer_rows, shapes, plan, (groups, length, width)
        )
        layer_out, input_grad, *mine = settle((layer_out, input_grad, *mine))
        weight_grads, mine = mine[:6], mine[6:]
        up_mine = mine.pop()
    else:
        scatter = lambda a: lax.psum(lax.psum_scatter(a.astype(jnp.float32), "dp", scatter_dimension=0, tiled=True), "seq")
        qkv_g = scatter(qkv_w_grad)
        weight_grads = [qkv_g[:, :width], qkv_g[:, width:2 * width], qkv_g[:, 2 * width:]]
        weight_grads += [scatter(out_w_grad), scatter(up_w_grad), scatter(down_w_grad)]
        small = lax.psum(small, ("dp", "seq"))
        layer_out, input_grad = swap_rows_back(layer_rows), swap_rows_back(input_rows)
        part = query_bias.shape[0]
        mine = list(lax.dynamic_slice(small, (0, me * part), (8, part)))
        up_part = up_bias.shape[0]
        up_mine = lax.dynamic_slice(small[8:8 + hidden_width // width].reshape(hidden_width), (me * up_part,), (up_part,))
    return (layer_out, input_grad, *weight_grads, mine[0], mine[1], mine[2], up_mine, *mine[3:8])


def solution(mesh):
    rows, matrix, vector = P("dp", "seq", None), P("dp", None), P("dp")
    return jax.shard_map(
        local,
        mesh=mesh,
        in_specs=(rows, vector, *[matrix] * 6, *[vector] * 9, rows),
        out_specs=(rows, rows, *[matrix] * 6, *[vector] * 9),
        check_vma=False,
    )
```

```python
import collections
import functools
import jax
import jax.numpy as jnp
from jax import lax
from jax.experimental import pallas as pl
from jax.experimental.pallas import tpu as pltpu
from jax.sharding import PartitionSpec as P

MESH = pl.DeviceIdType.MESH
HEAD_DIM = 64
eps_norm = 1e-05
masked_score = -1000000000.0


def flip(value, bits):
    bit = 1
    while bit <= bits:
        if bits & bit:
            value = value + bit - 2 * bit * lax.rem(lax.div(value, bit), 2)
        bit *= 2
    return value


class Place:
    def __init__(self, dp_size):
        self.dp = lax.axis_index("dp")
        self.seq = lax.axis_index("seq")
        self.depth = dp_size // 2
        self.z = lax.div(self.dp, 2)
        self.y = lax.rem(self.dp, 2)
        self.core = lax.rem(self.seq, 2)
        self.side = lax.div(self.seq, 2)

    def along_z(self, k):
        return flip(self.dp, 2 * k)

    def peers(self):
        result = [(self.along_z(k), self.seq) for k in range(1, self.depth)]
        result.append((flip(self.dp, 1), self.seq))
        result.append((self.dp, flip(self.seq, 1)))
        result.append((self.dp, flip(self.seq, 2)))
        return result

    def greet(self):
        barrier = pltpu.get_barrier_semaphore()
        peers = self.peers()
        for peer in peers:
            pl.semaphore_signal(barrier, inc=1, device_id=peer, device_id_type=MESH)
        pl.semaphore_wait(barrier, len(peers))


class Gather:
    def __init__(self, place, src, dst, rows, columns, to_columns, split, sems):
        self.place, self.src, self.dst = place, src, dst
        self.columns, self.to_columns, self.split = columns, to_columns, split
        self.first, count = rows
        self.send, self.recv, self.local = sems
        self.depth = place.depth
        self.unit = unit = count // 6
        half = place.core * (3 * unit)
        self.half = (half, 3 * unit)
        self.fetch = (half + place.side * unit, 2 * unit) if split else self.half
        self.far = (half + place.side * (2 * unit), unit)

    def view(self, z, y, window):
        rows = pl.ds(pl.multiple_of(self.first + window[0], self.unit), window[1])
        return self.dst.at[z, y, rows, pl.ds(*self.to_columns)]

    def copy(self, src, dst, index, peer):
        return pltpu.make_async_remote_copy(
            src_ref=src, dst_ref=dst, send_sem=self.send.at[index], recv_sem=self.recv.at[index],
            device_id=peer, device_id_type=MESH,
        )

    def mine(self):
        rows = pl.ds(pl.multiple_of(self.first + self.fetch[0], self.unit), self.fetch[1])
        return self.src.at[rows, pl.ds(*self.columns)]

    def own(self):
        p = self.place
        return pltpu.make_async_copy(self.mine(), self.view(p.z, p.y, self.fetch), self.local)

    def over_z(self, k):
        p = self.place
        return self.copy(self.mine(), self.view(p.z, p.y, self.fetch), k, (p.along_z(k), p.seq))

    def over_y(self):
        p = self.place
        ref = self.view(slice(None), p.y, self.fetch)
        return self.copy(ref, ref, 0, (flip(p.dp, 1), p.seq))

    def over_x(self):
        p, every = self.place, slice(None)
        ref = self.view(every, every, self.far)
        return self.copy(ref, ref, self.depth, (p.dp, flip(p.seq, 2)))

    def across(self):
        p, every = self.place, slice(None)
        ref = self.view(every, every, self.half)
        return self.copy(ref, ref, self.depth + 1, (p.dp, flip(p.seq, 1)))

    def stage_z(self):
        self.own().start()
        for k in range(1, self.depth):
            self.over_z(k).start()

    def stage_y(self):
        self.own().wait()
        for k in range(1, self.depth):
            self.over_z(k).wait_recv()
        self.over_y().start()

    def stage_x(self):
        self.over_y().wait_recv()
        if self.split:
            self.over_x().start()
        else:
            self.across().start()

    def stage_core(self):
        if self.split:
            self.over_x().wait_recv()
            self.across().start()

    def arrive(self):
        self.across().wait_recv()

    def finish(self):
        for k in range(1, self.depth):
            self.over_z(k).wait_send()
        self.over_y().wait_send()
        if self.split:
            self.over_x().wait_send()
        self.across().wait_send()


def gather_sems(dp_size, units):
    n = dp_size // 2 + 2
    return [pltpu.SemaphoreType.DMA((units, n)), pltpu.SemaphoreType.DMA((units, n)), pltpu.SemaphoreType.DMA((units,))]


class Spread:
    def __init__(self, place, src, dst, sems):
        self.place, self.src, self.dst = place, src, dst
        self.send, self.recv, self.local = sems

    def own(self):
        return pltpu.make_async_copy(self.src, self.dst.at[self.place.z, self.place.y], self.local)

    def over_z(self, k):
        p = self.place
        return pltpu.make_async_remote_copy(
            src_ref=self.src, dst_ref=self.dst.at[p.z, p.y], send_sem=self.send.at[k], recv_sem=self.recv.at[k],
            device_id=(p.along_z(k), p.seq), device_id_type=MESH,
        )

    def over_y(self):
        p = self.place
        ref = self.dst.at[:, p.y]
        return pltpu.make_async_remote_copy(
            src_ref=ref, dst_ref=ref, send_sem=self.send.at[0], recv_sem=self.recv.at[0],
            device_id=(flip(p.dp, 1), p.seq), device_id_type=MESH,
        )

    def start(self):
        self.own().start()
        for k in range(1, self.place.depth):
            self.over_z(k).start()

    def forward(self):
        self.own().wait()
        for k in range(1, self.place.depth):
            self.over_z(k).wait_recv()
        self.over_y().start()

    def finish(self):
        for k in range(1, self.place.depth):
            self.over_z(k).wait_send()
        self.over_y().wait()


def gather_steps(units, window):
    count = len(units)
    steps = [[unit.stage_z for unit in units[:window]]]
    for i in range(count + 4):
        step = []
        if i < count:
            step.append(units[i].stage_y)
            if i + window < count:
                step.append(units[i + window].stage_z)
        if 0 <= i - 2 < count:
            step.append(units[i - 2].stage_x)
        if 0 <= i - 4 < count:
            step.append(units[i - 4].stage_core)
        steps.append(step)
    return steps


def weight_units(place, srcs, dsts, plan, sems):
    send, recv, local = sems
    return [
        Gather(place, srcs[s], dsts[d], (first, rows), (column, width), (to, width), split, (send.at[i], recv.at[i], local.at[i]))
        for i, (s, d, first, rows, column, width, to, split) in enumerate(plan)
    ]


class Swap:
    def __init__(self, place, src, dst, send, recv, local):
        side = place.side
        length = src.shape[1]
        own = dst.at[pl.ds(pl.multiple_of(side * length, 8), length)]
        self.here = pltpu.make_async_copy(src.at[side], own, local)
        self.there = pltpu.make_async_remote_copy(
            src_ref=src.at[1 - side], dst_ref=own, send_sem=send, recv_sem=recv,
            device_id=(place.dp, flip(place.seq, 2)), device_id_type=MESH,
        )

    def start(self):
        self.here.start()
        self.there.start()

    def wait(self):
        self.here.wait()
        self.there.wait()


class SwapBack:
    def __init__(self, place, src, dst, send, recv, local):
        side, length = place.side, dst.shape[1]
        block = lambda i: src.at[pl.ds(pl.multiple_of(i * length, length), length)]
        self.here = pltpu.make_async_copy(block(side), dst.at[side], local)
        self.there = pltpu.make_async_remote_copy(
            src_ref=block(1 - side), dst_ref=dst.at[side], send_sem=send, recv_sem=recv,
            device_id=(place.dp, flip(place.seq, 2)), device_id_type=MESH,
        )

    def start(self):
        self.here.start()
        self.there.start()

    def wait(self):
        self.here.wait()
        self.there.wait()


class Reduce:
    def __init__(self, place, src, rows, columns, targets, to_row, split, own, bufs, sems):
        self.place, self.src, self.targets, self.split = place, src, targets, split
        self.columns, self.to_row = columns, to_row
        self.first, count = rows
        self.unit = unit = count // 6
        self.from_core, self.from_x, self.from_y, self.from_z, self.got, self.total = bufs
        self.send, self.recv = sems
        self.depth = place.depth
        self.half = place.core * (3 * unit)
        self.sibling_half = (1 - place.core) * (3 * unit)
        self.keep = (place.side * unit, 2 * unit) if split else (0, 3 * unit)
        self.loads = own is not None
        self.own = own if self.loads else self.view(self.half)

    def view(self, start):
        rows = pl.ds(pl.multiple_of(self.first + start, self.unit), 3 * self.unit)
        return self.src.at[:, :, rows, pl.ds(*self.columns)]

    def rows(self, window):
        return pl.ds(pl.multiple_of(window[0], self.unit), window[1])

    def copy(self, src, dst, index, peer):
        return pltpu.make_async_remote_copy(
            src_ref=src, dst_ref=dst, send_sem=self.send.at[index], recv_sem=self.recv.at[index],
            device_id=peer, device_id_type=MESH,
        )

    def load(self):
        return pltpu.make_async_copy(self.view(self.half), self.own, self.send.at[0])

    def core(self):
        p = self.place
        return self.copy(self.view(self.sibling_half), self.from_core, self.depth, (p.dp, flip(p.seq, 1)))

    def far(self):
        return ((1 - self.place.side) * (2 * self.unit), self.unit)

    def x(self):
        p = self.place
        return self.copy(self.own.at[:, :, self.rows(self.far())], self.from_x, self.depth + 1, (p.dp, flip(p.seq, 2)))

    def y(self):
        p = self.place
        src = self.own.at[:, 1 - p.y, self.rows(self.keep)]
        return self.copy(src, self.from_y.at[:, pl.ds(0, self.keep[1])], self.depth + 2, (flip(p.dp, 1), p.seq))

    def z(self, k):
        p = self.place
        src = self.own.at[flip(p.z, k), p.y, self.rows(self.keep)]
        return self.copy(src, self.from_z.at[k - 1, pl.ds(0, self.keep[1])], k, (p.along_z(k), p.seq))

    def x_last(self):
        p = self.place
        src = self.own.at[p.z, p.y, self.rows(self.keep)]
        return self.copy(src, self.got.at[pl.ds(0, self.keep[1])], self.depth + 3, (p.dp, flip(p.seq, 2)))

    def puts(self):
        p, n = self.place, self.depth
        rows = pl.ds(pl.multiple_of(self.to_row + self.half, self.unit), 3 * self.unit)
        here, there = [], []
        for i, (column, width, out, to) in enumerate(self.targets):
            src, dst = self.total.at[:, pl.ds(column, width)], out.at[rows, pl.ds(to, width)]
            here.append(pltpu.make_async_copy(src, dst, self.send.at[n + 6 + i]))
            there.append(self.copy(src, dst, n + 4 + i, (p.dp, flip(p.seq, 1))))
        return here + there

    def chip(self, z, y, window):
        rows = self.rows(window)
        return self.own[z, y, rows, :].astype(jnp.float32) + self.from_core[z, y, rows, :].astype(jnp.float32)

    def pieces(self, z, y):
        u, side = self.unit, self.place.side
        if not self.split:
            return [((i * u, u), (i * u, u), self.chip(z, y, (i * u, u))) for i in range(3)]
        solo = (side * (2 * u), u)
        gained = self.chip(z, y, solo) + self.from_x[z, y, :, :].astype(jnp.float32)
        return [((u, u), ((1 - side) * u, u), self.chip(z, y, (u, u))), (solo, (side * u, u), gained)]

    def stage_core(self):
        if self.loads:
            self.load().start()
        self.core().start()

    def stage_x(self):
        if self.loads:
            self.load().wait()
        self.core().wait_recv()
        if not self.split:
            return
        rows = self.rows(self.far())

        def body(z, carry):
            for y in range(2):
                self.own[z, y, rows, :] = self.chip(z, y, self.far()).astype(jnp.bfloat16)
            return carry

        lax.fori_loop(0, self.depth, body, 0)
        self.x().start()

    def stage_y(self):
        if self.split:
            self.x().wait_recv()
        y = 1 - self.place.y

        def body(z, carry):
            for at, _, value in self.pieces(z, y):
                self.own[z, y, self.rows(at), :] = value.astype(jnp.bfloat16)
            return carry

        lax.fori_loop(0, self.depth, body, 0)
        self.y().start()

    def column(self, z):
        return [
            (at, kept, value + self.from_y[z, self.rows(kept), :].astype(jnp.float32))
            for at, kept, value in self.pieces(z, self.place.y)
        ]

    def stage_z(self):
        self.y().wait_recv()
        for k in range(1, self.depth):
            z = flip(self.place.z, k)
            for at, _, value in self.column(z):
                self.own[z, self.place.y, self.rows(at), :] = value.astype(jnp.bfloat16)
            self.z(k).start()

    def stage_last(self):
        for k in range(1, self.depth):
            self.z(k).wait_recv()
        p = self.place
        for at, kept, value in self.column(p.z):
            for k in range(1, self.depth):
                value = value + self.from_z[k - 1, self.rows(kept), :].astype(jnp.float32)
            self.own[p.z, p.y, self.rows(at), :] = value.astype(jnp.bfloat16)
        self.x_last().start()

    def stage_out(self):
        self.x_last().wait_recv()
        p, u = self.place, self.unit
        mine = lambda at: self.own[p.z, p.y, self.rows(at), :].astype(jnp.float32)
        got = lambda at: self.got[self.rows(at), :].astype(jnp.float32)
        if self.split:
            side = p.side
            self.total[self.rows((u, u)), :] = mine((u, u)) + got((side * u, u))
            self.total[self.rows((side * (2 * u), u)), :] = mine((side * (2 * u), u))
            self.total[self.rows((2 * u - side * (2 * u), u)), :] = got(((1 - side) * u, u))
        else:
            whole = (0, 3 * u)
            self.total[...] = mine(whole) + got(whole)
        for put in self.puts():
            put.start()

    def finish(self):
        self.core().wait_send()
        if self.split:
            self.x().wait_send()
        self.y().wait_send()
        for k in range(1, self.depth):
            self.z(k).wait_send()
        self.x_last().wait_send()
        for put in self.puts():
            put.wait()


def reduce_scratch(dp_size, units, loads, rows, width):
    z, u = dp_size // 2, rows // 6
    low = lambda count, *shape: pltpu.VMEM((count, *shape, width), jnp.bfloat16)
    return [
        low(loads, z, 2, 3 * u), low(units, z, 2, 3 * u), low(units, z, 2, u), low(units, z, 3 * u), low(units, z - 1, 3 * u),
        low(units, 3 * u), pltpu.VMEM((units, 3 * u, width), jnp.float32),
        pltpu.SemaphoreType.DMA((units, z + 8)), pltpu.SemaphoreType.DMA((units, z + 8)),
    ]


def reduce_units(place, srcs, outs, plan, loads, scratch):
    own, bufs, send, recv = scratch[0], scratch[1:-2], scratch[-2], scratch[-1]
    return [
        Reduce(place, srcs[s], (first, rows), (column, width), [(a, w, outs[o], to) for a, w, o, to in targets], to_row, split,
               own.at[i] if i < loads else None, [b.at[i] for b in bufs], (send.at[i], recv.at[i]))
        for i, (s, first, rows, column, width, to_row, targets, split) in enumerate(plan)
    ]


STAGES = ("stage_core", "stage_x", "stage_y", "stage_z", "stage_last", "stage_out", "finish")


def reduce_steps(units):
    first, steps = -3, collections.defaultdict(list)
    for i, unit in enumerate(units):
        lag = 2 if unit.split else 0
        ages = (-3 if unit.loads else -1, 0, lag, lag + 2, lag + 4, lag + 6, lag + 8)
        for stage, age in zip(STAGES, ages):
            steps[i + age].append((-age, getattr(unit, stage)))
    ticks = range(first, max(steps) + 1)
    return [[call for _, call in sorted(steps[tick], key=lambda pair: pair[0])] for tick in ticks], first


class SumAll:
    def __init__(self, place, src, out, buf, got, send, recv):
        self.place, self.src, self.out, self.buf, self.got, self.send, self.recv = place, src, out, buf, got, send, recv

    def copy(self, stage, slot, peer):
        return pltpu.make_async_remote_copy(
            src_ref=self.buf.at[stage], dst_ref=self.got.at[slot], send_sem=self.send.at[slot], recv_sem=self.recv.at[slot],
            device_id=peer, device_id_type=MESH,
        )

    def copies(self, stage):
        p = self.place
        if stage < 3:
            peer = [(p.dp, flip(p.seq, 1)), (p.dp, flip(p.seq, 2)), (flip(p.dp, 1), p.seq)][stage]
            return [self.copy(stage, stage, peer)]
        return [self.copy(3, 2 + k, (p.along_z(k), p.seq)) for k in range(1, p.depth)]

    def begin(self):
        self.buf[0] = self.src[...]
        for c in self.copies(0):
            c.start()

    def advance(self, stage):
        for c in self.copies(stage):
            c.wait_recv()
        if stage < 3:
            self.buf[stage + 1] = self.buf[stage] + self.got[stage]
            for c in self.copies(stage + 1):
                c.start()
        else:
            z, n = self.place.z, self.place.depth
            pick = lambda i: i
            total = self.buf[3]
            parts = [self.buf[3]] + [self.got[2 + k] for k in range(1, n)]
            total = (parts[0] + parts[1]) + (parts[2] + parts[3])
            self.out[...] = total

    def finish(self):
        for stage in range(4):
            for c in self.copies(stage):
                c.wait_send()


def halves(width):
    lane = lax.broadcasted_iota(jnp.int32, (1, width), 1)
    return lane


def key_extra(extra_ref, length, core, rows, first_pos):
    block = rows // 4
    row = lax.broadcasted_iota(jnp.int32, (rows, 128), 0)
    lane = lax.broadcasted_iota(jnp.int32, (rows, 128), 1)
    part = row // block
    owner = jnp.where(part < 2, core, 1 - core)
    position = row - part * block + (owner + 2 * lax.rem(part, 2)) * block
    dead = jnp.where(position < length, 0.0, masked_score)
    for parity in range(2):
        base = HEAD_DIM * (1 - parity)
        at = lane - base
        value = jnp.where(at == 0, dead, jnp.where((at > 0) & (at < 4), -1.0, 0.0))
        extra_ref[parity, :, :] = value.astype(jnp.bfloat16)


def split3(value):
    high = value.astype(jnp.bfloat16).astype(jnp.float32)
    rest = value - high
    mid = rest.astype(jnp.bfloat16).astype(jnp.float32)
    return high, mid, rest - mid


def nt(a, b):
    return lax.dot_general(a, b, (((1,), (1,)), ((), ())), preferred_element_type=jnp.float32)


def nn(a, b):
    return jnp.dot(a, b, preferred_element_type=jnp.float32)


def greet_sibling(peer):
    barrier = pltpu.get_barrier_semaphore()
    pl.semaphore_signal(barrier, inc=1, device_id=peer, device_id_type=MESH)
    pl.semaphore_wait(barrier, 1)


def forward_slab(j, tile, qkv_ref, other_ref, extra_ref, ctx_ref, lse_ref, between=None):
    rows, width = ctx_ref.shape
    lane = lax.broadcasted_iota(jnp.int32, (1, 128), 1)
    cols = lambda base: pl.ds(base + 128 * j if isinstance(j, int) else pl.multiple_of(base + 128 * j, 128), 128)
    keys = jnp.concatenate([qkv_ref[:, cols(width)], other_ref[:, cols(0)]], axis=0)
    values = jnp.concatenate([qkv_ref[:, cols(2 * width)], other_ref[:, cols(width)]], axis=0)
    queries = qkv_ref[:, cols(0)]
    outs, stats = [], []
    for parity in range(2):
        mine = (lane < HEAD_DIM) if parity == 0 else (lane >= HEAD_DIM)
        mark = jnp.where(lane == HEAD_DIM * (1 - parity), 1.0, 0.0).astype(jnp.bfloat16)
        k_h = jnp.where(mine, keys, extra_ref[parity])
        v_h = jnp.where(mine, values, jnp.ones_like(values))
        q_h = jnp.where(mine, queries * jnp.bfloat16(HEAD_DIM ** -0.5), mark)
        pieces, tops = [], []
        for t in range(rows // tile):
            scores = nt(q_h[t * tile:(t + 1) * tile], k_h)
            top = jnp.max(scores, axis=-1, keepdims=True)
            pieces.append(nn(jnp.exp(scores - top).astype(jnp.bfloat16), v_h))
            tops.append(top)
        out, top = jnp.concatenate(pieces, axis=0), jnp.concatenate(tops, axis=0)
        other = HEAD_DIM * (1 - parity)
        total = out[:, other:other + 1]
        outs.append(out / total)
        stats.append(top + jnp.log(total))
        if between is not None:
            between()
    ctx_ref[:, cols(0)] = jnp.where(lane < HEAD_DIM, outs[0], outs[1]).astype(jnp.bfloat16)
    lse_ref[...] = jnp.where(lane == 2 * j, stats[0], jnp.where(lane == 2 * j + 1, stats[1], lse_ref[...]))


def backward_slab(j, block, ins, work, dk_ref, dv_ref, out_ref, between=None):
    qkv_ref, other_ref, ctx_ref, grad_ref, lse_ref = ins
    extra_ref, k_ref, v_ref, q_ref, g_ref, kt_ref, dq_ref = work
    rows, width = ctx_ref.shape
    low = jnp.bfloat16
    lane = lax.broadcasted_iota(jnp.int32, (1, 128), 1)
    sub = lax.broadcasted_iota(jnp.int32, (128, 1), 0)
    cols = lambda base: pl.ds(base + 128 * j if isinstance(j, int) else pl.multiple_of(base + 128 * j, 128), 128)
    keys = jnp.concatenate([qkv_ref[:, cols(width)], other_ref[:, cols(0)]], axis=0)
    values = jnp.concatenate([qkv_ref[:, cols(2 * width)], other_ref[:, cols(width)]], axis=0)
    queries = qkv_ref[:, cols(0)] * jnp.bfloat16(HEAD_DIM ** -0.5)
    grads = grad_ref[:, cols(0)]
    along = grads.astype(jnp.float32) * ctx_ref[:, cols(0)].astype(jnp.float32)
    lse = lse_ref[...]
    for parity in range(2):
        mine = (lane < HEAD_DIM) if parity == 0 else (lane >= HEAD_DIM)
        at = lane - HEAD_DIM * (1 - parity)
        delta = jnp.sum(jnp.where(mine, along, 0.0), axis=-1, keepdims=True)
        stat = jnp.sum(jnp.where(lane == 2 * j + parity, lse, 0.0), axis=-1, keepdims=True)
        s0, s1, s2 = split3(stat)
        d0, d1, d2 = split3(delta)
        q_more = jnp.where(at == 0, 1.0, jnp.where(at == 1, s0, jnp.where(at == 2, s1, jnp.where(at == 3, s2, 0.0)))).astype(low)
        g_more = jnp.where(at == 1, d0, jnp.where(at == 2, d1, jnp.where(at == 3, d2, 0.0))).astype(low)
        k_ref[parity] = jnp.where(mine, keys, extra_ref[parity])
        v_ref[parity] = jnp.where(mine, values, extra_ref[parity])
        q_ref[parity] = jnp.where(mine, queries, q_more)
        g_ref[parity] = jnp.where(mine, grads, g_more)
        kt_ref[parity] = jnp.where((sub < HEAD_DIM) if parity == 0 else (sub >= HEAD_DIM), keys.T, jnp.zeros((128, 2 * rows), low))
    dq_ref[...] = jnp.zeros_like(dq_ref)

    def part(b, carry):
        span = pl.ds(pl.multiple_of(b * block, block), block)
        made = []
        for parity in range(2):
            q_h, g_h = q_ref[parity], g_ref[parity]
            prob = jnp.exp(nt(k_ref[parity, span, :], q_h))
            slope = nt(v_ref[parity, span, :], g_h)
            ds = (prob * slope).astype(low)
            dv = nn(prob.astype(low), g_h)
            dk = nn(ds, q_h)
            dq_ref[...] += nn(kt_ref[parity, :, span], ds)
            made.append((dk, dv))
        dk_ref[span, :] = jnp.where(lane < HEAD_DIM, made[0][0], made[1][0])
        dv_ref[span, :] = jnp.where(lane < HEAD_DIM, made[0][1], made[1][1])
        return carry

    count, cuts = 2 * rows // block, (0, 2, 4) if between is not None else (0, 4)
    for low_cut, high_cut in zip(cuts, cuts[1:]):
        if low_cut:
            between()
        lax.fori_loop(low_cut * count // 4, high_cut * count // 4, part, 0)
    out_ref[:, cols(0)] = (dq_ref[...].T * (HEAD_DIM ** -0.5)).astype(low)


def backward_work(rows):
    low = lambda *shape: pltpu.VMEM(shape, jnp.bfloat16)
    return [
        low(2, 2 * rows, 128), low(2, 2 * rows, 128), low(2, 2 * rows, 128), low(2, rows, 128), low(2, rows, 128),
        low(2, 128, 2 * rows), pltpu.VMEM((128, rows), jnp.float32),
    ]


class Give:
    def __init__(self, peer, dk_ref, dv_ref, got_ref, out_ref, rows, width, sems):
        self.peer, self.pair, self.got_ref, self.out_ref = peer, (dk_ref, dv_ref), got_ref, out_ref
        self.rows, self.width, (self.send, self.recv) = rows, width, sems

    def copy(self, j, which):
        return pltpu.make_async_remote_copy(
            src_ref=self.pair[which].at[j % 2, pl.ds(self.rows, self.rows)], dst_ref=self.got_ref.at[j, which],
            send_sem=self.send.at[j, which], recv_sem=self.recv.at[j, which], device_id=self.peer, device_id_type=MESH,
        )

    def start(self, j):
        for which in range(2):
            self.copy(j, which).start()

    def take(self, j):
        for which in range(2):
            self.copy(j, which).wait()
            total = self.pair[which][j % 2, pl.ds(0, self.rows), :] + self.got_ref[j, which]
            self.out_ref[:, pl.ds((1 + which) * self.width + j * 128, 128)] = total.astype(jnp.bfloat16)


def forward_kernel(tile, length_ref, qkv_ref, ctx_ref, lse_ref, other_ref, extra_ref, send, recv):
    seq = lax.axis_index("seq")
    core, side = lax.rem(seq, 2), lax.div(seq, 2)
    peer = (lax.axis_index("dp"), flip(seq, 1))
    rows, width = ctx_ref.shape
    greet_sibling(peer)
    swap = pltpu.make_async_remote_copy(
        src_ref=qkv_ref.at[:, pl.ds(width, 2 * width)], dst_ref=other_ref, send_sem=send, recv_sem=recv,
        device_id=peer, device_id_type=MESH,
    )
    swap.start()
    key_extra(extra_ref, jnp.where(side == 0, length_ref[0], length_ref[1]), core, 2 * rows, 0)
    swap.wait()
    lse_ref[...] = jnp.zeros_like(lse_ref)

    def slab(j, carry):
        forward_slab(j, tile, qkv_ref, other_ref, extra_ref, ctx_ref, lse_ref)
        return carry

    lax.fori_loop(0, width // 128, slab, 0)


def attend_forward(lengths, qkv):
    rows, width = qkv.shape[0], qkv.shape[1] // 3
    vmem = pl.BlockSpec(memory_space=pltpu.VMEM)
    return pl.pallas_call(
        functools.partial(forward_kernel, min(256, rows)),
        out_shape=[
            jax.ShapeDtypeStruct((rows, width), jnp.bfloat16),
            jax.ShapeDtypeStruct((rows, 128), jnp.float32),
            jax.ShapeDtypeStruct((rows, 2 * width), jnp.bfloat16),
        ],
        in_specs=[pl.BlockSpec(memory_space=pltpu.SMEM), vmem],
        out_specs=[vmem] * 3,
        scratch_shapes=[pltpu.VMEM((2, 2 * rows, 128), jnp.bfloat16), pltpu.SemaphoreType.DMA, pltpu.SemaphoreType.DMA],
        compiler_params=pltpu.CompilerParams(collective_id=1, has_side_effects=True, vmem_limit_bytes=48 << 20),
        name="attend_forward",
    )(lengths, qkv)


def backward_kernel(block, length_ref, *refs):
    ins, out_ref, work, (dk_ref, dv_ref, got_ref, send, recv) = refs[:5], refs[5], refs[6:13], refs[13:]
    seq = lax.axis_index("seq")
    core, side = lax.rem(seq, 2), lax.div(seq, 2)
    peer = (lax.axis_index("dp"), flip(seq, 1))
    rows, width = ins[2].shape
    greet_sibling(peer)
    key_extra(work[0], jnp.where(side == 0, length_ref[0], length_ref[1]), core, 2 * rows, 0)
    give = Give(peer, dk_ref, dv_ref, got_ref, out_ref, rows, width, (send, recv))
    for j in range(width // 128):
        if j >= 2:
            give.take(j - 2)
        backward_slab(j, block, ins, work, dk_ref.at[j % 2], dv_ref.at[j % 2], out_ref)
        give.start(j)
    for j in range(width // 128 - 2, width // 128):
        give.take(j)


def attend_backward(lengths, qkv, other, ctx, grad, lse):
    rows, width = ctx.shape
    slabs = width // 128
    vmem = pl.BlockSpec(memory_space=pltpu.VMEM)
    return pl.pallas_call(
        functools.partial(backward_kernel, min(256, rows)),
        out_shape=jax.ShapeDtypeStruct(qkv.shape, jnp.bfloat16),
        in_specs=[pl.BlockSpec(memory_space=pltpu.SMEM)] + [vmem] * 5,
        out_specs=vmem,
        scratch_shapes=backward_work(rows) + give_scratch(rows, slabs),
        compiler_params=pltpu.CompilerParams(collective_id=2, has_side_effects=True, vmem_limit_bytes=56 << 20),
        name="attend_backward",
    )(lengths, qkv, other, ctx, grad, lse)


def give_scratch(rows, slabs):
    full = lambda *shape: pltpu.VMEM(shape, jnp.float32)
    return [
        full(2, 2 * rows, 128), full(2, 2 * rows, 128), full(slabs, 2, rows, 128),
        pltpu.SemaphoreType.DMA((slabs, 2)), pltpu.SemaphoreType.DMA((slabs, 2)),
    ]


def encode_kernel(dp_size, plan, window, tile, length_ref, *refs):
    srcs, vec, rows_in, cot_in = refs[:6], refs[6], refs[7], refs[8]
    results = refs[9:27]
    (send, recv, local, vec_buf, vec_send, vec_recv, vec_local, swap_sem, *bufs, x_buf, qkv_ref, ctx_ref, lse_ref, other_ref,
     norm_ref, unit_ref, scale_ref, act_ref, slope_ref, grad_ref, layer_ref, sums_ref, cot_buf, flat_vec, bias_up, sum_ref, out_sem,
     extra_ref, kv_send, kv_recv) = refs[27:]
    w_buf = bufs[0]
    place = Place(dp_size)
    rows, width = ctx_ref.shape
    place.greet()
    moves = [Swap(place, a, b, swap_sem.at[i, 0], swap_sem.at[i, 1], swap_sem.at[i, 2])
             for i, (a, b) in enumerate(((rows_in, x_buf), (cot_in, cot_buf)))]
    spread = Spread(place, vec, vec_buf, (vec_send, vec_recv, vec_local))
    units = weight_units(place, srcs, bufs, plan, (send, recv, local))
    steps = gather_steps(units, window)
    kept = (*bufs, x_buf, qkv_ref, ctx_ref, lse_ref, other_ref, norm_ref, unit_ref, scale_ref, act_ref, slope_ref, grad_ref,
            layer_ref, sums_ref, flat_vec)
    puts = [pltpu.make_async_copy(a, b, out_sem.at[i]) for i, (a, b) in enumerate(zip(kept, results))]
    clock = iter(steps)

    def run(count=1):
        for _ in range(count):
            for call in next(clock, ()):
                call()

    spread.start()
    moves[0].start()
    run()
    spread.forward()
    run()
    key_extra(extra_ref, jnp.where(place.side == 0, length_ref[0], length_ref[1]), place.core, 2 * rows, 0)
    lse_ref[...] = jnp.zeros_like(lse_ref)
    run()
    spread.finish()
    lane = lax.broadcasted_iota(jnp.int32, (8, 128), 1)
    total = jnp.zeros((8, width), jnp.float32)
    share = width // dp_size
    for owner in range(dp_size):
        piece = jnp.where(lane < share, vec_buf[owner // 2, owner % 2, 0:8, :], 0.0)
        padded = jnp.concatenate([piece, jnp.zeros((8, width - 128), jnp.float32)], axis=1)
        total = total + (pltpu.roll(padded, owner * share, 1) if owner else padded)
    flat_vec[...] = total
    wide = bias_up.shape[1] // dp_size // 128
    for owner in range(dp_size):
        for i in range(wide):
            bias_up[:, pl.ds((owner * wide + i) * 128, 128)] = vec_buf[owner // 2, owner % 2, 8 + i:9 + i, :]
    run(9)
    moves[0].wait()
    puts[4].start()

    def fetch(first):
        for i in range(first, first + 2):
            units[i].arrive()

    step = 256

    def project(first, count):
        def body(t, carry):
            cols = pl.ds(pl.multiple_of(first + t * step, step), step)
            weight = w_buf[:, :, :, cols].reshape(width, step)
            qkv_ref[:, cols] = nn(x_buf[...], weight).astype(jnp.bfloat16)
            return carry

        lax.fori_loop(0, count, body, 0)

    def project_bias(first, row):
        def body(t, carry):
            cols = pl.ds(pl.multiple_of(first + t * step, step), step)
            bias = flat_vec[row:row + 1, pl.ds(pl.multiple_of(t * step, step), step)]
            weight = w_buf[:, :, :, cols].reshape(width, step)
            qkv_ref[:, cols] = (nn(x_buf[...], weight) + bias).astype(jnp.bfloat16)
            return carry

        lax.fori_loop(0, width // step, body, 0)

    fetch(0)
    project(width, width // step)
    run()
    fetch(2)
    project_bias(2 * width, 1)
    swap = pltpu.make_async_remote_copy(
        src_ref=qkv_ref.at[:, pl.ds(width, 2 * width)], dst_ref=other_ref, send_sem=kv_send, recv_sem=kv_recv,
        device_id=(place.dp, flip(place.seq, 1)), device_id_type=MESH,
    )
    swap.start()
    run()
    fetch(4)
    project_bias(0, 0)
    run()
    swap.wait()
    for j in range(width // 128):
        forward_slab(j, tile, qkv_ref, other_ref, extra_ref, ctx_ref, lse_ref, run)
        if j == 1:
            moves[1].start()
    for i in (0, 5, 6, 7, 8):
        puts[i].start()
    low = jnp.bfloat16
    vec_row = lambda i, cols=slice(None): flat_vec[i:i + 1, cols]

    def out_part(t, carry):
        cols = pl.ds(pl.multiple_of(t * step, step), step)
        weight = bufs[1][:, :, :, cols].reshape(width, step)
        sum_ref[:, cols] = x_buf[:, cols].astype(jnp.float32) + (nn(ctx_ref[...], weight) + vec_row(2, cols))
        return carry

    units[6].arrive()
    units[7].arrive()
    lax.fori_loop(0, width // step, out_part, 0)
    puts[1].start()
    run()
    chunk = 128

    def stats(value):
        centred = value - jnp.mean(value, axis=-1, keepdims=True)
        scale = lax.rsqrt(jnp.mean(centred * centred, axis=-1, keepdims=True) + eps_norm)
        return centred * scale, scale

    def first_rows(t, carry):
        at = pl.ds(pl.multiple_of(t * chunk, chunk), chunk)
        unit, scale = stats(sum_ref[at, :])
        unit_ref[at, :] = unit
        scale_ref[at, :] = jnp.broadcast_to(scale, (chunk, 128))
        norm_ref[at, :] = (unit * vec_row(4) + vec_row(5)).astype(low)
        return carry

    lax.fori_loop(0, rows // chunk, first_rows, 0)
    for i in (9, 10, 11):
        puts[i].start()
    run()
    hidden = act_ref.shape[1]

    def up_part(t, carry):
        cols = pl.ds(pl.multiple_of(t * step, step), step)
        weight = bufs[2][:, :, :, cols].reshape(width, step)
        value = nn(norm_ref[...], weight) + bias_up[:, cols]
        below = 0.5 + 0.5 * lax.erf(value * (0.5 ** 0.5))
        act_ref[:, cols] = (value * below).astype(low)
        slope_ref[:, cols] = (below + value * jnp.exp(-0.5 * value * value) * 0.3989422804014327).astype(low)
        return carry

    for j in range(hidden // width):
        for unit in units[8 + 2 * j:10 + 2 * j]:
            unit.arrive()
        for t in range(j * width // step, (j + 1) * width // step):
            lax.fori_loop(t, t + 1, up_part, 0)
            run()
    for i in (2, 12, 13):
        puts[i].start()
    run(len(steps))
    half = width // 2
    count = hidden // width
    for h in range(2):
        for unit in units[-2 * count + h * count:len(units) - count + h * count]:
            unit.arrive()
        cols = pl.ds(h * half, half)
        weight = bufs[3][:, :, :, cols].reshape(hidden, half)
        sum_ref[:, cols] = norm_ref[:, cols].astype(jnp.float32) + (nn(act_ref[...], weight) + vec_row(3, cols))
    puts[3].start()
    moves[1].wait()
    length = jnp.where(place.side == 0, length_ref[0], length_ref[1])
    block = rows // 2
    sums_ref[...] = jnp.zeros_like(sums_ref)

    def second_rows(t, carry):
        at = pl.ds(pl.multiple_of(t * chunk, chunk), chunk)
        unit, scale = stats(sum_ref[at, :])
        layer_ref[at, :] = (unit * vec_row(6) + vec_row(7)).astype(low)
        row = lax.broadcasted_iota(jnp.int32, (chunk, 1), 0) + t * chunk
        position = lax.rem(row, block) + (place.core + 2 * lax.div(row, block)) * block
        given = jnp.where(position < length, cot_buf[at, :].astype(jnp.float32), 0.0)
        e = given * vec_row(6)
        first = jnp.mean(e, axis=-1, keepdims=True)
        second = jnp.mean(e * unit, axis=-1, keepdims=True)
        grad = scale * (e - first - unit * second)
        grad_ref[at, :] = grad
        for i, value in enumerate((given * unit, given, grad.astype(low).astype(jnp.float32))):
            sums_ref[i:i + 1, :] += jnp.sum(value, axis=0, keepdims=True)
        return carry

    lax.fori_loop(0, rows // chunk, second_rows, 0)
    for i in (14, 15, 16, 17):
        puts[i].start()
    for unit in units:
        unit.finish()
    for put in puts:
        put.wait()


def encode(dp_size, lengths, weights, dst_shapes, plan, vec, rows_in, cotangent, window=3):
    groups, length, width = rows_in.shape
    rows, z, slots = groups * length, dp_size // 2, dp_size // 2
    anywhere = pl.BlockSpec(memory_space=pl.ANY)
    low = lambda *shape: jax.ShapeDtypeStruct(shape, jnp.bfloat16)
    full = lambda *shape: jax.ShapeDtypeStruct(shape, jnp.float32)
    dma = pltpu.SemaphoreType.DMA
    hidden = dst_shapes[2][1]
    kept = [low(z, 2, *shape) for shape in dst_shapes] + [
        low(rows, width), low(rows, 3 * width), low(rows, width), full(rows, 128), low(rows, 2 * width),
        low(rows, width), full(rows, width), full(rows, 128), low(rows, hidden), low(rows, hidden), full(rows, width),
        low(rows, width), full(8, width), full(8, width),
    ]
    hold = lambda a: pltpu.VMEM(a.shape, a.dtype)
    return pl.pallas_call(
        functools.partial(encode_kernel, dp_size, plan, window, min(256, rows)),
        out_shape=kept,
        in_specs=[pl.BlockSpec(memory_space=pltpu.SMEM)] + [anywhere] * 9,
        out_specs=[anywhere] * len(kept),
        scratch_shapes=gather_sems(dp_size, len(plan)) + [
            pltpu.VMEM((z, 2, *vec.shape), jnp.float32), dma((slots,)), dma((slots,)), dma, dma((2, 3)),
            *[hold(a) for a in kept[:-1]], pltpu.VMEM((rows, width), jnp.bfloat16), hold(kept[-1]),
            pltpu.VMEM((1, hidden), jnp.float32), pltpu.VMEM((rows, width), jnp.float32), dma((len(kept),)),
            pltpu.VMEM((2, 2 * rows, 128), jnp.bfloat16), dma, dma,
        ],
        compiler_params=pltpu.CompilerParams(collective_id=0, has_side_effects=True, vmem_limit_bytes=60 << 20),
        name="encode",
    )(lengths, *weights, vec, rows_in, cotangent)


class Stream:
    def __init__(self, pieces, buf, sem):
        self.copies = [pltpu.make_async_copy(piece, buf.at[i % 2], sem.at[i % 2]) for i, piece in enumerate(pieces)]
        self.buf = buf
        for copy in self.copies[:2]:
            copy.start()

    def get(self, i):
        self.copies[i].wait()
        return self.buf.at[i % 2]

    def next(self, i):
        if i + 2 < len(self.copies):
            self.copies[i + 2].start()


class Stage:
    def __init__(self, buf, sem):
        self.buf, self.sem, self.flying = buf, sem, []

    def put(self, value, dst):
        slot = len(self.flying) % 2
        if len(self.flying) >= 2:
            self.flying[-2].wait()
        self.buf[slot] = value
        self.flying.append(pltpu.make_async_copy(self.buf.at[slot], dst, self.sem.at[slot]))
        self.flying[-1].start()

    def drain(self):
        for copy in self.flying[-2:]:
            copy.wait()
        self.flying = []


def column_sum(value):
    return jnp.sum(value.astype(jnp.float32), axis=0, keepdims=True)


def decode_kernel(dp_size, plan, loads, block, length_ref, *refs):
    (qkv_in, other_in, ctx_in, lse_in, x_in, qkv_w, out_w, up_w, down_w, norm_in, unit_in, scale_in, act_in, slope_in,
     grad_in, layer_in, sums_in, vec_in) = refs[:18]
    outs, vec_outs, layer_out, input_out, parts = refs[18:24], refs[24:33], refs[33], refs[34], refs[35:38]
    scratch = refs[38:]
    got_ref, give_send, give_recv, rows_ref, layer_ref, base_ref, ctx_ref, lse_ref, cgrad_ref, sums_ref, vec_ref = scratch[:11]
    small_ref, small_out, swap_sem, load_sem, late_sem, stream_sem, grad_ref = scratch[11:18]
    small_scratch, reduce_refs = scratch[18:22], scratch[22:]
    place = Place(dp_size)
    rows, width = ctx_ref.shape
    hidden = act_in.shape[1]
    slabs, low, step = width // 128, jnp.bfloat16, 256
    half = width // 2
    early = [pltpu.make_async_copy(a, b, load_sem.at[i]) for i, (a, b) in enumerate((
        (grad_in, base_ref), (layer_in, layer_ref), (ctx_in, ctx_ref), (lse_in, lse_ref), (sums_in, sums_ref), (vec_in, vec_ref)))]
    for copy in early:
        copy.start()
    place.greet()
    moves = [SwapBack(place, a, b, swap_sem.at[i, 0], swap_sem.at[i, 1], swap_sem.at[i, 2])
             for i, (a, b) in enumerate(((layer_ref, layer_out), (rows_ref, input_out)))]
    units = reduce_units(place, (*parts, grad_ref), outs, plan, loads, reduce_refs)
    small = SumAll(place, small_ref, small_out, *small_scratch)
    steps, first = reduce_steps(units)
    clock = iter(range(first, first + len(steps)))

    def tick(count=1):
        for _ in range(count):
            for call in steps[next(clock) - first]:
                call()

    def feed_backward(act_buf, slope_buf, down_buf, up_buf, low_ref, up_low, norm_ref, norm_t, unit_ref, scale_ref, out_buf, ctx_t,
                      tall, flat):
        chunks = hidden // width
        cut = lambda ref, i: ref.at[:, pl.ds(i * width, width)]
        acts = Stream([cut(act_in, i) for i in range(chunks)], act_buf, stream_sem.at[0])
        slopes = Stream([cut(slope_in, i) for i in range(chunks)], slope_buf, stream_sem.at[1])
        downs = Stream([down_w.at[pl.ds(i * width, width)] for i in range(chunks)], down_buf, stream_sem.at[2])
        ups = Stream([cut(up_w, i) for i in range(chunks)], up_buf, stream_sem.at[3])
        others = [pltpu.make_async_copy(a, b, late_sem.at[i]) for i, (a, b) in enumerate((
            (norm_in, norm_ref), (unit_in, unit_ref), (scale_in, scale_ref), (out_w, out_buf)))]
        for copy in others:
            copy.start()
        for copy in early:
            copy.wait()
        moves[0].start()
        small_ref[...] = jnp.zeros_like(small_ref)
        small_ref[3:4, :] = sums_ref[2:3, :]
        small_ref[6:8, :] = sums_ref[0:2, :]
        low_ref[...] = base_ref[...].astype(low)
        stage = Stage(tall, stream_sem.at[4])
        each = hidden // dp_size
        for i in range(chunks):
            act = acts.get(i)
            for o in range(width // each):
                owner = i * (width // each) + o
                value = nn(act[:, o * each:(o + 1) * each].T, low_ref[...])
                stage.put(value.astype(low), parts[0].at[owner // 2, owner % 2])
            acts.next(i)
        stage.drain()
        tick(-first)
        others[0].wait()
        norm_t[...] = norm_ref[...].T
        stage = Stage(flat, stream_sem.at[4])
        shape = (place.depth, 2, width // dp_size, half)
        for i in range(chunks):
            slope, down = slopes.get(i), downs.get(i)

            def slope_part(t, carry):
                cols = pl.ds(pl.multiple_of(t * step, step), step)
                value = nt(low_ref[...], down[cols, :]) * slope[:, cols].astype(jnp.float32)
                up_low[:, cols] = value.astype(low)
                return carry

            lax.fori_loop(0, width // step, slope_part, 0)
            slopes.next(i)
            downs.next(i)
            small_ref[8 + i:9 + i, :] = column_sum(up_low[...])
            for h in range(2):
                value = nn(norm_t[...], up_low[:, h * half:(h + 1) * half]).astype(low)
                stage.put(value.reshape(shape), parts[1].at[:, :, :, pl.ds(i * width + h * half, half)])
            tick()
            up = ups.get(i)

            def back_part(t, carry):
                cols = pl.ds(pl.multiple_of(t * step, step), step)
                base_ref[:, cols] += nt(up_low[...], up[cols, :])
                return carry

            lax.fori_loop(0, width // step, back_part, 0)
            ups.next(i)
            stage.drain()
            tick()
        for copy in others[1:]:
            copy.wait()
        chunk = 128
        gain = vec_ref[4:5, :]

        def first_rows(t, carry):
            at = pl.ds(pl.multiple_of(t * chunk, chunk), chunk)
            given, unit = base_ref[at, :], unit_ref[at, :]
            e = given * gain
            mean = jnp.mean(e, axis=-1, keepdims=True)
            along = jnp.mean(e * unit, axis=-1, keepdims=True)
            grad = scale_ref[at, :][:, :1] * (e - mean - unit * along)
            base_ref[at, :] = grad
            low_ref[at, :] = grad.astype(low)
            for i, value in ((4, given * unit), (5, given), (2, grad.astype(low))):
                small_ref[i:i + 1, :] += column_sum(value)
            return carry

        lax.fori_loop(0, rows // chunk, first_rows, 0)
        ctx_t[...] = ctx_ref[...].T
        for h in range(2):
            value = nn(ctx_t[...], low_ref[:, h * half:(h + 1) * half]).astype(low)
            stage.put(value.reshape(shape), parts[2].at[:, :, :, pl.ds(h * half, half)])
        tick()

        def context_part(t, carry):
            cols = pl.ds(pl.multiple_of(t * step, step), step)
            cgrad_ref[:, cols] = nt(low_ref[...], out_buf[cols, :]).astype(low)
            return carry

        lax.fori_loop(0, width // step, context_part, 0)
        stage.drain()
        tick()

    lows = lambda *shape: pltpu.VMEM(shape, low)
    full = lambda *shape: pltpu.VMEM(shape, jnp.float32)
    pl.run_scoped(
        feed_backward, lows(2, rows, width), lows(2, rows, width), lows(2, width, width), lows(2, width, width), lows(rows, width),
        lows(rows, width), lows(rows, width), lows(width, rows), full(rows, width), full(rows, 128), lows(width, width),
        lows(width, rows), lows(2, hidden // dp_size, width), lows(2, place.depth, 2, width // dp_size, half),
    )

    def attend(qkv_ref, other_ref, x_ref, xt_ref, w_ref, d_ref, dk_ref, dv_ref, *work):
        late = [pltpu.make_async_copy(a, b, late_sem.at[i]) for i, (a, b) in enumerate((
            (qkv_in, qkv_ref), (other_in, other_ref), (x_in, x_ref), (qkv_w, w_ref)))]
        for copy in late:
            copy.start()
        ins = (qkv_ref, other_ref, ctx_ref, cgrad_ref, lse_ref)
        give = Give((place.dp, flip(place.seq, 1)), dk_ref, dv_ref, got_ref, d_ref, rows, width, (give_send, give_recv))
        key_extra(work[0], jnp.where(place.side == 0, length_ref[0], length_ref[1]), place.core, 2 * rows, 0)
        late[2].wait()
        xt_ref[...] = x_ref[...].T
        late[0].wait()
        late[1].wait()

        def weight_part(pair):
            for which in range(3):
                cols = pl.ds(which * width + pair * step, step)
                value = nn(xt_ref[...], d_ref[:, cols]).astype(low)
                grad_ref[:, :, :, pl.ds(pair * width + which * step, step)] = value.reshape(*grad_ref.shape[:3], step)

        for j in range(slabs):
            if j >= 2:
                give.take(j - 2)
                if j % 2:
                    weight_part(j // 2 - 1)
            tick()
            backward_slab(j, block, ins, work, dk_ref.at[j % 2], dv_ref.at[j % 2], d_ref, tick if j < 4 else None)
            give.start(j)
        for j in range(slabs - 2, slabs):
            give.take(j)
        weight_part(slabs // 2 - 1)
        for i, base in ((0, 0), (1, 2 * width)):
            small_ref[i:i + 1, :] = column_sum(d_ref[:, pl.ds(base, width)])
        small.begin()
        tick()
        late[3].wait()

        def input_part(t, carry):
            cols = pl.ds(pl.multiple_of(t * step, step), step)
            rows_ref[:, cols] = (base_ref[:, cols] + nt(d_ref[...], w_ref[cols, :])).astype(low)
            return carry

        lax.fori_loop(0, width // step, input_part, 0)

    pl.run_scoped(
        attend, lows(rows, 3 * width), lows(rows, 2 * width), lows(rows, width), lows(width, rows), lows(width, 3 * width),
        lows(rows, 3 * width), full(2, 2 * rows, 128), full(2, 2 * rows, 128), *backward_work(rows),
    )
    moves[1].start()
    for i, now in enumerate(clock):
        for call in steps[now - first]:
            call()
        if i % 2 and i < 8:
            small.advance(i // 2)
    small.finish()
    share = width // dp_size
    turned = pltpu.roll(small_out[0:8, :], lax.rem(width - place.dp * share, width), 1)
    for i in range(8):
        vec_outs[i][...] = turned[i:i + 1, 0:share]
    wide = small_out[pl.ds(8 + place.z, 1), :]
    vec_outs[8][...] = jnp.where(place.y == 0, wide[:, :width // 2], wide[:, width // 2:])
    for move in moves:
        move.wait()


def decode(dp_size, lengths, ins, out_shapes, part_shapes, plan, rows_shape):
    x = ins[4]
    rows, width = x.shape
    z, loads = dp_size // 2, sum(1 for p in plan if p[0] < len(part_shapes))
    slabs, dma = width // 128, pltpu.SemaphoreType.DMA
    anywhere, vmem = pl.BlockSpec(memory_space=pl.ANY), pl.BlockSpec(memory_space=pltpu.VMEM)
    low = lambda *shape: pltpu.VMEM(shape, jnp.bfloat16)
    full = lambda *shape: pltpu.VMEM(shape, jnp.float32)
    sds = lambda shape, dtype: jax.ShapeDtypeStruct(shape, dtype)
    return pl.pallas_call(
        functools.partial(decode_kernel, dp_size, plan, loads, min(256, rows)),
        out_shape=[sds(s, jnp.float32) for s in out_shapes] + [sds((1, width // dp_size), jnp.float32)] * 8
        + [sds((1, width // 2), jnp.float32)] + [sds(rows_shape, jnp.bfloat16)] * 2 + [sds(s, jnp.bfloat16) for s in part_shapes],
        in_specs=[pl.BlockSpec(memory_space=pltpu.SMEM)] + [anywhere] * len(ins),
        out_specs=[anywhere] * 6 + [vmem] * 9 + [anywhere] * (2 + len(part_shapes)),
        scratch_shapes=[
            full(slabs, 2, rows, 128), dma((slabs, 2)), dma((slabs, 2)), low(rows, width), low(rows, width), full(rows, width),
            low(rows, width), full(rows, 128), low(rows, width), full(8, width), full(8, width),
            full(16, width), full(16, width), dma((2, 3)), dma((6,)), dma((4,)), dma((5, 2)), low(z, 2, plan[0][2], 3 * width),
            full(4, 16, width), full(z + 2, 16, width), dma((z + 2,)), dma((z + 2,)),
        ] + reduce_scratch(dp_size, len(plan), loads, plan[0][2], plan[0][4]),
        compiler_params=pltpu.CompilerParams(collective_id=3, has_side_effects=True, vmem_limit_bytes=62 << 20),
        name="decode",
    )(lengths, *ins)


def settle_kernel(count, *refs):
    srcs, dsts, bufs, sem = refs[:count], refs[count:2 * count], refs[2 * count:3 * count], refs[3 * count]
    gets = [pltpu.make_async_copy(a, b, sem.at[0, i]) for i, (a, b) in enumerate(zip(srcs, bufs))]
    puts = [pltpu.make_async_copy(a.at[0] if len(a.shape) > len(b.shape) else a, b, sem.at[1, i])
            for i, (a, b) in enumerate(zip(bufs, dsts))]
    for get in gets:
        get.start()
    for get, put in zip(gets, puts):
        get.wait()
        put.start()
    for put in puts:
        put.wait()


def settle(arrays):
    count = len(arrays)
    anywhere = pl.BlockSpec(memory_space=pl.ANY)
    shape = lambda a: a.shape[1:] if a.shape[0] == 1 else a.shape
    return pl.pallas_call(
        functools.partial(settle_kernel, count),
        out_shape=[jax.ShapeDtypeStruct(shape(a), a.dtype) for a in arrays],
        in_specs=[anywhere] * count,
        out_specs=[anywhere] * count,
        scratch_shapes=[pltpu.VMEM(a.shape, a.dtype) for a in arrays] + [pltpu.SemaphoreType.DMA((2, count))],
        compiler_params=pltpu.CompilerParams(vmem_limit_bytes=61 << 20),
        name="settle",
    )(*arrays)


def matmul(a, b):
    return jnp.dot(a, b, preferred_element_type=jnp.float32)


def inner_rows(a, b):
    return lax.dot_general(a, b, (((0,), (0,)), ((), ())), preferred_element_type=jnp.float32)


def times_transposed(a, b):
    return lax.dot_general(a, b, (((1,), (1,)), ((), ())), preferred_element_type=jnp.float32)


def swap_rows(rows):
    side = lax.div(lax.axis_index("seq"), 2)
    size = lax.axis_size("seq")
    got = lax.ppermute(lax.dynamic_index_in_dim(rows, 1 - side, 0, False), "seq", [(i, i ^ 2) for i in range(size)])
    kept = lax.dynamic_index_in_dim(rows, side, 0, False)
    first = jnp.where(side == 0, kept, got)
    second = jnp.where(side == 0, got, kept)
    return jnp.concatenate([first, second], axis=0)


def swap_rows_back(rows):
    side = lax.div(lax.axis_index("seq"), 2)
    size = lax.axis_size("seq")
    blocks = rows.reshape(2, rows.shape[0] // 2, rows.shape[1])
    got = lax.ppermute(lax.dynamic_index_in_dim(blocks, 1 - side, 0, False), "seq", [(i, i ^ 2) for i in range(size)])
    kept = lax.dynamic_index_in_dim(blocks, side, 0, False)
    return jnp.stack([jnp.where(side == 0, kept, got), jnp.where(side == 0, got, kept)])


def pack_vectors(narrow, wide):
    rows = jnp.stack([v.astype(jnp.float32) for v in narrow])
    rows = jnp.pad(rows, ((0, 0), (0, 128 - rows.shape[1])))
    more = wide.astype(jnp.float32).reshape(-1, 128)
    both = jnp.concatenate([rows, more], axis=0)
    return jnp.pad(both, ((0, 16 - both.shape[0]), (0, 0)))


def norm_stats(hidden):
    row_mean = jnp.mean(hidden, axis=-1, keepdims=True)
    centred = hidden - row_mean
    row_var = jnp.mean(centred * centred, axis=-1, keepdims=True)
    scale = lax.rsqrt(row_var + eps_norm)
    return centred * scale, scale


def norm_backward(grad, gain, unit, scale):
    e = grad * gain
    first = jnp.mean(e, axis=-1, keepdims=True)
    second = jnp.mean(e * unit, axis=-1, keepdims=True)
    return scale * (e - first - unit * second)


def col_sum(value):
    return jnp.sum(value, axis=0)


def local(
    inputs, lengths, query_weight, key_weight, value_weight, output_weight, up_weight, down_weight,
    query_bias, value_bias, output_bias, up_bias, down_bias, first_gain, first_shift, second_gain, second_shift, cotangent,
):
    dp_size = lax.axis_size("dp")
    groups, length, width = inputs.shape
    shard = query_weight.shape[0]
    fast = dp_size == 8 and shard == 96 and groups == 2
    rows = groups * length
    seq = lax.axis_index("seq")
    core, side = lax.rem(seq, 2), lax.div(seq, 2)
    narrow = [query_bias, value_bias, output_bias, down_bias, first_gain, first_shift, second_gain, second_shift]
    hidden_width = up_weight.shape[1]
    if fast:
        u = shard
        half = width // 2
        cuts = [(i, 0, 0, 0, width * i) for i in (1, 2, 0)] + [(3, 1, 0, 0, 0)]
        cuts += [(4, 2, 0, width * j, width * j) for j in range(hidden_width // width)]
        plan = [(s, d, row, u, col + half * h, half, to + half * h) for s, d, row, col, to in cuts for h in range(2)]
        plan += [(5, 3, u * j, u, half * h, half, half * h) for h in range(2) for j in range(down_weight.shape[0] // u)]
        plan = [(*p, i < len(plan) - 6) for i, p in enumerate(plan)]
        weights = [query_weight, key_weight, value_weight, output_weight, up_weight, down_weight]
        shapes = [(u, 3 * width), (u, width), (u, hidden_width), (down_weight.shape[0], width)]
        (qkv_w, out_w, up_w, down_w, flat_in, qkv, context, lse, other, first_norm, unit_1, scale_1, hidden_act, slope,
         second_sum_grad, layer_rows, sums, flat_vec) = encode(
            dp_size, lengths, weights, shapes, plan, pack_vectors(narrow, up_bias), inputs, cotangent
        )
        qkv_w, out_w = qkv_w.reshape(width, 3 * width), out_w.reshape(width, width)
        up_w, down_w = up_w.reshape(width, hidden_width), down_w.reshape(hidden_width, width)
    else:
        gather = lambda a: lax.all_gather(a, "dp", axis=0, tiled=True)
        qkv_w = gather(jnp.concatenate([query_weight, key_weight, value_weight], axis=1))
        out_w, up_w, down_w = gather(output_weight), gather(up_weight), gather(down_weight)
        flat_vec = jnp.stack([gather(v.astype(jnp.float32)) for v in narrow])
        bias_up = gather(up_bias.astype(jnp.float32))
        flat_in, flat_cot = swap_rows(inputs), swap_rows(cotangent)
    bias_q, bias_v, bias_out, bias_down, gain_1, shift_1, gain_2, shift_2 = [flat_vec[i] for i in range(8)]
    if not fast:
        bias_qkv = jnp.concatenate([bias_q, jnp.zeros_like(bias_q), bias_v])
        qkv = (matmul(flat_in, qkv_w) + bias_qkv).astype(jnp.bfloat16)
        context, lse, other = attend_forward(lengths, qkv)
        first_sum = flat_in.astype(jnp.float32) + (matmul(context, out_w) + bias_out)
        unit_1, scale_1 = norm_stats(first_sum)
        first_norm = (unit_1 * gain_1 + shift_1).astype(jnp.bfloat16)
        up_pre = matmul(first_norm, up_w) + bias_up
        below = 0.5 + 0.5 * lax.erf(up_pre * (0.5 ** 0.5))
        hidden_act = (up_pre * below).astype(jnp.bfloat16)
        slope = (below + up_pre * jnp.exp(-0.5 * up_pre * up_pre) * 0.3989422804014327).astype(jnp.bfloat16)
        down_out = matmul(hidden_act, down_w) + bias_down
        second_sum = first_norm.astype(jnp.float32) + down_out
        unit_2, scale_2 = norm_stats(second_sum)
        layer_rows = (unit_2 * gain_2 + shift_2).astype(jnp.bfloat16)

        row = jnp.arange(rows)
        position = lax.rem(row, length) + (core + 2 * lax.div(row, length)) * length
        live = (position < lengths[side]).astype(jnp.float32)
        grad_out = flat_cot.astype(jnp.float32) * live[:, None]
        second_gain_grad, second_shift_grad = col_sum(grad_out * unit_2), col_sum(grad_out)
        second_sum_grad = norm_backward(grad_out, gain_2, unit_2, scale_2)
        down_bias_grad = col_sum(second_sum_grad.astype(jnp.bfloat16).astype(jnp.float32))
    low = jnp.bfloat16
    if not fast:
        down_low = second_sum_grad.astype(jnp.bfloat16)
        down_w_grad = inner_rows(hidden_act, down_low).astype(low)
        up_low = (times_transposed(down_low, down_w) * slope.astype(jnp.float32)).astype(low)
        up_w_grad = inner_rows(first_norm, up_low).astype(low)
        up_bias_grad = col_sum(up_low.astype(jnp.float32))
        norm_grad = second_sum_grad + times_transposed(up_low, up_w)
        first_gain_grad, first_shift_grad = col_sum(norm_grad * unit_1), col_sum(norm_grad)
        first_sum_grad = norm_backward(norm_grad, gain_1, unit_1, scale_1)
        attended_low = first_sum_grad.astype(low)
        out_w_grad = inner_rows(context, attended_low).astype(low)
        out_bias_grad = col_sum(attended_low.astype(jnp.float32))
        context_grad = times_transposed(attended_low, out_w).astype(low)
        qkv_low = attend_backward(lengths, qkv, other, context, context_grad, lse)
        qkv_w_grad = inner_rows(flat_in, qkv_low)
        qkv_bias_grad = col_sum(qkv_low.astype(jnp.float32))
        input_rows = (first_sum_grad + times_transposed(qkv_low, qkv_w)).astype(low)
        small = jnp.concatenate([
            jnp.stack([qkv_bias_grad[:width], qkv_bias_grad[2 * width:], out_bias_grad, down_bias_grad, first_gain_grad,
                       first_shift_grad, second_gain_grad, second_shift_grad]),
            up_bias_grad.reshape(-1, width),
        ], axis=0)
    me = lax.axis_index("dp")
    if fast:
        plan = [(0, u * j, u, half * h, half, u * j, [(0, half, 5, half * h)]) for j in range(down_weight.shape[0] // u) for h in range(2)]
        plan += [(1, 0, u, half * i, half, 0, [(0, half, 4, half * i)]) for i in range(hidden_width // half)]
        plan += [(2, 0, u, half * h, half, 0, [(0, half, 3, half * h)]) for h in range(2)]
        for p in range(width // 256):
            plan.append((3, 0, u, width * p, half, 0, [(0, 256, 0, 256 * p), (256, 128, 1, 256 * p)]))
            plan.append((3, 0, u, width * p + half, half, 0, [(0, 128, 1, 256 * p + 128), (128, 256, 2, 256 * p)]))
        plan = [(*p, 2 <= i < len(plan) - 8) for i, p in enumerate(plan)]
        shapes = [(u, width)] * 4 + [up_weight.shape, down_weight.shape]
        halves_of = lambda shape: (dp_size // 2, 2, *shape)
        part_shapes = [halves_of(down_weight.shape), halves_of(up_weight.shape), halves_of(output_weight.shape)]
        ins = (qkv, other, context, lse, flat_in, qkv_w, out_w, up_w, down_w, first_norm, unit_1, scale_1, hidden_act, slope,
               second_sum_grad, layer_rows, sums, flat_vec)
        results = decode(dp_size, lengths, ins, shapes, part_shapes, plan, (groups, length, width))
        mine, layer_out, input_grad = results[:15], results[15], results[16]
        layer_out, input_grad, *mine = settle((layer_out, input_grad, *mine))
        weight_grads, mine = mine[:6], mine[6:]
        up_mine = mine.pop()
    else:
        scatter = lambda a: lax.psum(lax.psum_scatter(a.astype(jnp.float32), "dp", scatter_dimension=0, tiled=True), "seq")
        qkv_g = scatter(qkv_w_grad)
        weight_grads = [qkv_g[:, :width], qkv_g[:, width:2 * width], qkv_g[:, 2 * width:]]
        weight_grads += [scatter(out_w_grad), scatter(up_w_grad), scatter(down_w_grad)]
        small = lax.psum(small, ("dp", "seq"))
        layer_out, input_grad = swap_rows_back(layer_rows), swap_rows_back(input_rows)
        part = query_bias.shape[0]
        mine = list(lax.dynamic_slice(small, (0, me * part), (8, part)))
        up_part = up_bias.shape[0]
        up_mine = lax.dynamic_slice(small[8:8 + hidden_width // width].reshape(hidden_width), (me * up_part,), (up_part,))
    return (layer_out, input_grad, *weight_grads, mine[0], mine[1], mine[2], up_mine, *mine[3:8])


def solution(mesh):
    rows, matrix, vector = P("dp", "seq", None), P("dp", None), P("dp")
    return jax.shard_map(
        local,
        mesh=mesh,
        in_specs=(rows, vector, *[matrix] * 6, *[vector] * 9, rows),
        out_specs=(rows, rows, *[matrix] * 6, *[vector] * 9),
        check_vma=False,
    )
```

```python
import collections
import functools
import jax
import jax.numpy as jnp
from jax import lax
from jax.experimental import pallas as pl
from jax.experimental.pallas import tpu as pltpu
from jax.sharding import PartitionSpec as P

MESH = pl.DeviceIdType.MESH
HEAD_DIM = 64
eps_norm = 1e-05
masked_score = -1000000000.0


def flip(value, bits):
    bit = 1
    while bit <= bits:
        if bits & bit:
            value = value + bit - 2 * bit * lax.rem(lax.div(value, bit), 2)
        bit *= 2
    return value


class Place:
    def __init__(self, dp_size):
        self.dp = lax.axis_index("dp")
        self.seq = lax.axis_index("seq")
        self.depth = dp_size // 2
        self.z = lax.div(self.dp, 2)
        self.y = lax.rem(self.dp, 2)
        self.core = lax.rem(self.seq, 2)
        self.side = lax.div(self.seq, 2)

    def along_z(self, k):
        return flip(self.dp, 2 * k)

    def peers(self):
        result = [(self.along_z(k), self.seq) for k in range(1, self.depth)]
        result.append((flip(self.dp, 1), self.seq))
        result.append((self.dp, flip(self.seq, 1)))
        result.append((self.dp, flip(self.seq, 2)))
        return result

    def greet(self):
        barrier = pltpu.get_barrier_semaphore()
        peers = self.peers()
        for peer in peers:
            pl.semaphore_signal(barrier, inc=1, device_id=peer, device_id_type=MESH)
        pl.semaphore_wait(barrier, len(peers))


class Gather:
    def __init__(self, place, src, dst, rows, columns, to_columns, split, sems):
        self.place, self.src, self.dst = place, src, dst
        self.columns, self.to_columns, self.split = columns, to_columns, split
        self.first, count = rows
        self.send, self.recv, self.local = sems
        self.depth = place.depth
        self.unit = unit = count // 6
        half = place.core * (3 * unit)
        self.half = (half, 3 * unit)
        self.fetch = (half + place.side * unit, 2 * unit) if split else self.half
        self.far = (half + place.side * (2 * unit), unit)

    def view(self, z, y, window):
        rows = pl.ds(pl.multiple_of(self.first + window[0], self.unit), window[1])
        return self.dst.at[z, y, rows, pl.ds(*self.to_columns)]

    def copy(self, src, dst, index, peer):
        return pltpu.make_async_remote_copy(
            src_ref=src, dst_ref=dst, send_sem=self.send.at[index], recv_sem=self.recv.at[index],
            device_id=peer, device_id_type=MESH,
        )

    def mine(self):
        rows = pl.ds(pl.multiple_of(self.first + self.fetch[0], self.unit), self.fetch[1])
        return self.src.at[rows, pl.ds(*self.columns)]

    def own(self):
        p = self.place
        return pltpu.make_async_copy(self.mine(), self.view(p.z, p.y, self.fetch), self.local)

    def over_z(self, k):
        p = self.place
        return self.copy(self.mine(), self.view(p.z, p.y, self.fetch), k, (p.along_z(k), p.seq))

    def over_y(self):
        p = self.place
        ref = self.view(slice(None), p.y, self.fetch)
        return self.copy(ref, ref, 0, (flip(p.dp, 1), p.seq))

    def over_x(self):
        p, every = self.place, slice(None)
        ref = self.view(every, every, self.far)
        return self.copy(ref, ref, self.depth, (p.dp, flip(p.seq, 2)))

    def across(self):
        p, every = self.place, slice(None)
        ref = self.view(every, every, self.half)
        return self.copy(ref, ref, self.depth + 1, (p.dp, flip(p.seq, 1)))

    def stage_z(self):
        self.own().start()
        for k in range(1, self.depth):
            self.over_z(k).start()

    def stage_y(self):
        self.own().wait()
        for k in range(1, self.depth):
            self.over_z(k).wait_recv()
        self.over_y().start()

    def stage_x(self):
        self.over_y().wait_recv()
        if self.split:
            self.over_x().start()
        else:
            self.across().start()

    def stage_core(self):
        if self.split:
            self.over_x().wait_recv()
            self.across().start()

    def arrive(self):
        self.across().wait_recv()

    def finish(self):
        for k in range(1, self.depth):
            self.over_z(k).wait_send()
        self.over_y().wait_send()
        if self.split:
            self.over_x().wait_send()
        self.across().wait_send()


def gather_sems(dp_size, units):
    n = dp_size // 2 + 2
    return [pltpu.SemaphoreType.DMA((units, n)), pltpu.SemaphoreType.DMA((units, n)), pltpu.SemaphoreType.DMA((units,))]


class Spread:
    def __init__(self, place, src, dst, sems):
        self.place, self.src, self.dst = place, src, dst
        self.send, self.recv, self.local = sems

    def own(self):
        return pltpu.make_async_copy(self.src, self.dst.at[self.place.z, self.place.y], self.local)

    def over_z(self, k):
        p = self.place
        return pltpu.make_async_remote_copy(
            src_ref=self.src, dst_ref=self.dst.at[p.z, p.y], send_sem=self.send.at[k], recv_sem=self.recv.at[k],
            device_id=(p.along_z(k), p.seq), device_id_type=MESH,
        )

    def over_y(self):
        p = self.place
        ref = self.dst.at[:, p.y]
        return pltpu.make_async_remote_copy(
            src_ref=ref, dst_ref=ref, send_sem=self.send.at[0], recv_sem=self.recv.at[0],
            device_id=(flip(p.dp, 1), p.seq), device_id_type=MESH,
        )

    def start(self):
        self.own().start()
        for k in range(1, self.place.depth):
            self.over_z(k).start()

    def forward(self):
        self.own().wait()
        for k in range(1, self.place.depth):
            self.over_z(k).wait_recv()
        self.over_y().start()

    def finish(self):
        for k in range(1, self.place.depth):
            self.over_z(k).wait_send()
        self.over_y().wait()


def gather_steps(units, window):
    count = len(units)
    steps = [[unit.stage_z for unit in units[:window]]]
    for i in range(count + 4):
        step = []
        if i < count:
            step.append(units[i].stage_y)
            if i + window < count:
                step.append(units[i + window].stage_z)
        if 0 <= i - 2 < count:
            step.append(units[i - 2].stage_x)
        if 0 <= i - 4 < count:
            step.append(units[i - 4].stage_core)
        steps.append(step)
    return steps


def weight_units(place, srcs, dsts, plan, sems):
    send, recv, local = sems
    return [
        Gather(place, srcs[s], dsts[d], (first, rows), (column, width), (to, width), split, (send.at[i], recv.at[i], local.at[i]))
        for i, (s, d, first, rows, column, width, to, split) in enumerate(plan)
    ]


class Swap:
    def __init__(self, place, src, dst, send, recv, local):
        side = place.side
        length = src.shape[1]
        own = dst.at[pl.ds(pl.multiple_of(side * length, 8), length)]
        self.here = pltpu.make_async_copy(src.at[side], own, local)
        self.there = pltpu.make_async_remote_copy(
            src_ref=src.at[1 - side], dst_ref=own, send_sem=send, recv_sem=recv,
            device_id=(place.dp, flip(place.seq, 2)), device_id_type=MESH,
        )

    def start(self):
        self.here.start()
        self.there.start()

    def wait(self):
        self.here.wait()
        self.there.wait()


class SwapBack:
    def __init__(self, place, src, dst, send, recv, local):
        side, length = place.side, dst.shape[1]
        block = lambda i: src.at[pl.ds(pl.multiple_of(i * length, length), length)]
        self.here = pltpu.make_async_copy(block(side), dst.at[side], local)
        self.there = pltpu.make_async_remote_copy(
            src_ref=block(1 - side), dst_ref=dst.at[side], send_sem=send, recv_sem=recv,
            device_id=(place.dp, flip(place.seq, 2)), device_id_type=MESH,
        )

    def start(self):
        self.here.start()
        self.there.start()

    def wait(self):
        self.here.wait()
        self.there.wait()


class Reduce:
    def __init__(self, place, src, rows, columns, targets, to_row, split, own, bufs, sems):
        self.place, self.src, self.targets, self.split = place, src, targets, split
        self.columns, self.to_row = columns, to_row
        self.first, count = rows
        self.unit = unit = count // 6
        self.from_core, self.from_x, self.from_y, self.from_z, self.got, self.total = bufs
        self.send, self.recv = sems
        self.depth = place.depth
        self.half = place.core * (3 * unit)
        self.sibling_half = (1 - place.core) * (3 * unit)
        self.keep = (place.side * unit, 2 * unit) if split else (0, 3 * unit)
        self.loads = own is not None
        self.own = own if self.loads else self.view(self.half)

    def view(self, start):
        rows = pl.ds(pl.multiple_of(self.first + start, self.unit), 3 * self.unit)
        return self.src.at[:, :, rows, pl.ds(*self.columns)]

    def rows(self, window):
        return pl.ds(pl.multiple_of(window[0], self.unit), window[1])

    def copy(self, src, dst, index, peer):
        return pltpu.make_async_remote_copy(
            src_ref=src, dst_ref=dst, send_sem=self.send.at[index], recv_sem=self.recv.at[index],
            device_id=peer, device_id_type=MESH,
        )

    def load(self):
        return pltpu.make_async_copy(self.view(self.half), self.own, self.send.at[0])

    def core(self):
        p = self.place
        return self.copy(self.view(self.sibling_half), self.from_core, self.depth, (p.dp, flip(p.seq, 1)))

    def far(self):
        return ((1 - self.place.side) * (2 * self.unit), self.unit)

    def x(self):
        p = self.place
        return self.copy(self.own.at[:, :, self.rows(self.far())], self.from_x, self.depth + 1, (p.dp, flip(p.seq, 2)))

    def y(self):
        p = self.place
        src = self.own.at[:, 1 - p.y, self.rows(self.keep)]
        return self.copy(src, self.from_y.at[:, pl.ds(0, self.keep[1])], self.depth + 2, (flip(p.dp, 1), p.seq))

    def z(self, k):
        p = self.place
        src = self.own.at[flip(p.z, k), p.y, self.rows(self.keep)]
        return self.copy(src, self.from_z.at[k - 1, pl.ds(0, self.keep[1])], k, (p.along_z(k), p.seq))

    def x_last(self):
        p = self.place
        src = self.own.at[p.z, p.y, self.rows(self.keep)]
        return self.copy(src, self.got.at[pl.ds(0, self.keep[1])], self.depth + 3, (p.dp, flip(p.seq, 2)))

    def puts(self):
        p, n = self.place, self.depth
        rows = pl.ds(pl.multiple_of(self.to_row + self.half, self.unit), 3 * self.unit)
        here, there = [], []
        for i, (column, width, out, to) in enumerate(self.targets):
            src, dst = self.total.at[:, pl.ds(column, width)], out.at[rows, pl.ds(to, width)]
            here.append(pltpu.make_async_copy(src, dst, self.send.at[n + 6 + i]))
            there.append(self.copy(src, dst, n + 4 + i, (p.dp, flip(p.seq, 1))))
        return here + there

    def chip(self, z, y, window):
        rows = self.rows(window)
        return self.own[z, y, rows, :].astype(jnp.float32) + self.from_core[z, y, rows, :].astype(jnp.float32)

    def pieces(self, z, y):
        u, side = self.unit, self.place.side
        if not self.split:
            return [((i * u, u), (i * u, u), self.chip(z, y, (i * u, u))) for i in range(3)]
        solo = (side * (2 * u), u)
        gained = self.chip(z, y, solo) + self.from_x[z, y, :, :].astype(jnp.float32)
        return [((u, u), ((1 - side) * u, u), self.chip(z, y, (u, u))), (solo, (side * u, u), gained)]

    def stage_core(self):
        if self.loads:
            self.load().start()
        self.core().start()

    def stage_x(self):
        if self.loads:
            self.load().wait()
        self.core().wait_recv()
        if not self.split:
            return
        rows = self.rows(self.far())

        def body(z, carry):
            for y in range(2):
                self.own[z, y, rows, :] = self.chip(z, y, self.far()).astype(jnp.bfloat16)
            return carry

        lax.fori_loop(0, self.depth, body, 0)
        self.x().start()

    def stage_y(self):
        if self.split:
            self.x().wait_recv()
        y = 1 - self.place.y

        def body(z, carry):
            for at, _, value in self.pieces(z, y):
                self.own[z, y, self.rows(at), :] = value.astype(jnp.bfloat16)
            return carry

        lax.fori_loop(0, self.depth, body, 0)
        self.y().start()

    def column(self, z):
        return [
            (at, kept, value + self.from_y[z, self.rows(kept), :].astype(jnp.float32))
            for at, kept, value in self.pieces(z, self.place.y)
        ]

    def stage_z(self):
        self.y().wait_recv()
        for k in range(1, self.depth):
            z = flip(self.place.z, k)
            for at, _, value in self.column(z):
                self.own[z, self.place.y, self.rows(at), :] = value.astype(jnp.bfloat16)
            self.z(k).start()

    def stage_last(self):
        for k in range(1, self.depth):
            self.z(k).wait_recv()
        p = self.place
        for at, kept, value in self.column(p.z):
            for k in range(1, self.depth):
                value = value + self.from_z[k - 1, self.rows(kept), :].astype(jnp.float32)
            self.own[p.z, p.y, self.rows(at), :] = value.astype(jnp.bfloat16)
        self.x_last().start()

    def stage_out(self):
        self.x_last().wait_recv()
        p, u = self.place, self.unit
        mine = lambda at: self.own[p.z, p.y, self.rows(at), :].astype(jnp.float32)
        got = lambda at: self.got[self.rows(at), :].astype(jnp.float32)
        if self.split:
            side = p.side
            self.total[self.rows((u, u)), :] = mine((u, u)) + got((side * u, u))
            self.total[self.rows((side * (2 * u), u)), :] = mine((side * (2 * u), u))
            self.total[self.rows((2 * u - side * (2 * u), u)), :] = got(((1 - side) * u, u))
        else:
            whole = (0, 3 * u)
            self.total[...] = mine(whole) + got(whole)
        for put in self.puts():
            put.start()

    def finish(self):
        self.core().wait_send()
        if self.split:
            self.x().wait_send()
        self.y().wait_send()
        for k in range(1, self.depth):
            self.z(k).wait_send()
        self.x_last().wait_send()
        for put in self.puts():
            put.wait()


def reduce_scratch(dp_size, units, loads, rows, width):
    z, u = dp_size // 2, rows // 6
    low = lambda count, *shape: pltpu.VMEM((count, *shape, width), jnp.bfloat16)
    return [
        low(loads, z, 2, 3 * u), low(units, z, 2, 3 * u), low(units, z, 2, u), low(units, z, 3 * u), low(units, z - 1, 3 * u),
        low(units, 3 * u), pltpu.VMEM((units, 3 * u, width), jnp.float32),
        pltpu.SemaphoreType.DMA((units, z + 8)), pltpu.SemaphoreType.DMA((units, z + 8)),
    ]


def reduce_units(place, srcs, outs, plan, loads, scratch):
    own, bufs, send, recv = scratch[0], scratch[1:-2], scratch[-2], scratch[-1]
    return [
        Reduce(place, srcs[s], (first, rows), (column, width), [(a, w, outs[o], to) for a, w, o, to in targets], to_row, split,
               own.at[i] if i < loads else None, [b.at[i] for b in bufs], (send.at[i], recv.at[i]))
        for i, (s, first, rows, column, width, to_row, targets, split) in enumerate(plan)
    ]


STAGES = ("stage_core", "stage_x", "stage_y", "stage_z", "stage_last", "stage_out", "finish")


def reduce_steps(units):
    first, steps = -3, collections.defaultdict(list)
    for i, unit in enumerate(units):
        lag = 2 if unit.split else 0
        ages = (-3 if unit.loads else -1, 0, lag, lag + 2, lag + 4, lag + 6, lag + 8)
        for stage, age in zip(STAGES, ages):
            steps[i + age].append((-age, getattr(unit, stage)))
    ticks = range(first, max(steps) + 1)
    return [[call for _, call in sorted(steps[tick], key=lambda pair: pair[0])] for tick in ticks], first


class SumAll:
    def __init__(self, place, src, out, buf, got, send, recv):
        self.place, self.src, self.out, self.buf, self.got, self.send, self.recv = place, src, out, buf, got, send, recv

    def copy(self, stage, slot, peer):
        return pltpu.make_async_remote_copy(
            src_ref=self.buf.at[stage], dst_ref=self.got.at[slot], send_sem=self.send.at[slot], recv_sem=self.recv.at[slot],
            device_id=peer, device_id_type=MESH,
        )

    def copies(self, stage):
        p = self.place
        if stage < 3:
            peer = [(p.dp, flip(p.seq, 1)), (p.dp, flip(p.seq, 2)), (flip(p.dp, 1), p.seq)][stage]
            return [self.copy(stage, stage, peer)]
        return [self.copy(3, 2 + k, (p.along_z(k), p.seq)) for k in range(1, p.depth)]

    def begin(self):
        self.buf[0] = self.src[...]
        for c in self.copies(0):
            c.start()

    def advance(self, stage):
        for c in self.copies(stage):
            c.wait_recv()
        if stage < 3:
            self.buf[stage + 1] = self.buf[stage] + self.got[stage]
            for c in self.copies(stage + 1):
                c.start()
        else:
            z, n = self.place.z, self.place.depth
            pick = lambda i: i
            total = self.buf[3]
            parts = [self.buf[3]] + [self.got[2 + k] for k in range(1, n)]
            total = (parts[0] + parts[1]) + (parts[2] + parts[3])
            self.out[...] = total

    def finish(self):
        for stage in range(4):
            for c in self.copies(stage):
                c.wait_send()


def halves(width):
    lane = lax.broadcasted_iota(jnp.int32, (1, width), 1)
    return lane


def key_extra(extra_ref, length, core, rows, first_pos):
    block = rows // 4
    row = lax.broadcasted_iota(jnp.int32, (rows, 128), 0)
    lane = lax.broadcasted_iota(jnp.int32, (rows, 128), 1)
    part = row // block
    owner = jnp.where(part < 2, core, 1 - core)
    position = row - part * block + (owner + 2 * lax.rem(part, 2)) * block
    dead = jnp.where(position < length, 0.0, masked_score)
    for parity in range(2):
        base = HEAD_DIM * (1 - parity)
        at = lane - base
        value = jnp.where(at == 0, dead, jnp.where((at > 0) & (at < 4), -1.0, 0.0))
        extra_ref[parity, :, :] = value.astype(jnp.bfloat16)


def split3(value):
    high = value.astype(jnp.bfloat16).astype(jnp.float32)
    rest = value - high
    mid = rest.astype(jnp.bfloat16).astype(jnp.float32)
    return high, mid, rest - mid


def nt(a, b):
    return lax.dot_general(a, b, (((1,), (1,)), ((), ())), preferred_element_type=jnp.float32)


def nn(a, b):
    return jnp.dot(a, b, preferred_element_type=jnp.float32)


def greet_sibling(peer):
    barrier = pltpu.get_barrier_semaphore()
    pl.semaphore_signal(barrier, inc=1, device_id=peer, device_id_type=MESH)
    pl.semaphore_wait(barrier, 1)


def forward_slab(j, tile, qkv_ref, other_ref, extra_ref, ctx_ref, lse_ref, between=None):
    rows, width = ctx_ref.shape
    lane = lax.broadcasted_iota(jnp.int32, (1, 128), 1)
    cols = lambda base: pl.ds(base + 128 * j if isinstance(j, int) else pl.multiple_of(base + 128 * j, 128), 128)
    keys = jnp.concatenate([qkv_ref[:, cols(width)], other_ref[:, cols(0)]], axis=0)
    values = jnp.concatenate([qkv_ref[:, cols(2 * width)], other_ref[:, cols(width)]], axis=0)
    queries = qkv_ref[:, cols(0)]
    outs, stats = [], []
    for parity in range(2):
        mine = (lane < HEAD_DIM) if parity == 0 else (lane >= HEAD_DIM)
        mark = jnp.where(lane == HEAD_DIM * (1 - parity), 1.0, 0.0).astype(jnp.bfloat16)
        k_h = jnp.where(mine, keys, extra_ref[parity])
        v_h = jnp.where(mine, values, jnp.ones_like(values))
        q_h = jnp.where(mine, queries * jnp.bfloat16(HEAD_DIM ** -0.5), mark)
        pieces, tops = [], []
        for t in range(rows // tile):
            scores = nt(q_h[t * tile:(t + 1) * tile], k_h)
            top = jnp.max(scores, axis=-1, keepdims=True)
            pieces.append(nn(jnp.exp(scores - top).astype(jnp.bfloat16), v_h))
            tops.append(top)
        out, top = jnp.concatenate(pieces, axis=0), jnp.concatenate(tops, axis=0)
        other = HEAD_DIM * (1 - parity)
        total = out[:, other:other + 1]
        outs.append(out / total)
        stats.append(top + jnp.log(total))
        if between is not None:
            between()
    ctx_ref[:, cols(0)] = jnp.where(lane < HEAD_DIM, outs[0], outs[1]).astype(jnp.bfloat16)
    lse_ref[...] = jnp.where(lane == 2 * j, stats[0], jnp.where(lane == 2 * j + 1, stats[1], lse_ref[...]))


def backward_slab(j, block, ins, work, dk_ref, dv_ref, out_ref, between=None):
    qkv_ref, other_ref, ctx_ref, grad_ref, lse_ref = ins
    extra_ref, k_ref, v_ref, q_ref, g_ref, kt_ref, dq_ref = work
    rows, width = ctx_ref.shape
    low = jnp.bfloat16
    lane = lax.broadcasted_iota(jnp.int32, (1, 128), 1)
    sub = lax.broadcasted_iota(jnp.int32, (128, 1), 0)
    cols = lambda base: pl.ds(base + 128 * j if isinstance(j, int) else pl.multiple_of(base + 128 * j, 128), 128)
    keys = jnp.concatenate([qkv_ref[:, cols(width)], other_ref[:, cols(0)]], axis=0)
    values = jnp.concatenate([qkv_ref[:, cols(2 * width)], other_ref[:, cols(width)]], axis=0)
    queries = qkv_ref[:, cols(0)] * jnp.bfloat16(HEAD_DIM ** -0.5)
    grads = grad_ref[:, cols(0)]
    along = grads.astype(jnp.float32) * ctx_ref[:, cols(0)].astype(jnp.float32)
    lse = lse_ref[...]
    for parity in range(2):
        mine = (lane < HEAD_DIM) if parity == 0 else (lane >= HEAD_DIM)
        at = lane - HEAD_DIM * (1 - parity)
        delta = jnp.sum(jnp.where(mine, along, 0.0), axis=-1, keepdims=True)
        stat = jnp.sum(jnp.where(lane == 2 * j + parity, lse, 0.0), axis=-1, keepdims=True)
        s0, s1, s2 = split3(stat)
        d0, d1, d2 = split3(delta)
        q_more = jnp.where(at == 0, 1.0, jnp.where(at == 1, s0, jnp.where(at == 2, s1, jnp.where(at == 3, s2, 0.0)))).astype(low)
        g_more = jnp.where(at == 1, d0, jnp.where(at == 2, d1, jnp.where(at == 3, d2, 0.0))).astype(low)
        k_ref[parity] = jnp.where(mine, keys, extra_ref[parity])
        v_ref[parity] = jnp.where(mine, values, extra_ref[parity])
        q_ref[parity] = jnp.where(mine, queries, q_more)
        g_ref[parity] = jnp.where(mine, grads, g_more)
        kt_ref[parity] = jnp.where((sub < HEAD_DIM) if parity == 0 else (sub >= HEAD_DIM), keys.T, jnp.zeros((128, 2 * rows), low))
    dq_ref[...] = jnp.zeros_like(dq_ref)

    def part(b, carry):
        span = pl.ds(pl.multiple_of(b * block, block), block)
        made = []
        for parity in range(2):
            q_h, g_h = q_ref[parity], g_ref[parity]
            prob = jnp.exp(nt(k_ref[parity, span, :], q_h))
            slope = nt(v_ref[parity, span, :], g_h)
            ds = (prob * slope).astype(low)
            dv = nn(prob.astype(low), g_h)
            dk = nn(ds, q_h)
            dq_ref[...] += nn(kt_ref[parity, :, span], ds)
            made.append((dk, dv))
        dk_ref[span, :] = jnp.where(lane < HEAD_DIM, made[0][0], made[1][0])
        dv_ref[span, :] = jnp.where(lane < HEAD_DIM, made[0][1], made[1][1])
        return carry

    count, cuts = 2 * rows // block, (0, 2, 4) if between is not None else (0, 4)
    for low_cut, high_cut in zip(cuts, cuts[1:]):
        if low_cut:
            between()
        lax.fori_loop(low_cut * count // 4, high_cut * count // 4, part, 0)
    out_ref[:, cols(0)] = (dq_ref[...].T * (HEAD_DIM ** -0.5)).astype(low)


def backward_work(rows):
    low = lambda *shape: pltpu.VMEM(shape, jnp.bfloat16)
    return [
        low(2, 2 * rows, 128), low(2, 2 * rows, 128), low(2, 2 * rows, 128), low(2, rows, 128), low(2, rows, 128),
        low(2, 128, 2 * rows), pltpu.VMEM((128, rows), jnp.float32),
    ]


class Give:
    def __init__(self, peer, dk_ref, dv_ref, got_ref, out_ref, rows, width, sems):
        self.peer, self.pair, self.got_ref, self.out_ref = peer, (dk_ref, dv_ref), got_ref, out_ref
        self.rows, self.width, (self.send, self.recv) = rows, width, sems

    def copy(self, j, which):
        return pltpu.make_async_remote_copy(
            src_ref=self.pair[which].at[lax.rem(j, 2), pl.ds(self.rows, self.rows)], dst_ref=self.got_ref.at[j, which],
            send_sem=self.send.at[j, which], recv_sem=self.recv.at[j, which], device_id=self.peer, device_id_type=MESH,
        )

    def start(self, j):
        for which in range(2):
            self.copy(j, which).start()

    def take(self, j):
        for which in range(2):
            self.copy(j, which).wait()
            total = self.pair[which][lax.rem(j, 2), pl.ds(0, self.rows), :] + self.got_ref[j, which]
            start = (1 + which) * self.width + j * 128
            self.out_ref[:, pl.ds(start if isinstance(j, int) else pl.multiple_of(start, 128), 128)] = total.astype(jnp.bfloat16)


def forward_kernel(tile, length_ref, qkv_ref, ctx_ref, lse_ref, other_ref, extra_ref, send, recv):
    seq = lax.axis_index("seq")
    core, side = lax.rem(seq, 2), lax.div(seq, 2)
    peer = (lax.axis_index("dp"), flip(seq, 1))
    rows, width = ctx_ref.shape
    greet_sibling(peer)
    swap = pltpu.make_async_remote_copy(
        src_ref=qkv_ref.at[:, pl.ds(width, 2 * width)], dst_ref=other_ref, send_sem=send, recv_sem=recv,
        device_id=peer, device_id_type=MESH,
    )
    swap.start()
    key_extra(extra_ref, jnp.where(side == 0, length_ref[0], length_ref[1]), core, 2 * rows, 0)
    swap.wait()
    lse_ref[...] = jnp.zeros_like(lse_ref)

    def slab(j, carry):
        forward_slab(j, tile, qkv_ref, other_ref, extra_ref, ctx_ref, lse_ref)
        return carry

    lax.fori_loop(0, width // 128, slab, 0)


def attend_forward(lengths, qkv):
    rows, width = qkv.shape[0], qkv.shape[1] // 3
    vmem = pl.BlockSpec(memory_space=pltpu.VMEM)
    return pl.pallas_call(
        functools.partial(forward_kernel, min(256, rows)),
        out_shape=[
            jax.ShapeDtypeStruct((rows, width), jnp.bfloat16),
            jax.ShapeDtypeStruct((rows, 128), jnp.float32),
            jax.ShapeDtypeStruct((rows, 2 * width), jnp.bfloat16),
        ],
        in_specs=[pl.BlockSpec(memory_space=pltpu.SMEM), vmem],
        out_specs=[vmem] * 3,
        scratch_shapes=[pltpu.VMEM((2, 2 * rows, 128), jnp.bfloat16), pltpu.SemaphoreType.DMA, pltpu.SemaphoreType.DMA],
        compiler_params=pltpu.CompilerParams(collective_id=1, has_side_effects=True, vmem_limit_bytes=48 << 20),
        name="attend_forward",
    )(lengths, qkv)


def backward_kernel(block, length_ref, *refs):
    ins, out_ref, work, (dk_ref, dv_ref, got_ref, send, recv) = refs[:5], refs[5], refs[6:13], refs[13:]
    seq = lax.axis_index("seq")
    core, side = lax.rem(seq, 2), lax.div(seq, 2)
    peer = (lax.axis_index("dp"), flip(seq, 1))
    rows, width = ins[2].shape
    greet_sibling(peer)
    key_extra(work[0], jnp.where(side == 0, length_ref[0], length_ref[1]), core, 2 * rows, 0)
    give = Give(peer, dk_ref, dv_ref, got_ref, out_ref, rows, width, (send, recv))
    for j in range(width // 128):
        if j >= 2:
            give.take(j - 2)
        backward_slab(j, block, ins, work, dk_ref.at[j % 2], dv_ref.at[j % 2], out_ref)
        give.start(j)
    for j in range(width // 128 - 2, width // 128):
        give.take(j)


def attend_backward(lengths, qkv, other, ctx, grad, lse):
    rows, width = ctx.shape
    slabs = width // 128
    vmem = pl.BlockSpec(memory_space=pltpu.VMEM)
    return pl.pallas_call(
        functools.partial(backward_kernel, min(256, rows)),
        out_shape=jax.ShapeDtypeStruct(qkv.shape, jnp.bfloat16),
        in_specs=[pl.BlockSpec(memory_space=pltpu.SMEM)] + [vmem] * 5,
        out_specs=vmem,
        scratch_shapes=backward_work(rows) + give_scratch(rows, slabs),
        compiler_params=pltpu.CompilerParams(collective_id=2, has_side_effects=True, vmem_limit_bytes=56 << 20),
        name="attend_backward",
    )(lengths, qkv, other, ctx, grad, lse)


def give_scratch(rows, slabs):
    full = lambda *shape: pltpu.VMEM(shape, jnp.float32)
    return [
        full(2, 2 * rows, 128), full(2, 2 * rows, 128), full(slabs, 2, rows, 128),
        pltpu.SemaphoreType.DMA((slabs, 2)), pltpu.SemaphoreType.DMA((slabs, 2)),
    ]


def encode_kernel(dp_size, plan, window, tile, length_ref, *refs):
    srcs, vec, rows_in, cot_in = refs[:6], refs[6], refs[7], refs[8]
    results = refs[9:27]
    (send, recv, local, vec_buf, vec_send, vec_recv, vec_local, swap_sem, *bufs, x_buf, qkv_ref, ctx_ref, lse_ref, other_ref,
     norm_ref, unit_ref, scale_ref, act_ref, slope_ref, grad_ref, layer_ref, sums_ref, cot_buf, flat_vec, bias_up, sum_ref, out_sem,
     extra_ref, kv_send, kv_recv) = refs[27:]
    w_buf = bufs[0]
    place = Place(dp_size)
    rows, width = ctx_ref.shape
    place.greet()
    moves = [Swap(place, a, b, swap_sem.at[i, 0], swap_sem.at[i, 1], swap_sem.at[i, 2])
             for i, (a, b) in enumerate(((rows_in, x_buf), (cot_in, cot_buf)))]
    spread = Spread(place, vec, vec_buf, (vec_send, vec_recv, vec_local))
    units = weight_units(place, srcs, bufs, plan, (send, recv, local))
    steps = gather_steps(units, window)
    kept = (*bufs, x_buf, qkv_ref, ctx_ref, lse_ref, other_ref, norm_ref, unit_ref, scale_ref, act_ref, slope_ref, grad_ref,
            layer_ref, sums_ref, flat_vec)
    puts = [pltpu.make_async_copy(a, b, out_sem.at[i]) for i, (a, b) in enumerate(zip(kept, results))]
    clock = iter(steps)

    def run(count=1):
        for _ in range(count):
            for call in next(clock, ()):
                call()

    spread.start()
    moves[0].start()
    run()
    spread.forward()
    run()
    key_extra(extra_ref, jnp.where(place.side == 0, length_ref[0], length_ref[1]), place.core, 2 * rows, 0)
    lse_ref[...] = jnp.zeros_like(lse_ref)
    run()
    spread.finish()
    lane = lax.broadcasted_iota(jnp.int32, (8, 128), 1)
    total = jnp.zeros((8, width), jnp.float32)
    share = width // dp_size
    for owner in range(dp_size):
        piece = jnp.where(lane < share, vec_buf[owner // 2, owner % 2, 0:8, :], 0.0)
        padded = jnp.concatenate([piece, jnp.zeros((8, width - 128), jnp.float32)], axis=1)
        total = total + (pltpu.roll(padded, owner * share, 1) if owner else padded)
    flat_vec[...] = total
    wide = bias_up.shape[1] // dp_size // 128
    for owner in range(dp_size):
        for i in range(wide):
            bias_up[:, pl.ds((owner * wide + i) * 128, 128)] = vec_buf[owner // 2, owner % 2, 8 + i:9 + i, :]
    run(9)
    moves[0].wait()
    puts[4].start()

    def fetch(first):
        for i in range(first, first + 2):
            units[i].arrive()

    step = 256

    def project(first, count):
        def body(t, carry):
            cols = pl.ds(pl.multiple_of(first + t * step, step), step)
            weight = w_buf[:, :, :, cols].reshape(width, step)
            qkv_ref[:, cols] = nn(x_buf[...], weight).astype(jnp.bfloat16)
            return carry

        lax.fori_loop(0, count, body, 0)

    def project_bias(first, row):
        def body(t, carry):
            cols = pl.ds(pl.multiple_of(first + t * step, step), step)
            bias = flat_vec[row:row + 1, pl.ds(pl.multiple_of(t * step, step), step)]
            weight = w_buf[:, :, :, cols].reshape(width, step)
            qkv_ref[:, cols] = (nn(x_buf[...], weight) + bias).astype(jnp.bfloat16)
            return carry

        lax.fori_loop(0, width // step, body, 0)

    fetch(0)
    project(width, width // step)
    run()
    fetch(2)
    project_bias(2 * width, 1)
    swap = pltpu.make_async_remote_copy(
        src_ref=qkv_ref.at[:, pl.ds(width, 2 * width)], dst_ref=other_ref, send_sem=kv_send, recv_sem=kv_recv,
        device_id=(place.dp, flip(place.seq, 1)), device_id_type=MESH,
    )
    swap.start()
    run()
    fetch(4)
    project_bias(0, 0)
    run()
    swap.wait()
    counts = []
    taken = [step for step in clock]
    clock = iter(taken)

    def forward_two(j, carry):
        def between():
            counts.append(len(counts))
            for k in range(width // 128):
                index = 2 * k + len(counts) - 1
                if index < len(taken):
                    @pl.when(j == k)
                    def _():
                        for call in taken[index]:
                            call()

        forward_slab(j, tile, qkv_ref, other_ref, extra_ref, ctx_ref, lse_ref, between)

        @pl.when(j == 1)
        def _():
            moves[1].start()

        return carry

    lax.fori_loop(0, width // 128, forward_two, 0)
    for _ in range(2 * (width // 128)):
        next(clock, ())
    for i in (0, 5, 6, 7, 8):
        puts[i].start()
    low = jnp.bfloat16
    vec_row = lambda i, cols=slice(None): flat_vec[i:i + 1, cols]

    def out_part(t, carry):
        cols = pl.ds(pl.multiple_of(t * step, step), step)
        weight = bufs[1][:, :, :, cols].reshape(width, step)
        sum_ref[:, cols] = x_buf[:, cols].astype(jnp.float32) + (nn(ctx_ref[...], weight) + vec_row(2, cols))
        return carry

    units[6].arrive()
    units[7].arrive()
    lax.fori_loop(0, width // step, out_part, 0)
    puts[1].start()
    run()
    chunk = 128

    def stats(value):
        centred = value - jnp.mean(value, axis=-1, keepdims=True)
        scale = lax.rsqrt(jnp.mean(centred * centred, axis=-1, keepdims=True) + eps_norm)
        return centred * scale, scale

    def first_rows(t, carry):
        at = pl.ds(pl.multiple_of(t * chunk, chunk), chunk)
        unit, scale = stats(sum_ref[at, :])
        unit_ref[at, :] = unit
        scale_ref[at, :] = jnp.broadcast_to(scale, (chunk, 128))
        norm_ref[at, :] = (unit * vec_row(4) + vec_row(5)).astype(low)
        return carry

    lax.fori_loop(0, rows // chunk, first_rows, 0)
    for i in (9, 10, 11):
        puts[i].start()
    run()
    hidden = act_ref.shape[1]

    def up_part(t, carry):
        cols = pl.ds(pl.multiple_of(t * step, step), step)
        weight = bufs[2][:, :, :, cols].reshape(width, step)
        value = nn(norm_ref[...], weight) + bias_up[:, cols]
        below = 0.5 + 0.5 * lax.erf(value * (0.5 ** 0.5))
        act_ref[:, cols] = (value * below).astype(low)
        slope_ref[:, cols] = (below + value * jnp.exp(-0.5 * value * value) * 0.3989422804014327).astype(low)
        return carry

    for j in range(hidden // width):
        for unit in units[8 + 2 * j:10 + 2 * j]:
            unit.arrive()
        ahead = [next(clock, ()) for _ in range(width // step)]
        base = j * width // step

        def up_step(t, carry):
            up_part(t, carry)
            for k, calls in enumerate(ahead):
                if calls:
                    @pl.when(t == base + k)
                    def _():
                        for call in calls:
                            call()
            return carry

        lax.fori_loop(base, base + width // step, up_step, 0)
    for i in (2, 12, 13):
        puts[i].start()
    run(len(steps))
    half = width // 2
    count = hidden // width
    for h in range(2):
        for unit in units[-2 * count + h * count:len(units) - count + h * count]:
            unit.arrive()
        cols = pl.ds(h * half, half)
        weight = bufs[3][:, :, :, cols].reshape(hidden, half)
        sum_ref[:, cols] = norm_ref[:, cols].astype(jnp.float32) + (nn(act_ref[...], weight) + vec_row(3, cols))
    puts[3].start()
    moves[1].wait()
    length = jnp.where(place.side == 0, length_ref[0], length_ref[1])
    block = rows // 2
    sums_ref[...] = jnp.zeros_like(sums_ref)

    def second_rows(t, carry):
        at = pl.ds(pl.multiple_of(t * chunk, chunk), chunk)
        unit, scale = stats(sum_ref[at, :])
        layer_ref[at, :] = (unit * vec_row(6) + vec_row(7)).astype(low)
        row = lax.broadcasted_iota(jnp.int32, (chunk, 1), 0) + t * chunk
        position = lax.rem(row, block) + (place.core + 2 * lax.div(row, block)) * block
        given = jnp.where(position < length, cot_buf[at, :].astype(jnp.float32), 0.0)
        e = given * vec_row(6)
        first = jnp.mean(e, axis=-1, keepdims=True)
        second = jnp.mean(e * unit, axis=-1, keepdims=True)
        grad = scale * (e - first - unit * second)
        grad_ref[at, :] = grad
        for i, value in enumerate((given * unit, given, grad.astype(low).astype(jnp.float32))):
            sums_ref[i:i + 1, :] += jnp.sum(value, axis=0, keepdims=True)
        return carry

    lax.fori_loop(0, rows // chunk, second_rows, 0)
    for i in (14, 15, 16, 17):
        puts[i].start()
    for unit in units:
        unit.finish()
    for put in puts:
        put.wait()


def encode(dp_size, lengths, weights, dst_shapes, plan, vec, rows_in, cotangent, window=3):
    groups, length, width = rows_in.shape
    rows, z, slots = groups * length, dp_size // 2, dp_size // 2
    anywhere = pl.BlockSpec(memory_space=pl.ANY)
    low = lambda *shape: jax.ShapeDtypeStruct(shape, jnp.bfloat16)
    full = lambda *shape: jax.ShapeDtypeStruct(shape, jnp.float32)
    dma = pltpu.SemaphoreType.DMA
    hidden = dst_shapes[2][1]
    kept = [low(z, 2, *shape) for shape in dst_shapes] + [
        low(rows, width), low(rows, 3 * width), low(rows, width), full(rows, 128), low(rows, 2 * width),
        low(rows, width), full(rows, width), full(rows, 128), low(rows, hidden), low(rows, hidden), full(rows, width),
        low(rows, width), full(8, width), full(8, width),
    ]
    hold = lambda a: pltpu.VMEM(a.shape, a.dtype)
    return pl.pallas_call(
        functools.partial(encode_kernel, dp_size, plan, window, min(256, rows)),
        out_shape=kept,
        in_specs=[pl.BlockSpec(memory_space=pltpu.SMEM)] + [anywhere] * 9,
        out_specs=[anywhere] * len(kept),
        scratch_shapes=gather_sems(dp_size, len(plan)) + [
            pltpu.VMEM((z, 2, *vec.shape), jnp.float32), dma((slots,)), dma((slots,)), dma, dma((2, 3)),
            *[hold(a) for a in kept[:-1]], pltpu.VMEM((rows, width), jnp.bfloat16), hold(kept[-1]),
            pltpu.VMEM((1, hidden), jnp.float32), pltpu.VMEM((rows, width), jnp.float32), dma((len(kept),)),
            pltpu.VMEM((2, 2 * rows, 128), jnp.bfloat16), dma, dma,
        ],
        compiler_params=pltpu.CompilerParams(collective_id=0, has_side_effects=True, vmem_limit_bytes=60 << 20),
        name="encode",
    )(lengths, *weights, vec, rows_in, cotangent)


class Stream:
    def __init__(self, pieces, buf, sem):
        self.copies = [pltpu.make_async_copy(piece, buf.at[i % 2], sem.at[i % 2]) for i, piece in enumerate(pieces)]
        self.buf = buf
        for copy in self.copies[:2]:
            copy.start()

    def get(self, i):
        self.copies[i].wait()
        return self.buf.at[i % 2]

    def next(self, i):
        if i + 2 < len(self.copies):
            self.copies[i + 2].start()


class Stage:
    def __init__(self, buf, sem):
        self.buf, self.sem, self.flying = buf, sem, []

    def put(self, value, dst):
        slot = len(self.flying) % 2
        if len(self.flying) >= 2:
            self.flying[-2].wait()
        self.buf[slot] = value
        self.flying.append(pltpu.make_async_copy(self.buf.at[slot], dst, self.sem.at[slot]))
        self.flying[-1].start()

    def drain(self):
        for copy in self.flying[-2:]:
            copy.wait()
        self.flying = []


def column_sum(value):
    return jnp.sum(value.astype(jnp.float32), axis=0, keepdims=True)


def decode_kernel(dp_size, plan, loads, block, length_ref, *refs):
    (qkv_in, other_in, ctx_in, lse_in, x_in, qkv_w, out_w, up_w, down_w, norm_in, unit_in, scale_in, act_in, slope_in,
     grad_in, layer_in, sums_in, vec_in) = refs[:18]
    outs, vec_outs, layer_out, input_out, parts = refs[18:24], refs[24:33], refs[33], refs[34], refs[35:38]
    scratch = refs[38:]
    got_ref, give_send, give_recv, rows_ref, layer_ref, base_ref, ctx_ref, lse_ref, cgrad_ref, sums_ref, vec_ref = scratch[:11]
    small_ref, small_out, swap_sem, load_sem, late_sem, stream_sem, grad_ref = scratch[11:18]
    small_scratch, reduce_refs = scratch[18:22], scratch[22:]
    place = Place(dp_size)
    rows, width = ctx_ref.shape
    hidden = act_in.shape[1]
    slabs, low, step = width // 128, jnp.bfloat16, 256
    half = width // 2
    early = [pltpu.make_async_copy(a, b, load_sem.at[i]) for i, (a, b) in enumerate((
        (grad_in, base_ref), (layer_in, layer_ref), (ctx_in, ctx_ref), (lse_in, lse_ref), (sums_in, sums_ref), (vec_in, vec_ref)))]
    for copy in early:
        copy.start()
    place.greet()
    moves = [SwapBack(place, a, b, swap_sem.at[i, 0], swap_sem.at[i, 1], swap_sem.at[i, 2])
             for i, (a, b) in enumerate(((layer_ref, layer_out), (rows_ref, input_out)))]
    units = reduce_units(place, (*parts, grad_ref), outs, plan, loads, reduce_refs)
    small = SumAll(place, small_ref, small_out, *small_scratch)
    steps, first = reduce_steps(units)
    clock = iter(range(first, first + len(steps)))

    def tick(count=1):
        for _ in range(count):
            for call in steps[next(clock) - first]:
                call()

    def feed_backward(act_buf, slope_buf, down_buf, up_buf, low_ref, up_low, norm_ref, norm_t, unit_ref, scale_ref, out_buf, ctx_t,
                      tall, flat):
        chunks = hidden // width
        cut = lambda ref, i: ref.at[:, pl.ds(i * width, width)]
        acts = Stream([cut(act_in, i) for i in range(chunks)], act_buf, stream_sem.at[0])
        slopes = Stream([cut(slope_in, i) for i in range(chunks)], slope_buf, stream_sem.at[1])
        downs = Stream([down_w.at[pl.ds(i * width, width)] for i in range(chunks)], down_buf, stream_sem.at[2])
        ups = Stream([cut(up_w, i) for i in range(chunks)], up_buf, stream_sem.at[3])
        others = [pltpu.make_async_copy(a, b, late_sem.at[i]) for i, (a, b) in enumerate((
            (norm_in, norm_ref), (unit_in, unit_ref), (scale_in, scale_ref), (out_w, out_buf)))]
        for copy in others:
            copy.start()
        for copy in early:
            copy.wait()
        moves[0].start()
        small_ref[...] = jnp.zeros_like(small_ref)
        small_ref[3:4, :] = sums_ref[2:3, :]
        small_ref[6:8, :] = sums_ref[0:2, :]
        low_ref[...] = base_ref[...].astype(low)
        stage = Stage(tall, stream_sem.at[4])
        each = hidden // dp_size
        for i in range(chunks):
            act = acts.get(i)
            for o in range(width // each):
                owner = i * (width // each) + o
                value = nn(act[:, o * each:(o + 1) * each].T, low_ref[...])
                stage.put(value.astype(low), parts[0].at[owner // 2, owner % 2])
            acts.next(i)
        stage.drain()
        tick(-first)
        others[0].wait()
        norm_t[...] = norm_ref[...].T
        stage = Stage(flat, stream_sem.at[4])
        shape = (place.depth, 2, width // dp_size, half)
        for i in range(chunks):
            slope, down = slopes.get(i), downs.get(i)

            def slope_part(t, carry):
                cols = pl.ds(pl.multiple_of(t * step, step), step)
                value = nt(low_ref[...], down[cols, :]) * slope[:, cols].astype(jnp.float32)
                up_low[:, cols] = value.astype(low)
                return carry

            lax.fori_loop(0, width // step, slope_part, 0)
            slopes.next(i)
            downs.next(i)
            small_ref[8 + i:9 + i, :] = column_sum(up_low[...])
            for h in range(2):
                value = nn(norm_t[...], up_low[:, h * half:(h + 1) * half]).astype(low)
                stage.put(value.reshape(shape), parts[1].at[:, :, :, pl.ds(i * width + h * half, half)])
            tick()
            up = ups.get(i)

            def back_part(t, carry):
                cols = pl.ds(pl.multiple_of(t * step, step), step)
                base_ref[:, cols] += nt(up_low[...], up[cols, :])
                return carry

            lax.fori_loop(0, width // step, back_part, 0)
            ups.next(i)
            stage.drain()
            tick()
        for copy in others[1:]:
            copy.wait()
        chunk = 128
        gain = vec_ref[4:5, :]

        def first_rows(t, carry):
            at = pl.ds(pl.multiple_of(t * chunk, chunk), chunk)
            given, unit = base_ref[at, :], unit_ref[at, :]
            e = given * gain
            mean = jnp.mean(e, axis=-1, keepdims=True)
            along = jnp.mean(e * unit, axis=-1, keepdims=True)
            grad = scale_ref[at, :][:, :1] * (e - mean - unit * along)
            base_ref[at, :] = grad
            low_ref[at, :] = grad.astype(low)
            for i, value in ((4, given * unit), (5, given), (2, grad.astype(low))):
                small_ref[i:i + 1, :] += column_sum(value)
            return carry

        lax.fori_loop(0, rows // chunk, first_rows, 0)
        ctx_t[...] = ctx_ref[...].T
        for h in range(2):
            value = nn(ctx_t[...], low_ref[:, h * half:(h + 1) * half]).astype(low)
            stage.put(value.reshape(shape), parts[2].at[:, :, :, pl.ds(h * half, half)])
        tick()

        def context_part(t, carry):
            cols = pl.ds(pl.multiple_of(t * step, step), step)
            cgrad_ref[:, cols] = nt(low_ref[...], out_buf[cols, :]).astype(low)
            return carry

        lax.fori_loop(0, width // step, context_part, 0)
        stage.drain()
        tick()

    lows = lambda *shape: pltpu.VMEM(shape, low)
    full = lambda *shape: pltpu.VMEM(shape, jnp.float32)
    pl.run_scoped(
        feed_backward, lows(2, rows, width), lows(2, rows, width), lows(2, width, width), lows(2, width, width), lows(rows, width),
        lows(rows, width), lows(rows, width), lows(width, rows), full(rows, width), full(rows, 128), lows(width, width),
        lows(width, rows), lows(2, hidden // dp_size, width), lows(2, place.depth, 2, width // dp_size, half),
    )

    def attend(qkv_ref, other_ref, x_ref, xt_ref, w_ref, d_ref, dk_ref, dv_ref, *work):
        late = [pltpu.make_async_copy(a, b, late_sem.at[i]) for i, (a, b) in enumerate((
            (qkv_in, qkv_ref), (other_in, other_ref), (x_in, x_ref), (qkv_w, w_ref)))]
        for copy in late:
            copy.start()
        ins = (qkv_ref, other_ref, ctx_ref, cgrad_ref, lse_ref)
        give = Give((place.dp, flip(place.seq, 1)), dk_ref, dv_ref, got_ref, d_ref, rows, width, (give_send, give_recv))
        key_extra(work[0], jnp.where(place.side == 0, length_ref[0], length_ref[1]), place.core, 2 * rows, 0)
        late[2].wait()
        xt_ref[...] = x_ref[...].T
        late[0].wait()
        late[1].wait()

        def weight_part(pair):
            for which in range(3):
                cols = pl.ds(which * width + pair * step, step)
                value = nn(xt_ref[...], d_ref[:, cols]).astype(low)
                grad_ref[:, :, :, pl.ds(pair * width + which * step, step)] = value.reshape(*grad_ref.shape[:3], step)

        before, amid = [], []
        for k in range(slabs):
            before.append(steps[next(clock) - first])
            amid.append(steps[next(clock) - first] if k != slabs - 2 else [])

        def when_slab(j, chosen):
            for k, calls in enumerate(chosen):
                if calls:
                    @pl.when(j == k)
                    def _():
                        for call in calls:
                            call()

        def slab_step(j, carry):
            @pl.when(j >= 2)
            def _():
                give.take(j - 2)

            when_slab(j, [[functools.partial(weight_part, k // 2 - 1)] if k % 2 and k > 2 else [] for k in range(slabs)])
            when_slab(j, before)
            slot = lax.rem(j, 2)
            backward_slab(j, block, ins, work, dk_ref.at[slot], dv_ref.at[slot], d_ref, lambda: when_slab(j, amid))
            give.start(j)
            return carry

        lax.fori_loop(0, slabs, slab_step, 0)
        for j in range(slabs - 2, slabs):
            give.take(j)
        weight_part(slabs // 2 - 1)
        for i, base in ((0, 0), (1, 2 * width)):
            small_ref[i:i + 1, :] = column_sum(d_ref[:, pl.ds(base, width)])
        small.begin()
        tick()
        late[3].wait()

        def input_part(t, carry):
            cols = pl.ds(pl.multiple_of(t * step, step), step)
            rows_ref[:, cols] = (base_ref[:, cols] + nt(d_ref[...], w_ref[cols, :])).astype(low)
            return carry

        lax.fori_loop(0, width // step, input_part, 0)

    pl.run_scoped(
        attend, lows(rows, 3 * width), lows(rows, 2 * width), lows(rows, width), lows(width, rows), lows(width, 3 * width),
        lows(rows, 3 * width), full(2, 2 * rows, 128), full(2, 2 * rows, 128), *backward_work(rows),
    )
    moves[1].start()
    for i, now in enumerate(clock):
        for call in steps[now - first]:
            call()
        if i % 2 and i < 8:
            small.advance(i // 2)
    small.finish()
    share = width // dp_size
    turned = pltpu.roll(small_out[0:8, :], lax.rem(width - place.dp * share, width), 1)
    for i in range(8):
        vec_outs[i][...] = turned[i:i + 1, 0:share]
    wide = small_out[pl.ds(8 + place.z, 1), :]
    vec_outs[8][...] = jnp.where(place.y == 0, wide[:, :width // 2], wide[:, width // 2:])
    for move in moves:
        move.wait()


def decode(dp_size, lengths, ins, out_shapes, part_shapes, plan, rows_shape):
    x = ins[4]
    rows, width = x.shape
    z, loads = dp_size // 2, sum(1 for p in plan if p[0] < len(part_shapes))
    slabs, dma = width // 128, pltpu.SemaphoreType.DMA
    anywhere, vmem = pl.BlockSpec(memory_space=pl.ANY), pl.BlockSpec(memory_space=pltpu.VMEM)
    low = lambda *shape: pltpu.VMEM(shape, jnp.bfloat16)
    full = lambda *shape: pltpu.VMEM(shape, jnp.float32)
    sds = lambda shape, dtype: jax.ShapeDtypeStruct(shape, dtype)
    return pl.pallas_call(
        functools.partial(decode_kernel, dp_size, plan, loads, min(512, rows)),
        out_shape=[sds(s, jnp.float32) for s in out_shapes] + [sds((1, width // dp_size), jnp.float32)] * 8
        + [sds((1, width // 2), jnp.float32)] + [sds(rows_shape, jnp.bfloat16)] * 2 + [sds(s, jnp.bfloat16) for s in part_shapes],
        in_specs=[pl.BlockSpec(memory_space=pltpu.SMEM)] + [anywhere] * len(ins),
        out_specs=[anywhere] * 6 + [vmem] * 9 + [anywhere] * (2 + len(part_shapes)),
        scratch_shapes=[
            full(slabs, 2, rows, 128), dma((slabs, 2)), dma((slabs, 2)), low(rows, width), low(rows, width), full(rows, width),
            low(rows, width), full(rows, 128), low(rows, width), full(8, width), full(8, width),
            full(16, width), full(16, width), dma((2, 3)), dma((6,)), dma((4,)), dma((5, 2)), low(z, 2, plan[0][2], 3 * width),
            full(4, 16, width), full(z + 2, 16, width), dma((z + 2,)), dma((z + 2,)),
        ] + reduce_scratch(dp_size, len(plan), loads, plan[0][2], plan[0][4]),
        compiler_params=pltpu.CompilerParams(collective_id=3, has_side_effects=True, vmem_limit_bytes=62 << 20),
        name="decode",
    )(lengths, *ins)


def settle_kernel(count, *refs):
    srcs, dsts, bufs, sem = refs[:count], refs[count:2 * count], refs[2 * count:3 * count], refs[3 * count]
    gets = [pltpu.make_async_copy(a, b, sem.at[0, i]) for i, (a, b) in enumerate(zip(srcs, bufs))]
    puts = [pltpu.make_async_copy(a.at[0] if len(a.shape) > len(b.shape) else a, b, sem.at[1, i])
            for i, (a, b) in enumerate(zip(bufs, dsts))]
    for get in gets:
        get.start()
    for get, put in zip(gets, puts):
        get.wait()
        put.start()
    for put in puts:
        put.wait()


def settle(arrays):
    count = len(arrays)
    anywhere = pl.BlockSpec(memory_space=pl.ANY)
    shape = lambda a: a.shape[1:] if a.shape[0] == 1 else a.shape
    return pl.pallas_call(
        functools.partial(settle_kernel, count),
        out_shape=[jax.ShapeDtypeStruct(shape(a), a.dtype) for a in arrays],
        in_specs=[anywhere] * count,
        out_specs=[anywhere] * count,
        scratch_shapes=[pltpu.VMEM(a.shape, a.dtype) for a in arrays] + [pltpu.SemaphoreType.DMA((2, count))],
        compiler_params=pltpu.CompilerParams(vmem_limit_bytes=61 << 20),
        name="settle",
    )(*arrays)


def matmul(a, b):
    return jnp.dot(a, b, preferred_element_type=jnp.float32)


def inner_rows(a, b):
    return lax.dot_general(a, b, (((0,), (0,)), ((), ())), preferred_element_type=jnp.float32)


def times_transposed(a, b):
    return lax.dot_general(a, b, (((1,), (1,)), ((), ())), preferred_element_type=jnp.float32)


def swap_rows(rows):
    side = lax.div(lax.axis_index("seq"), 2)
    size = lax.axis_size("seq")
    got = lax.ppermute(lax.dynamic_index_in_dim(rows, 1 - side, 0, False), "seq", [(i, i ^ 2) for i in range(size)])
    kept = lax.dynamic_index_in_dim(rows, side, 0, False)
    first = jnp.where(side == 0, kept, got)
    second = jnp.where(side == 0, got, kept)
    return jnp.concatenate([first, second], axis=0)


def swap_rows_back(rows):
    side = lax.div(lax.axis_index("seq"), 2)
    size = lax.axis_size("seq")
    blocks = rows.reshape(2, rows.shape[0] // 2, rows.shape[1])
    got = lax.ppermute(lax.dynamic_index_in_dim(blocks, 1 - side, 0, False), "seq", [(i, i ^ 2) for i in range(size)])
    kept = lax.dynamic_index_in_dim(blocks, side, 0, False)
    return jnp.stack([jnp.where(side == 0, kept, got), jnp.where(side == 0, got, kept)])


def pack_vectors(narrow, wide):
    rows = jnp.stack([v.astype(jnp.float32) for v in narrow])
    rows = jnp.pad(rows, ((0, 0), (0, 128 - rows.shape[1])))
    more = wide.astype(jnp.float32).reshape(-1, 128)
    both = jnp.concatenate([rows, more], axis=0)
    return jnp.pad(both, ((0, 16 - both.shape[0]), (0, 0)))


def norm_stats(hidden):
    row_mean = jnp.mean(hidden, axis=-1, keepdims=True)
    centred = hidden - row_mean
    row_var = jnp.mean(centred * centred, axis=-1, keepdims=True)
    scale = lax.rsqrt(row_var + eps_norm)
    return centred * scale, scale


def norm_backward(grad, gain, unit, scale):
    e = grad * gain
    first = jnp.mean(e, axis=-1, keepdims=True)
    second = jnp.mean(e * unit, axis=-1, keepdims=True)
    return scale * (e - first - unit * second)


def col_sum(value):
    return jnp.sum(value, axis=0)


def local(
    inputs, lengths, query_weight, key_weight, value_weight, output_weight, up_weight, down_weight,
    query_bias, value_bias, output_bias, up_bias, down_bias, first_gain, first_shift, second_gain, second_shift, cotangent,
):
    dp_size = lax.axis_size("dp")
    groups, length, width = inputs.shape
    shard = query_weight.shape[0]
    fast = dp_size == 8 and shard == 96 and groups == 2
    rows = groups * length
    seq = lax.axis_index("seq")
    core, side = lax.rem(seq, 2), lax.div(seq, 2)
    narrow = [query_bias, value_bias, output_bias, down_bias, first_gain, first_shift, second_gain, second_shift]
    hidden_width = up_weight.shape[1]
    if fast:
        u = shard
        half = width // 2
        cuts = [(i, 0, 0, 0, width * i) for i in (1, 2, 0)] + [(3, 1, 0, 0, 0)]
        cuts += [(4, 2, 0, width * j, width * j) for j in range(hidden_width // width)]
        plan = [(s, d, row, u, col + half * h, half, to + half * h) for s, d, row, col, to in cuts for h in range(2)]
        plan += [(5, 3, u * j, u, half * h, half, half * h) for h in range(2) for j in range(down_weight.shape[0] // u)]
        plan = [(*p, i < len(plan) - 6) for i, p in enumerate(plan)]
        weights = [query_weight, key_weight, value_weight, output_weight, up_weight, down_weight]
        shapes = [(u, 3 * width), (u, width), (u, hidden_width), (down_weight.shape[0], width)]
        (qkv_w, out_w, up_w, down_w, flat_in, qkv, context, lse, other, first_norm, unit_1, scale_1, hidden_act, slope,
         second_sum_grad, layer_rows, sums, flat_vec) = encode(
            dp_size, lengths, weights, shapes, plan, pack_vectors(narrow, up_bias), inputs, cotangent
        )
        qkv_w, out_w = qkv_w.reshape(width, 3 * width), out_w.reshape(width, width)
        up_w, down_w = up_w.reshape(width, hidden_width), down_w.reshape(hidden_width, width)
    else:
        gather = lambda a: lax.all_gather(a, "dp", axis=0, tiled=True)
        qkv_w = gather(jnp.concatenate([query_weight, key_weight, value_weight], axis=1))
        out_w, up_w, down_w = gather(output_weight), gather(up_weight), gather(down_weight)
        flat_vec = jnp.stack([gather(v.astype(jnp.float32)) for v in narrow])
        bias_up = gather(up_bias.astype(jnp.float32))
        flat_in, flat_cot = swap_rows(inputs), swap_rows(cotangent)
    bias_q, bias_v, bias_out, bias_down, gain_1, shift_1, gain_2, shift_2 = [flat_vec[i] for i in range(8)]
    if not fast:
        bias_qkv = jnp.concatenate([bias_q, jnp.zeros_like(bias_q), bias_v])
        qkv = (matmul(flat_in, qkv_w) + bias_qkv).astype(jnp.bfloat16)
        context, lse, other = attend_forward(lengths, qkv)
        first_sum = flat_in.astype(jnp.float32) + (matmul(context, out_w) + bias_out)
        unit_1, scale_1 = norm_stats(first_sum)
        first_norm = (unit_1 * gain_1 + shift_1).astype(jnp.bfloat16)
        up_pre = matmul(first_norm, up_w) + bias_up
        below = 0.5 + 0.5 * lax.erf(up_pre * (0.5 ** 0.5))
        hidden_act = (up_pre * below).astype(jnp.bfloat16)
        slope = (below + up_pre * jnp.exp(-0.5 * up_pre * up_pre) * 0.3989422804014327).astype(jnp.bfloat16)
        down_out = matmul(hidden_act, down_w) + bias_down
        second_sum = first_norm.astype(jnp.float32) + down_out
        unit_2, scale_2 = norm_stats(second_sum)
        layer_rows = (unit_2 * gain_2 + shift_2).astype(jnp.bfloat16)

        row = jnp.arange(rows)
        position = lax.rem(row, length) + (core + 2 * lax.div(row, length)) * length
        live = (position < lengths[side]).astype(jnp.float32)
        grad_out = flat_cot.astype(jnp.float32) * live[:, None]
        second_gain_grad, second_shift_grad = col_sum(grad_out * unit_2), col_sum(grad_out)
        second_sum_grad = norm_backward(grad_out, gain_2, unit_2, scale_2)
        down_bias_grad = col_sum(second_sum_grad.astype(jnp.bfloat16).astype(jnp.float32))
    low = jnp.bfloat16
    if not fast:
        down_low = second_sum_grad.astype(jnp.bfloat16)
        down_w_grad = inner_rows(hidden_act, down_low).astype(low)
        up_low = (times_transposed(down_low, down_w) * slope.astype(jnp.float32)).astype(low)
        up_w_grad = inner_rows(first_norm, up_low).astype(low)
        up_bias_grad = col_sum(up_low.astype(jnp.float32))
        norm_grad = second_sum_grad + times_transposed(up_low, up_w)
        first_gain_grad, first_shift_grad = col_sum(norm_grad * unit_1), col_sum(norm_grad)
        first_sum_grad = norm_backward(norm_grad, gain_1, unit_1, scale_1)
        attended_low = first_sum_grad.astype(low)
        out_w_grad = inner_rows(context, attended_low).astype(low)
        out_bias_grad = col_sum(attended_low.astype(jnp.float32))
        context_grad = times_transposed(attended_low, out_w).astype(low)
        qkv_low = attend_backward(lengths, qkv, other, context, context_grad, lse)
        qkv_w_grad = inner_rows(flat_in, qkv_low)
        qkv_bias_grad = col_sum(qkv_low.astype(jnp.float32))
        input_rows = (first_sum_grad + times_transposed(qkv_low, qkv_w)).astype(low)
        small = jnp.concatenate([
            jnp.stack([qkv_bias_grad[:width], qkv_bias_grad[2 * width:], out_bias_grad, down_bias_grad, first_gain_grad,
                       first_shift_grad, second_gain_grad, second_shift_grad]),
            up_bias_grad.reshape(-1, width),
        ], axis=0)
    me = lax.axis_index("dp")
    if fast:
        plan = [(0, u * j, u, half * h, half, u * j, [(0, half, 5, half * h)]) for j in range(down_weight.shape[0] // u) for h in range(2)]
        plan += [(1, 0, u, half * i, half, 0, [(0, half, 4, half * i)]) for i in range(hidden_width // half)]
        plan += [(2, 0, u, half * h, half, 0, [(0, half, 3, half * h)]) for h in range(2)]
        for p in range(width // 256):
            plan.append((3, 0, u, width * p, half, 0, [(0, 256, 0, 256 * p), (256, 128, 1, 256 * p)]))
            plan.append((3, 0, u, width * p + half, half, 0, [(0, 128, 1, 256 * p + 128), (128, 256, 2, 256 * p)]))
        plan = [(*p, 2 <= i < len(plan) - 8) for i, p in enumerate(plan)]
        shapes = [(u, width)] * 4 + [up_weight.shape, down_weight.shape]
        halves_of = lambda shape: (dp_size // 2, 2, *shape)
        part_shapes = [halves_of(down_weight.shape), halves_of(up_weight.shape), halves_of(output_weight.shape)]
        ins = (qkv, other, context, lse, flat_in, qkv_w, out_w, up_w, down_w, first_norm, unit_1, scale_1, hidden_act, slope,
               second_sum_grad, layer_rows, sums, flat_vec)
        results = decode(dp_size, lengths, ins, shapes, part_shapes, plan, (groups, length, width))
        mine, layer_out, input_grad = results[:15], results[15], results[16]
        layer_out, input_grad, *mine = settle((layer_out, input_grad, *mine))
        weight_grads, mine = mine[:6], mine[6:]
        up_mine = mine.pop()
    else:
        scatter = lambda a: lax.psum(lax.psum_scatter(a.astype(jnp.float32), "dp", scatter_dimension=0, tiled=True), "seq")
        qkv_g = scatter(qkv_w_grad)
        weight_grads = [qkv_g[:, :width], qkv_g[:, width:2 * width], qkv_g[:, 2 * width:]]
        weight_grads += [scatter(out_w_grad), scatter(up_w_grad), scatter(down_w_grad)]
        small = lax.psum(small, ("dp", "seq"))
        layer_out, input_grad = swap_rows_back(layer_rows), swap_rows_back(input_rows)
        part = query_bias.shape[0]
        mine = list(lax.dynamic_slice(small, (0, me * part), (8, part)))
        up_part = up_bias.shape[0]
        up_mine = lax.dynamic_slice(small[8:8 + hidden_width // width].reshape(hidden_width), (me * up_part,), (up_part,))
    return (layer_out, input_grad, *weight_grads, mine[0], mine[1], mine[2], up_mine, *mine[3:8])


def solution(mesh):
    rows, matrix, vector = P("dp", "seq", None), P("dp", None), P("dp")
    return jax.shard_map(
        local,
        mesh=mesh,
        in_specs=(rows, vector, *[matrix] * 6, *[vector] * 9, rows),
        out_specs=(rows, rows, *[matrix] * 6, *[vector] * 9),
        check_vma=False,
    )
```

```python
import collections
import functools
import jax
import jax.numpy as jnp
from jax import lax
from jax.experimental import pallas as pl
from jax.experimental.pallas import tpu as pltpu
from jax.sharding import PartitionSpec as P

MESH = pl.DeviceIdType.MESH
HEAD_DIM = 64
eps_norm = 1e-05
masked_score = -1000000000.0


def flip(value, bits):
    bit = 1
    while bit <= bits:
        if bits & bit:
            value = value + bit - 2 * bit * lax.rem(lax.div(value, bit), 2)
        bit *= 2
    return value


class Place:
    def __init__(self, dp_size):
        self.dp = lax.axis_index("dp")
        self.seq = lax.axis_index("seq")
        self.depth = dp_size // 2
        self.z = lax.div(self.dp, 2)
        self.y = lax.rem(self.dp, 2)
        self.core = lax.rem(self.seq, 2)
        self.side = lax.div(self.seq, 2)

    def along_z(self, k):
        return flip(self.dp, 2 * k)

    def peers(self):
        result = [(self.along_z(k), self.seq) for k in range(1, self.depth)]
        result.append((flip(self.dp, 1), self.seq))
        result.append((self.dp, flip(self.seq, 1)))
        result.append((self.dp, flip(self.seq, 2)))
        return result

    def greet(self):
        barrier = pltpu.get_barrier_semaphore()
        peers = self.peers()
        for peer in peers:
            pl.semaphore_signal(barrier, inc=1, device_id=peer, device_id_type=MESH)
        pl.semaphore_wait(barrier, len(peers))


class Gather:
    def __init__(self, place, src, dst, rows, columns, to_columns, split, sems):
        self.place, self.src, self.dst = place, src, dst
        self.columns, self.to_columns, self.split = columns, to_columns, split
        self.first, count = rows
        self.send, self.recv, self.local = sems
        self.depth = place.depth
        self.unit = unit = count // 6
        half = place.core * (3 * unit)
        self.half = (half, 3 * unit)
        self.fetch = (half + place.side * unit, 2 * unit) if split else self.half
        self.far = (half + place.side * (2 * unit), unit)

    def view(self, z, y, window):
        rows = pl.ds(pl.multiple_of(self.first + window[0], self.unit), window[1])
        return self.dst.at[z, y, rows, pl.ds(*self.to_columns)]

    def copy(self, src, dst, index, peer):
        return pltpu.make_async_remote_copy(
            src_ref=src, dst_ref=dst, send_sem=self.send.at[index], recv_sem=self.recv.at[index],
            device_id=peer, device_id_type=MESH,
        )

    def mine(self):
        rows = pl.ds(pl.multiple_of(self.first + self.fetch[0], self.unit), self.fetch[1])
        return self.src.at[rows, pl.ds(*self.columns)]

    def own(self):
        p = self.place
        return pltpu.make_async_copy(self.mine(), self.view(p.z, p.y, self.fetch), self.local)

    def over_z(self, k):
        p = self.place
        return self.copy(self.mine(), self.view(p.z, p.y, self.fetch), k, (p.along_z(k), p.seq))

    def over_y(self):
        p = self.place
        ref = self.view(slice(None), p.y, self.fetch)
        return self.copy(ref, ref, 0, (flip(p.dp, 1), p.seq))

    def over_x(self):
        p, every = self.place, slice(None)
        ref = self.view(every, every, self.far)
        return self.copy(ref, ref, self.depth, (p.dp, flip(p.seq, 2)))

    def across(self):
        p, every = self.place, slice(None)
        ref = self.view(every, every, self.half)
        return self.copy(ref, ref, self.depth + 1, (p.dp, flip(p.seq, 1)))

    def stage_z(self):
        self.own().start()
        for k in range(1, self.depth):
            self.over_z(k).start()

    def stage_y(self):
        self.own().wait()
        for k in range(1, self.depth):
            self.over_z(k).wait_recv()
        self.over_y().start()

    def stage_x(self):
        self.over_y().wait_recv()
        if self.split:
            self.over_x().start()
        else:
            self.across().start()

    def stage_core(self):
        if self.split:
            self.over_x().wait_recv()
            self.across().start()

    def arrive(self):
        self.across().wait_recv()

    def finish(self):
        for k in range(1, self.depth):
            self.over_z(k).wait_send()
        self.over_y().wait_send()
        if self.split:
            self.over_x().wait_send()
        self.across().wait_send()


def gather_sems(dp_size, units):
    n = dp_size // 2 + 2
    return [pltpu.SemaphoreType.DMA((units, n)), pltpu.SemaphoreType.DMA((units, n)), pltpu.SemaphoreType.DMA((units,))]


class Spread:
    def __init__(self, place, src, dst, sems):
        self.place, self.src, self.dst = place, src, dst
        self.send, self.recv, self.local = sems

    def own(self):
        return pltpu.make_async_copy(self.src, self.dst.at[self.place.z, self.place.y], self.local)

    def over_z(self, k):
        p = self.place
        return pltpu.make_async_remote_copy(
            src_ref=self.src, dst_ref=self.dst.at[p.z, p.y], send_sem=self.send.at[k], recv_sem=self.recv.at[k],
            device_id=(p.along_z(k), p.seq), device_id_type=MESH,
        )

    def over_y(self):
        p = self.place
        ref = self.dst.at[:, p.y]
        return pltpu.make_async_remote_copy(
            src_ref=ref, dst_ref=ref, send_sem=self.send.at[0], recv_sem=self.recv.at[0],
            device_id=(flip(p.dp, 1), p.seq), device_id_type=MESH,
        )

    def start(self):
        self.own().start()
        for k in range(1, self.place.depth):
            self.over_z(k).start()

    def forward(self):
        self.own().wait()
        for k in range(1, self.place.depth):
            self.over_z(k).wait_recv()
        self.over_y().start()

    def finish(self):
        for k in range(1, self.place.depth):
            self.over_z(k).wait_send()
        self.over_y().wait()


def gather_steps(units, window):
    count = len(units)
    steps = [[unit.stage_z for unit in units[:window]]]
    for i in range(count + 4):
        step = []
        if i < count:
            step.append(units[i].stage_y)
            if i + window < count:
                step.append(units[i + window].stage_z)
        if 0 <= i - 2 < count:
            step.append(units[i - 2].stage_x)
        if 0 <= i - 4 < count:
            step.append(units[i - 4].stage_core)
        steps.append(step)
    return steps


def weight_units(place, srcs, dsts, plan, sems):
    send, recv, local = sems
    return [
        Gather(place, srcs[s], dsts[d], (first, rows), (column, width), (to, width), split, (send.at[i], recv.at[i], local.at[i]))
        for i, (s, d, first, rows, column, width, to, split) in enumerate(plan)
    ]


class Swap:
    def __init__(self, place, src, dst, send, recv, local):
        side = place.side
        length = src.shape[1]
        own = dst.at[pl.ds(pl.multiple_of(side * length, 8), length)]
        self.here = pltpu.make_async_copy(src.at[side], own, local)
        self.there = pltpu.make_async_remote_copy(
            src_ref=src.at[1 - side], dst_ref=own, send_sem=send, recv_sem=recv,
            device_id=(place.dp, flip(place.seq, 2)), device_id_type=MESH,
        )

    def start(self):
        self.here.start()
        self.there.start()

    def wait(self):
        self.here.wait()
        self.there.wait()


class SwapBack:
    def __init__(self, place, src, dst, send, recv, local):
        side, length = place.side, dst.shape[1]
        block = lambda i: src.at[pl.ds(pl.multiple_of(i * length, length), length)]
        self.here = pltpu.make_async_copy(block(side), dst.at[side], local)
        self.there = pltpu.make_async_remote_copy(
            src_ref=block(1 - side), dst_ref=dst.at[side], send_sem=send, recv_sem=recv,
            device_id=(place.dp, flip(place.seq, 2)), device_id_type=MESH,
        )

    def start(self):
        self.here.start()
        self.there.start()

    def wait(self):
        self.here.wait()
        self.there.wait()


class Reduce:
    def __init__(self, place, src, rows, columns, targets, to_row, split, own, bufs, sems):
        self.place, self.src, self.targets, self.split = place, src, targets, split
        self.columns, self.to_row = columns, to_row
        self.first, count = rows
        self.unit = unit = count // 6
        self.from_core, self.from_x, self.from_y, self.from_z, self.got, self.total = bufs
        self.send, self.recv = sems
        self.depth = place.depth
        self.half = place.core * (3 * unit)
        self.sibling_half = (1 - place.core) * (3 * unit)
        self.keep = (place.side * unit, 2 * unit) if split else (0, 3 * unit)
        self.loads = own is not None
        self.own = own if self.loads else self.view(self.half)

    def view(self, start):
        rows = pl.ds(pl.multiple_of(self.first + start, self.unit), 3 * self.unit)
        return self.src.at[:, :, rows, pl.ds(*self.columns)]

    def rows(self, window):
        return pl.ds(pl.multiple_of(window[0], self.unit), window[1])

    def copy(self, src, dst, index, peer):
        return pltpu.make_async_remote_copy(
            src_ref=src, dst_ref=dst, send_sem=self.send.at[index], recv_sem=self.recv.at[index],
            device_id=peer, device_id_type=MESH,
        )

    def load(self):
        return pltpu.make_async_copy(self.view(self.half), self.own, self.send.at[0])

    def core(self):
        p = self.place
        return self.copy(self.view(self.sibling_half), self.from_core, self.depth, (p.dp, flip(p.seq, 1)))

    def far(self):
        return ((1 - self.place.side) * (2 * self.unit), self.unit)

    def x(self):
        p = self.place
        return self.copy(self.own.at[:, :, self.rows(self.far())], self.from_x, self.depth + 1, (p.dp, flip(p.seq, 2)))

    def y(self):
        p = self.place
        src = self.own.at[:, 1 - p.y, self.rows(self.keep)]
        return self.copy(src, self.from_y.at[:, pl.ds(0, self.keep[1])], self.depth + 2, (flip(p.dp, 1), p.seq))

    def z(self, k):
        p = self.place
        src = self.own.at[flip(p.z, k), p.y, self.rows(self.keep)]
        return self.copy(src, self.from_z.at[k - 1, pl.ds(0, self.keep[1])], k, (p.along_z(k), p.seq))

    def x_last(self):
        p = self.place
        src = self.own.at[p.z, p.y, self.rows(self.keep)]
        return self.copy(src, self.got.at[pl.ds(0, self.keep[1])], self.depth + 3, (p.dp, flip(p.seq, 2)))

    def puts(self):
        p, n = self.place, self.depth
        rows = pl.ds(pl.multiple_of(self.to_row + self.half, self.unit), 3 * self.unit)
        here, there = [], []
        for i, (column, width, out, to) in enumerate(self.targets):
            src, dst = self.total.at[:, pl.ds(column, width)], out.at[rows, pl.ds(to, width)]
            here.append(pltpu.make_async_copy(src, dst, self.send.at[n + 6 + i]))
            there.append(self.copy(src, dst, n + 4 + i, (p.dp, flip(p.seq, 1))))
        return here + there

    def chip(self, z, y, window):
        rows = self.rows(window)
        return self.own[z, y, rows, :].astype(jnp.float32) + self.from_core[z, y, rows, :].astype(jnp.float32)

    def pieces(self, z, y):
        u, side = self.unit, self.place.side
        if not self.split:
            return [((i * u, u), (i * u, u), self.chip(z, y, (i * u, u))) for i in range(3)]
        solo = (side * (2 * u), u)
        gained = self.chip(z, y, solo) + self.from_x[z, y, :, :].astype(jnp.float32)
        return [((u, u), ((1 - side) * u, u), self.chip(z, y, (u, u))), (solo, (side * u, u), gained)]

    def stage_core(self):
        if self.loads:
            self.load().start()
        self.core().start()

    def stage_x(self):
        if self.loads:
            self.load().wait()
        self.core().wait_recv()
        if not self.split:
            return
        rows = self.rows(self.far())

        def body(z, carry):
            for y in range(2):
                self.own[z, y, rows, :] = self.chip(z, y, self.far()).astype(jnp.bfloat16)
            return carry

        lax.fori_loop(0, self.depth, body, 0)
        self.x().start()

    def stage_y(self):
        if self.split:
            self.x().wait_recv()
        y = 1 - self.place.y

        def body(z, carry):
            for at, _, value in self.pieces(z, y):
                self.own[z, y, self.rows(at), :] = value.astype(jnp.bfloat16)
            return carry

        lax.fori_loop(0, self.depth, body, 0)
        self.y().start()

    def column(self, z):
        return [
            (at, kept, value + self.from_y[z, self.rows(kept), :].astype(jnp.float32))
            for at, kept, value in self.pieces(z, self.place.y)
        ]

    def stage_z(self):
        self.y().wait_recv()
        for k in range(1, self.depth):
            z = flip(self.place.z, k)
            for at, _, value in self.column(z):
                self.own[z, self.place.y, self.rows(at), :] = value.astype(jnp.bfloat16)
            self.z(k).start()

    def stage_last(self):
        for k in range(1, self.depth):
            self.z(k).wait_recv()
        p = self.place
        for at, kept, value in self.column(p.z):
            for k in range(1, self.depth):
                value = value + self.from_z[k - 1, self.rows(kept), :].astype(jnp.float32)
            self.own[p.z, p.y, self.rows(at), :] = value.astype(jnp.bfloat16)
        self.x_last().start()

    def stage_out(self):
        self.x_last().wait_recv()
        p, u = self.place, self.unit
        mine = lambda at: self.own[p.z, p.y, self.rows(at), :].astype(jnp.float32)
        got = lambda at: self.got[self.rows(at), :].astype(jnp.float32)
        if self.split:
            side = p.side
            self.total[self.rows((u, u)), :] = mine((u, u)) + got((side * u, u))
            self.total[self.rows((side * (2 * u), u)), :] = mine((side * (2 * u), u))
            self.total[self.rows((2 * u - side * (2 * u), u)), :] = got(((1 - side) * u, u))
        else:
            whole = (0, 3 * u)
            self.total[...] = mine(whole) + got(whole)
        for put in self.puts():
            put.start()

    def finish(self):
        self.core().wait_send()
        if self.split:
            self.x().wait_send()
        self.y().wait_send()
        for k in range(1, self.depth):
            self.z(k).wait_send()
        self.x_last().wait_send()
        for put in self.puts():
            put.wait()


def reduce_scratch(dp_size, units, loads, rows, width):
    z, u = dp_size // 2, rows // 6
    low = lambda count, *shape: pltpu.VMEM((count, *shape, width), jnp.bfloat16)
    return [
        low(loads, z, 2, 3 * u), low(units, z, 2, 3 * u), low(units, z, 2, u), low(units, z, 3 * u), low(units, z - 1, 3 * u),
        low(units, 3 * u), pltpu.VMEM((units, 3 * u, width), jnp.float32),
        pltpu.SemaphoreType.DMA((units, z + 8)), pltpu.SemaphoreType.DMA((units, z + 8)),
    ]


def reduce_units(place, srcs, outs, plan, loads, scratch):
    own, bufs, send, recv = scratch[0], scratch[1:-2], scratch[-2], scratch[-1]
    return [
        Reduce(place, srcs[s], (first, rows), (column, width), [(a, w, outs[o], to) for a, w, o, to in targets], to_row, split,
               own.at[i] if i < loads else None, [b.at[i] for b in bufs], (send.at[i], recv.at[i]))
        for i, (s, first, rows, column, width, to_row, targets, split) in enumerate(plan)
    ]


STAGES = ("stage_core", "stage_x", "stage_y", "stage_z", "stage_last", "stage_out", "finish")


def reduce_steps(units):
    first, steps = -3, collections.defaultdict(list)
    for i, unit in enumerate(units):
        lag = 2 if unit.split else 0
        ages = (-3 if unit.loads else -1, 0, lag, lag + 2, lag + 4, lag + 6, lag + 8)
        for stage, age in zip(STAGES, ages):
            steps[i + age].append((-age, getattr(unit, stage)))
    ticks = range(first, max(steps) + 1)
    return [[call for _, call in sorted(steps[tick], key=lambda pair: pair[0])] for tick in ticks], first


class SumAll:
    def __init__(self, place, src, out, buf, got, send, recv):
        self.place, self.src, self.out, self.buf, self.got, self.send, self.recv = place, src, out, buf, got, send, recv

    def copy(self, stage, slot, peer):
        return pltpu.make_async_remote_copy(
            src_ref=self.buf.at[stage], dst_ref=self.got.at[slot], send_sem=self.send.at[slot], recv_sem=self.recv.at[slot],
            device_id=peer, device_id_type=MESH,
        )

    def copies(self, stage):
        p = self.place
        if stage < 3:
            peer = [(p.dp, flip(p.seq, 1)), (p.dp, flip(p.seq, 2)), (flip(p.dp, 1), p.seq)][stage]
            return [self.copy(stage, stage, peer)]
        return [self.copy(3, 2 + k, (p.along_z(k), p.seq)) for k in range(1, p.depth)]

    def begin(self):
        self.buf[0] = self.src[...]
        for c in self.copies(0):
            c.start()

    def advance(self, stage):
        for c in self.copies(stage):
            c.wait_recv()
        if stage < 3:
            self.buf[stage + 1] = self.buf[stage] + self.got[stage]
            for c in self.copies(stage + 1):
                c.start()
        else:
            z, n = self.place.z, self.place.depth
            pick = lambda i: i
            total = self.buf[3]
            parts = [self.buf[3]] + [self.got[2 + k] for k in range(1, n)]
            total = (parts[0] + parts[1]) + (parts[2] + parts[3])
            self.out[...] = total

    def finish(self):
        for stage in range(4):
            for c in self.copies(stage):
                c.wait_send()


def halves(width):
    lane = lax.broadcasted_iota(jnp.int32, (1, width), 1)
    return lane


def key_extra(extra_ref, length, core, rows, first_pos):
    block = rows // 4
    row = lax.broadcasted_iota(jnp.int32, (rows, 128), 0)
    lane = lax.broadcasted_iota(jnp.int32, (rows, 128), 1)
    part = row // block
    owner = jnp.where(part < 2, core, 1 - core)
    position = row - part * block + (owner + 2 * lax.rem(part, 2)) * block
    dead = jnp.where(position < length, 0.0, masked_score)
    for parity in range(2):
        base = HEAD_DIM * (1 - parity)
        at = lane - base
        value = jnp.where(at == 0, dead, jnp.where((at > 0) & (at < 4), -1.0, 0.0))
        extra_ref[parity, :, :] = value.astype(jnp.bfloat16)


def split3(value):
    high = value.astype(jnp.bfloat16).astype(jnp.float32)
    rest = value - high
    mid = rest.astype(jnp.bfloat16).astype(jnp.float32)
    return high, mid, rest - mid


def nt(a, b):
    return lax.dot_general(a, b, (((1,), (1,)), ((), ())), preferred_element_type=jnp.float32)


def nn(a, b):
    return jnp.dot(a, b, preferred_element_type=jnp.float32)


def greet_sibling(peer):
    barrier = pltpu.get_barrier_semaphore()
    pl.semaphore_signal(barrier, inc=1, device_id=peer, device_id_type=MESH)
    pl.semaphore_wait(barrier, 1)


def forward_slab(j, tile, qkv_ref, other_ref, extra_ref, ctx_ref, lse_ref, between=None):
    rows, width = ctx_ref.shape
    lane = lax.broadcasted_iota(jnp.int32, (1, 128), 1)
    cols = lambda base: pl.ds(base + 128 * j if isinstance(j, int) else pl.multiple_of(base + 128 * j, 128), 128)
    keys = jnp.concatenate([qkv_ref[:, cols(width)], other_ref[:, cols(0)]], axis=0)
    values = jnp.concatenate([qkv_ref[:, cols(2 * width)], other_ref[:, cols(width)]], axis=0)
    queries = qkv_ref[:, cols(0)]
    outs, stats = [], []
    for parity in range(2):
        mine = (lane < HEAD_DIM) if parity == 0 else (lane >= HEAD_DIM)
        mark = jnp.where(lane == HEAD_DIM * (1 - parity), 1.0, 0.0).astype(jnp.bfloat16)
        k_h = jnp.where(mine, keys, extra_ref[parity])
        v_h = jnp.where(mine, values, jnp.ones_like(values))
        q_h = jnp.where(mine, queries * jnp.bfloat16(HEAD_DIM ** -0.5), mark)
        pieces, tops = [], []
        for t in range(rows // tile):
            scores = nt(q_h[t * tile:(t + 1) * tile], k_h)
            top = jnp.max(scores, axis=-1, keepdims=True)
            pieces.append(nn(jnp.exp(scores - top).astype(jnp.bfloat16), v_h))
            tops.append(top)
        out, top = jnp.concatenate(pieces, axis=0), jnp.concatenate(tops, axis=0)
        other = HEAD_DIM * (1 - parity)
        total = out[:, other:other + 1]
        outs.append(out / total)
        stats.append(top + jnp.log(total))
        if between is not None:
            between()
    ctx_ref[:, cols(0)] = jnp.where(lane < HEAD_DIM, outs[0], outs[1]).astype(jnp.bfloat16)
    lse_ref[...] = jnp.where(lane == 2 * j, stats[0], jnp.where(lane == 2 * j + 1, stats[1], lse_ref[...]))


def backward_slab(j, block, ins, work, dk_ref, dv_ref, out_ref, between=None):
    qkv_ref, other_ref, ctx_ref, grad_ref, lse_ref = ins
    extra_ref, k_ref, v_ref, q_ref, g_ref, kt_ref, dq_ref = work
    rows, width = ctx_ref.shape
    low = jnp.bfloat16
    lane = lax.broadcasted_iota(jnp.int32, (1, 128), 1)
    sub = lax.broadcasted_iota(jnp.int32, (128, 1), 0)
    cols = lambda base: pl.ds(base + 128 * j if isinstance(j, int) else pl.multiple_of(base + 128 * j, 128), 128)
    keys = jnp.concatenate([qkv_ref[:, cols(width)], other_ref[:, cols(0)]], axis=0)
    values = jnp.concatenate([qkv_ref[:, cols(2 * width)], other_ref[:, cols(width)]], axis=0)
    queries = qkv_ref[:, cols(0)] * jnp.bfloat16(HEAD_DIM ** -0.5)
    grads = grad_ref[:, cols(0)]
    along = grads.astype(jnp.float32) * ctx_ref[:, cols(0)].astype(jnp.float32)
    lse = lse_ref[...]
    for parity in range(2):
        mine = (lane < HEAD_DIM) if parity == 0 else (lane >= HEAD_DIM)
        at = lane - HEAD_DIM * (1 - parity)
        delta = jnp.sum(jnp.where(mine, along, 0.0), axis=-1, keepdims=True)
        stat = jnp.sum(jnp.where(lane == 2 * j + parity, lse, 0.0), axis=-1, keepdims=True)
        s0, s1, s2 = split3(stat)
        d0, d1, d2 = split3(delta)
        q_more = jnp.where(at == 0, 1.0, jnp.where(at == 1, s0, jnp.where(at == 2, s1, jnp.where(at == 3, s2, 0.0)))).astype(low)
        g_more = jnp.where(at == 1, d0, jnp.where(at == 2, d1, jnp.where(at == 3, d2, 0.0))).astype(low)
        k_ref[parity] = jnp.where(mine, keys, extra_ref[parity])
        v_ref[parity] = jnp.where(mine, values, extra_ref[parity])
        q_ref[parity] = jnp.where(mine, queries, q_more)
        g_ref[parity] = jnp.where(mine, grads, g_more)
        kt_ref[parity] = jnp.where((sub < HEAD_DIM) if parity == 0 else (sub >= HEAD_DIM), keys.T, jnp.zeros((128, 2 * rows), low))
    dq_ref[...] = jnp.zeros_like(dq_ref)

    def part(b, carry):
        span = pl.ds(pl.multiple_of(b * block, block), block)
        made = []
        for parity in range(2):
            q_h, g_h = q_ref[parity], g_ref[parity]
            prob = jnp.exp(nt(k_ref[parity, span, :], q_h))
            slope = nt(v_ref[parity, span, :], g_h)
            ds = (prob * slope).astype(low)
            dv = nn(prob.astype(low), g_h)
            dk = nn(ds, q_h)
            dq_ref[...] += nn(kt_ref[parity, :, span], ds)
            made.append((dk, dv))
        dk_ref[span, :] = jnp.where(lane < HEAD_DIM, made[0][0], made[1][0])
        dv_ref[span, :] = jnp.where(lane < HEAD_DIM, made[0][1], made[1][1])
        return carry

    count, cuts = 2 * rows // block, (0, 2, 4) if between is not None else (0, 4)
    for low_cut, high_cut in zip(cuts, cuts[1:]):
        if low_cut:
            between()
        lax.fori_loop(low_cut * count // 4, high_cut * count // 4, part, 0)
    out_ref[:, cols(0)] = (dq_ref[...].T * (HEAD_DIM ** -0.5)).astype(low)


def backward_work(rows):
    low = lambda *shape: pltpu.VMEM(shape, jnp.bfloat16)
    return [
        low(2, 2 * rows, 128), low(2, 2 * rows, 128), low(2, 2 * rows, 128), low(2, rows, 128), low(2, rows, 128),
        low(2, 128, 2 * rows), pltpu.VMEM((128, rows), jnp.float32),
    ]


class Give:
    def __init__(self, peer, dk_ref, dv_ref, got_ref, out_ref, rows, width, sems):
        self.peer, self.pair, self.got_ref, self.out_ref = peer, (dk_ref, dv_ref), got_ref, out_ref
        self.rows, self.width, (self.send, self.recv) = rows, width, sems

    def copy(self, j, which):
        return pltpu.make_async_remote_copy(
            src_ref=self.pair[which].at[lax.rem(j, 2), pl.ds(self.rows, self.rows)], dst_ref=self.got_ref.at[j, which],
            send_sem=self.send.at[j, which], recv_sem=self.recv.at[j, which], device_id=self.peer, device_id_type=MESH,
        )

    def start(self, j):
        for which in range(2):
            self.copy(j, which).start()

    def take(self, j):
        for which in range(2):
            self.copy(j, which).wait()
            total = self.pair[which][lax.rem(j, 2), pl.ds(0, self.rows), :] + self.got_ref[j, which]
            start = (1 + which) * self.width + j * 128
            self.out_ref[:, pl.ds(start if isinstance(j, int) else pl.multiple_of(start, 128), 128)] = total.astype(jnp.bfloat16)


def forward_kernel(tile, length_ref, qkv_ref, ctx_ref, lse_ref, other_ref, extra_ref, send, recv):
    seq = lax.axis_index("seq")
    core, side = lax.rem(seq, 2), lax.div(seq, 2)
    peer = (lax.axis_index("dp"), flip(seq, 1))
    rows, width = ctx_ref.shape
    greet_sibling(peer)
    swap = pltpu.make_async_remote_copy(
        src_ref=qkv_ref.at[:, pl.ds(width, 2 * width)], dst_ref=other_ref, send_sem=send, recv_sem=recv,
        device_id=peer, device_id_type=MESH,
    )
    swap.start()
    key_extra(extra_ref, jnp.where(side == 0, length_ref[0], length_ref[1]), core, 2 * rows, 0)
    swap.wait()
    lse_ref[...] = jnp.zeros_like(lse_ref)

    def slab(j, carry):
        forward_slab(j, tile, qkv_ref, other_ref, extra_ref, ctx_ref, lse_ref)
        return carry

    lax.fori_loop(0, width // 128, slab, 0)


def attend_forward(lengths, qkv):
    rows, width = qkv.shape[0], qkv.shape[1] // 3
    vmem = pl.BlockSpec(memory_space=pltpu.VMEM)
    return pl.pallas_call(
        functools.partial(forward_kernel, min(256, rows)),
        out_shape=[
            jax.ShapeDtypeStruct((rows, width), jnp.bfloat16),
            jax.ShapeDtypeStruct((rows, 128), jnp.float32),
            jax.ShapeDtypeStruct((rows, 2 * width), jnp.bfloat16),
        ],
        in_specs=[pl.BlockSpec(memory_space=pltpu.SMEM), vmem],
        out_specs=[vmem] * 3,
        scratch_shapes=[pltpu.VMEM((2, 2 * rows, 128), jnp.bfloat16), pltpu.SemaphoreType.DMA, pltpu.SemaphoreType.DMA],
        compiler_params=pltpu.CompilerParams(collective_id=1, has_side_effects=True, vmem_limit_bytes=48 << 20),
        name="attend_forward",
    )(lengths, qkv)


def backward_kernel(block, length_ref, *refs):
    ins, out_ref, work, (dk_ref, dv_ref, got_ref, send, recv) = refs[:5], refs[5], refs[6:13], refs[13:]
    seq = lax.axis_index("seq")
    core, side = lax.rem(seq, 2), lax.div(seq, 2)
    peer = (lax.axis_index("dp"), flip(seq, 1))
    rows, width = ins[2].shape
    greet_sibling(peer)
    key_extra(work[0], jnp.where(side == 0, length_ref[0], length_ref[1]), core, 2 * rows, 0)
    give = Give(peer, dk_ref, dv_ref, got_ref, out_ref, rows, width, (send, recv))
    for j in range(width // 128):
        if j >= 2:
            give.take(j - 2)
        backward_slab(j, block, ins, work, dk_ref.at[j % 2], dv_ref.at[j % 2], out_ref)
        give.start(j)
    for j in range(width // 128 - 2, width // 128):
        give.take(j)


def attend_backward(lengths, qkv, other, ctx, grad, lse):
    rows, width = ctx.shape
    slabs = width // 128
    vmem = pl.BlockSpec(memory_space=pltpu.VMEM)
    return pl.pallas_call(
        functools.partial(backward_kernel, min(256, rows)),
        out_shape=jax.ShapeDtypeStruct(qkv.shape, jnp.bfloat16),
        in_specs=[pl.BlockSpec(memory_space=pltpu.SMEM)] + [vmem] * 5,
        out_specs=vmem,
        scratch_shapes=backward_work(rows) + give_scratch(rows, slabs),
        compiler_params=pltpu.CompilerParams(collective_id=2, has_side_effects=True, vmem_limit_bytes=56 << 20),
        name="attend_backward",
    )(lengths, qkv, other, ctx, grad, lse)


def give_scratch(rows, slabs):
    full = lambda *shape: pltpu.VMEM(shape, jnp.float32)
    return [
        full(2, 2 * rows, 128), full(2, 2 * rows, 128), full(slabs, 2, rows, 128),
        pltpu.SemaphoreType.DMA((slabs, 2)), pltpu.SemaphoreType.DMA((slabs, 2)),
    ]


def encode_kernel(dp_size, plan, window, tile, length_ref, *refs):
    srcs, vec, rows_in, cot_in = refs[:6], refs[6], refs[7], refs[8]
    results = refs[9:27]
    (send, recv, local, vec_buf, vec_send, vec_recv, vec_local, swap_sem, *bufs, x_buf, qkv_ref, ctx_ref, lse_ref, other_ref,
     norm_ref, unit_ref, scale_ref, act_ref, slope_ref, grad_ref, layer_ref, sums_ref, cot_buf, flat_vec, bias_up, sum_ref, out_sem,
     extra_ref, kv_send, kv_recv) = refs[27:]
    w_buf = bufs[0]
    place = Place(dp_size)
    rows, width = ctx_ref.shape
    place.greet()
    moves = [Swap(place, a, b, swap_sem.at[i, 0], swap_sem.at[i, 1], swap_sem.at[i, 2])
             for i, (a, b) in enumerate(((rows_in, x_buf), (cot_in, cot_buf)))]
    spread = Spread(place, vec, vec_buf, (vec_send, vec_recv, vec_local))
    units = weight_units(place, srcs, bufs, plan, (send, recv, local))
    steps = gather_steps(units, window)
    kept = (*bufs, x_buf, qkv_ref, ctx_ref, lse_ref, other_ref, norm_ref, unit_ref, scale_ref, act_ref, slope_ref, grad_ref,
            layer_ref, sums_ref, flat_vec)
    puts = [pltpu.make_async_copy(a, b, out_sem.at[i]) for i, (a, b) in enumerate(zip(kept, results))]
    clock = iter(steps)

    def run(count=1):
        for _ in range(count):
            for call in next(clock, ()):
                call()

    spread.start()
    moves[0].start()
    run()
    spread.forward()
    run()
    key_extra(extra_ref, jnp.where(place.side == 0, length_ref[0], length_ref[1]), place.core, 2 * rows, 0)
    lse_ref[...] = jnp.zeros_like(lse_ref)
    run()
    spread.finish()
    lane = lax.broadcasted_iota(jnp.int32, (8, 128), 1)
    total = jnp.zeros((8, width), jnp.float32)
    share = width // dp_size
    for owner in range(dp_size):
        piece = jnp.where(lane < share, vec_buf[owner // 2, owner % 2, 0:8, :], 0.0)
        padded = jnp.concatenate([piece, jnp.zeros((8, width - 128), jnp.float32)], axis=1)
        total = total + (pltpu.roll(padded, owner * share, 1) if owner else padded)
    flat_vec[...] = total
    wide = bias_up.shape[1] // dp_size // 128
    for owner in range(dp_size):
        for i in range(wide):
            bias_up[:, pl.ds((owner * wide + i) * 128, 128)] = vec_buf[owner // 2, owner % 2, 8 + i:9 + i, :]
    run(9)
    moves[0].wait()
    puts[4].start()

    def fetch(first):
        for i in range(first, first + 2):
            units[i].arrive()

    step = 256

    def project(first, count):
        def body(t, carry):
            cols = pl.ds(pl.multiple_of(first + t * step, step), step)
            weight = w_buf[:, :, :, cols].reshape(width, step)
            qkv_ref[:, cols] = nn(x_buf[...], weight).astype(jnp.bfloat16)
            return carry

        lax.fori_loop(0, count, body, 0)

    def project_bias(first, row):
        def body(t, carry):
            cols = pl.ds(pl.multiple_of(first + t * step, step), step)
            bias = flat_vec[row:row + 1, pl.ds(pl.multiple_of(t * step, step), step)]
            weight = w_buf[:, :, :, cols].reshape(width, step)
            qkv_ref[:, cols] = (nn(x_buf[...], weight) + bias).astype(jnp.bfloat16)
            return carry

        lax.fori_loop(0, width // step, body, 0)

    fetch(0)
    project(width, width // step)
    run()
    fetch(2)
    project_bias(2 * width, 1)
    swap = pltpu.make_async_remote_copy(
        src_ref=qkv_ref.at[:, pl.ds(width, 2 * width)], dst_ref=other_ref, send_sem=kv_send, recv_sem=kv_recv,
        device_id=(place.dp, flip(place.seq, 1)), device_id_type=MESH,
    )
    swap.start()
    run()
    fetch(4)
    project_bias(0, 0)
    run()
    swap.wait()
    counts = []
    taken = [step for step in clock]
    clock = iter(taken)

    def forward_two(j, carry):
        def between():
            counts.append(len(counts))
            for k in range(width // 128):
                index = 2 * k + len(counts) - 1
                if index < len(taken):
                    @pl.when(j == k)
                    def _():
                        for call in taken[index]:
                            call()

        forward_slab(j, tile, qkv_ref, other_ref, extra_ref, ctx_ref, lse_ref, between)

        @pl.when(j == 1)
        def _():
            moves[1].start()

        return carry

    lax.fori_loop(0, width // 128, forward_two, 0)
    for _ in range(2 * (width // 128)):
        next(clock, ())
    for i in (0, 5, 6, 7, 8):
        puts[i].start()
    low = jnp.bfloat16
    vec_row = lambda i, cols=slice(None): flat_vec[i:i + 1, cols]

    def out_part(t, carry):
        cols = pl.ds(pl.multiple_of(t * step, step), step)
        weight = bufs[1][:, :, :, cols].reshape(width, step)
        sum_ref[:, cols] = x_buf[:, cols].astype(jnp.float32) + (nn(ctx_ref[...], weight) + vec_row(2, cols))
        return carry

    units[6].arrive()
    units[7].arrive()
    lax.fori_loop(0, width // step, out_part, 0)
    puts[1].start()
    run()
    chunk = 128

    def stats(value):
        centred = value - jnp.mean(value, axis=-1, keepdims=True)
        scale = lax.rsqrt(jnp.mean(centred * centred, axis=-1, keepdims=True) + eps_norm)
        return centred * scale, scale

    def first_rows(t, carry):
        at = pl.ds(pl.multiple_of(t * chunk, chunk), chunk)
        unit, scale = stats(sum_ref[at, :])
        unit_ref[at, :] = unit
        scale_ref[at, :] = jnp.broadcast_to(scale, (chunk, 128))
        norm_ref[at, :] = (unit * vec_row(4) + vec_row(5)).astype(low)
        return carry

    lax.fori_loop(0, rows // chunk, first_rows, 0)
    for i in (9, 10, 11):
        puts[i].start()
    run()
    hidden = act_ref.shape[1]

    def up_part(t, carry):
        cols = pl.ds(pl.multiple_of(t * step, step), step)
        weight = bufs[2][:, :, :, cols].reshape(width, step)
        value = nn(norm_ref[...], weight) + bias_up[:, cols]
        below = 0.5 + 0.5 * lax.erf(value * (0.5 ** 0.5))
        act_ref[:, cols] = (value * below).astype(low)
        slope_ref[:, cols] = (below + value * jnp.exp(-0.5 * value * value) * 0.3989422804014327).astype(low)
        return carry

    for j in range(hidden // width):
        for unit in units[8 + 2 * j:10 + 2 * j]:
            unit.arrive()
        ahead = [next(clock, ()) for _ in range(width // step)]
        base = j * width // step

        def up_step(t, carry):
            up_part(t, carry)
            for k, calls in enumerate(ahead):
                if calls:
                    @pl.when(t == base + k)
                    def _():
                        for call in calls:
                            call()
            return carry

        lax.fori_loop(base, base + width // step, up_step, 0)
    for i in (2, 12, 13):
        puts[i].start()
    run(len(steps))
    half = width // 2
    count = hidden // width
    for h in range(2):
        for unit in units[-2 * count + h * count:len(units) - count + h * count]:
            unit.arrive()
        cols = pl.ds(h * half, half)
        weight = bufs[3][:, :, :, cols].reshape(hidden, half)
        sum_ref[:, cols] = norm_ref[:, cols].astype(jnp.float32) + (nn(act_ref[...], weight) + vec_row(3, cols))
    puts[3].start()
    moves[1].wait()
    length = jnp.where(place.side == 0, length_ref[0], length_ref[1])
    block = rows // 2
    sums_ref[...] = jnp.zeros_like(sums_ref)

    def second_rows(t, carry):
        at = pl.ds(pl.multiple_of(t * chunk, chunk), chunk)
        unit, scale = stats(sum_ref[at, :])
        layer_ref[at, :] = (unit * vec_row(6) + vec_row(7)).astype(low)
        row = lax.broadcasted_iota(jnp.int32, (chunk, 1), 0) + t * chunk
        position = lax.rem(row, block) + (place.core + 2 * lax.div(row, block)) * block
        given = jnp.where(position < length, cot_buf[at, :].astype(jnp.float32), 0.0)
        e = given * vec_row(6)
        first = jnp.mean(e, axis=-1, keepdims=True)
        second = jnp.mean(e * unit, axis=-1, keepdims=True)
        grad = scale * (e - first - unit * second)
        grad_ref[at, :] = grad
        for i, value in enumerate((given * unit, given, grad.astype(low).astype(jnp.float32))):
            sums_ref[i:i + 1, :] += jnp.sum(value, axis=0, keepdims=True)
        return carry

    lax.fori_loop(0, rows // chunk, second_rows, 0)
    for i in (14, 15, 16, 17):
        puts[i].start()
    for unit in units:
        unit.finish()
    for put in puts:
        put.wait()


def encode(dp_size, lengths, weights, dst_shapes, plan, vec, rows_in, cotangent, window=3):
    groups, length, width = rows_in.shape
    rows, z, slots = groups * length, dp_size // 2, dp_size // 2
    anywhere = pl.BlockSpec(memory_space=pl.ANY)
    low = lambda *shape: jax.ShapeDtypeStruct(shape, jnp.bfloat16)
    full = lambda *shape: jax.ShapeDtypeStruct(shape, jnp.float32)
    dma = pltpu.SemaphoreType.DMA
    hidden = dst_shapes[2][1]
    kept = [low(z, 2, *shape) for shape in dst_shapes] + [
        low(rows, width), low(rows, 3 * width), low(rows, width), full(rows, 128), low(rows, 2 * width),
        low(rows, width), full(rows, width), full(rows, 128), low(rows, hidden), low(rows, hidden), full(rows, width),
        low(rows, width), full(8, width), full(8, width),
    ]
    hold = lambda a: pltpu.VMEM(a.shape, a.dtype)
    return pl.pallas_call(
        functools.partial(encode_kernel, dp_size, plan, window, min(256, rows)),
        out_shape=kept,
        in_specs=[pl.BlockSpec(memory_space=pltpu.SMEM)] + [anywhere] * 9,
        out_specs=[anywhere] * len(kept),
        scratch_shapes=gather_sems(dp_size, len(plan)) + [
            pltpu.VMEM((z, 2, *vec.shape), jnp.float32), dma((slots,)), dma((slots,)), dma, dma((2, 3)),
            *[hold(a) for a in kept[:-1]], pltpu.VMEM((rows, width), jnp.bfloat16), hold(kept[-1]),
            pltpu.VMEM((1, hidden), jnp.float32), pltpu.VMEM((rows, width), jnp.float32), dma((len(kept),)),
            pltpu.VMEM((2, 2 * rows, 128), jnp.bfloat16), dma, dma,
        ],
        compiler_params=pltpu.CompilerParams(collective_id=0, has_side_effects=True, vmem_limit_bytes=60 << 20),
        name="encode",
    )(lengths, *weights, vec, rows_in, cotangent)


class Stream:
    def __init__(self, pieces, buf, sem):
        self.copies = [pltpu.make_async_copy(piece, buf.at[i % 2], sem.at[i % 2]) for i, piece in enumerate(pieces)]
        self.buf = buf
        for copy in self.copies[:2]:
            copy.start()

    def get(self, i):
        self.copies[i].wait()
        return self.buf.at[i % 2]

    def next(self, i):
        if i + 2 < len(self.copies):
            self.copies[i + 2].start()


class Stage:
    def __init__(self, buf, sem):
        self.buf, self.sem, self.flying = buf, sem, []

    def put(self, value, dst):
        slot = len(self.flying) % 2
        if len(self.flying) >= 2:
            self.flying[-2].wait()
        self.buf[slot] = value
        self.flying.append(pltpu.make_async_copy(self.buf.at[slot], dst, self.sem.at[slot]))
        self.flying[-1].start()

    def drain(self):
        for copy in self.flying[-2:]:
            copy.wait()
        self.flying = []


def column_sum(value):
    return jnp.sum(value.astype(jnp.float32), axis=0, keepdims=True)


def decode_kernel(dp_size, plan, loads, block, length_ref, *refs):
    (qkv_in, other_in, ctx_in, lse_in, x_in, qkv_w, out_w, up_w, down_w, norm_in, unit_in, scale_in, act_in, slope_in,
     grad_in, layer_in, sums_in, vec_in) = refs[:18]
    outs, vec_outs, layer_out, input_out, parts = refs[18:24], refs[24:33], refs[33], refs[34], refs[35:38]
    scratch = refs[38:]
    got_ref, give_send, give_recv, rows_ref, layer_ref, base_ref, ctx_ref, lse_ref, cgrad_ref, sums_ref, vec_ref = scratch[:11]
    small_ref, small_out, swap_sem, load_sem, late_sem, stream_sem, grad_ref = scratch[11:18]
    small_scratch, reduce_refs = scratch[18:22], scratch[22:]
    place = Place(dp_size)
    rows, width = ctx_ref.shape
    hidden = act_in.shape[1]
    slabs, low, step = width // 128, jnp.bfloat16, 256
    half = width // 2
    early = [pltpu.make_async_copy(a, b, load_sem.at[i]) for i, (a, b) in enumerate((
        (grad_in, base_ref), (layer_in, layer_ref), (ctx_in, ctx_ref), (lse_in, lse_ref), (sums_in, sums_ref), (vec_in, vec_ref)))]
    for copy in early:
        copy.start()
    place.greet()
    moves = [SwapBack(place, a, b, swap_sem.at[i, 0], swap_sem.at[i, 1], swap_sem.at[i, 2])
             for i, (a, b) in enumerate(((layer_ref, layer_out), (rows_ref, input_out)))]
    units = reduce_units(place, (*parts, grad_ref), outs, plan, loads, reduce_refs)
    small = SumAll(place, small_ref, small_out, *small_scratch)
    steps, first = reduce_steps(units)
    clock = iter(range(first, first + len(steps)))

    def tick(count=1):
        for _ in range(count):
            for call in steps[next(clock) - first]:
                call()

    def feed_backward(act_buf, slope_buf, down_buf, up_buf, low_ref, up_low, norm_ref, norm_t, unit_ref, scale_ref, out_buf, ctx_t,
                      tall, flat):
        chunks = hidden // width
        cut = lambda ref, i: ref.at[:, pl.ds(i * width, width)]
        acts = Stream([cut(act_in, i) for i in range(chunks)], act_buf, stream_sem.at[0])
        slopes = Stream([cut(slope_in, i) for i in range(chunks)], slope_buf, stream_sem.at[1])
        downs = Stream([down_w.at[pl.ds(i * width, width)] for i in range(chunks)], down_buf, stream_sem.at[2])
        ups = Stream([cut(up_w, i) for i in range(chunks)], up_buf, stream_sem.at[3])
        others = [pltpu.make_async_copy(a, b, late_sem.at[i]) for i, (a, b) in enumerate((
            (norm_in, norm_ref), (unit_in, unit_ref), (scale_in, scale_ref), (out_w, out_buf)))]
        for copy in others:
            copy.start()
        for copy in early:
            copy.wait()
        moves[0].start()
        small_ref[...] = jnp.zeros_like(small_ref)
        small_ref[3:4, :] = sums_ref[2:3, :]
        small_ref[6:8, :] = sums_ref[0:2, :]
        low_ref[...] = base_ref[...].astype(low)
        stage = Stage(tall, stream_sem.at[4])
        each = hidden // dp_size
        for i in range(chunks):
            act = acts.get(i)
            for o in range(width // each):
                owner = i * (width // each) + o
                value = nn(act[:, o * each:(o + 1) * each].T, low_ref[...])
                stage.put(value.astype(low), parts[0].at[owner // 2, owner % 2])
            acts.next(i)
        stage.drain()
        tick(-first)
        others[0].wait()
        norm_t[...] = norm_ref[...].T
        stage = Stage(flat, stream_sem.at[4])
        shape = (place.depth, 2, width // dp_size, half)
        for i in range(chunks):
            slope, down = slopes.get(i), downs.get(i)

            def slope_part(t, carry):
                cols = pl.ds(pl.multiple_of(t * step, step), step)
                value = nt(low_ref[...], down[cols, :]) * slope[:, cols].astype(jnp.float32)
                up_low[:, cols] = value.astype(low)
                return carry

            lax.fori_loop(0, width // step, slope_part, 0)
            slopes.next(i)
            downs.next(i)
            small_ref[8 + i:9 + i, :] = column_sum(up_low[...])
            for h in range(2):
                value = nn(norm_t[...], up_low[:, h * half:(h + 1) * half]).astype(low)
                stage.put(value.reshape(shape), parts[1].at[:, :, :, pl.ds(i * width + h * half, half)])
            tick()
            up = ups.get(i)

            def back_part(t, carry):
                cols = pl.ds(pl.multiple_of(t * step, step), step)
                base_ref[:, cols] += nt(up_low[...], up[cols, :])
                return carry

            lax.fori_loop(0, width // step, back_part, 0)
            ups.next(i)
            stage.drain()
            tick()
        for copy in others[1:]:
            copy.wait()
        chunk = 128
        gain = vec_ref[4:5, :]

        def first_rows(t, carry):
            at = pl.ds(pl.multiple_of(t * chunk, chunk), chunk)
            given, unit = base_ref[at, :], unit_ref[at, :]
            e = given * gain
            mean = jnp.mean(e, axis=-1, keepdims=True)
            along = jnp.mean(e * unit, axis=-1, keepdims=True)
            grad = scale_ref[at, :][:, :1] * (e - mean - unit * along)
            base_ref[at, :] = grad
            low_ref[at, :] = grad.astype(low)
            for i, value in ((4, given * unit), (5, given), (2, grad.astype(low))):
                small_ref[i:i + 1, :] += column_sum(value)
            return carry

        lax.fori_loop(0, rows // chunk, first_rows, 0)
        ctx_t[...] = ctx_ref[...].T
        for h in range(2):
            value = nn(ctx_t[...], low_ref[:, h * half:(h + 1) * half]).astype(low)
            stage.put(value.reshape(shape), parts[2].at[:, :, :, pl.ds(h * half, half)])
        tick()

        def context_part(t, carry):
            cols = pl.ds(pl.multiple_of(t * step, step), step)
            cgrad_ref[:, cols] = nt(low_ref[...], out_buf[cols, :]).astype(low)
            return carry

        lax.fori_loop(0, width // step, context_part, 0)
        stage.drain()
        tick()

    lows = lambda *shape: pltpu.VMEM(shape, low)
    full = lambda *shape: pltpu.VMEM(shape, jnp.float32)
    pl.run_scoped(
        feed_backward, lows(2, rows, width), lows(2, rows, width), lows(2, width, width), lows(2, width, width), lows(rows, width),
        lows(rows, width), lows(rows, width), lows(width, rows), full(rows, width), full(rows, 128), lows(width, width),
        lows(width, rows), lows(2, hidden // dp_size, width), lows(2, place.depth, 2, width // dp_size, half),
    )

    def attend(qkv_ref, other_ref, x_ref, xt_ref, w_ref, d_ref, dk_ref, dv_ref, *work):
        late = [pltpu.make_async_copy(a, b, late_sem.at[i]) for i, (a, b) in enumerate((
            (qkv_in, qkv_ref), (other_in, other_ref), (x_in, x_ref), (qkv_w, w_ref)))]
        for copy in late:
            copy.start()
        ins = (qkv_ref, other_ref, ctx_ref, cgrad_ref, lse_ref)
        give = Give((place.dp, flip(place.seq, 1)), dk_ref, dv_ref, got_ref, d_ref, rows, width, (give_send, give_recv))
        key_extra(work[0], jnp.where(place.side == 0, length_ref[0], length_ref[1]), place.core, 2 * rows, 0)
        late[2].wait()
        xt_ref[...] = x_ref[...].T
        late[0].wait()
        late[1].wait()

        def weight_part(pair):
            for which in range(3):
                cols = pl.ds(which * width + pair * step, step)
                value = nn(xt_ref[...], d_ref[:, cols]).astype(low)
                grad_ref[:, :, :, pl.ds(pair * width + which * step, step)] = value.reshape(*grad_ref.shape[:3], step)

        before, amid = [], []
        for k in range(slabs):
            before.append(steps[next(clock) - first])
            amid.append(steps[next(clock) - first] if k != slabs - 2 else [])

        def when_slab(j, chosen):
            for k, calls in enumerate(chosen):
                if calls:
                    @pl.when(j == k)
                    def _():
                        for call in calls:
                            call()

        def slab_step(j, carry):
            @pl.when(j >= 2)
            def _():
                give.take(j - 2)

            when_slab(j, [[functools.partial(weight_part, k // 2 - 1)] if k % 2 and k > 2 else [] for k in range(slabs)])
            when_slab(j, before)
            slot = lax.rem(j, 2)
            backward_slab(j, block, ins, work, dk_ref.at[slot], dv_ref.at[slot], d_ref, lambda: when_slab(j, amid))
            give.start(j)
            return carry

        lax.fori_loop(0, slabs, slab_step, 0)
        for j in range(slabs - 2, slabs):
            give.take(j)
        weight_part(slabs // 2 - 1)
        for i, base in ((0, 0), (1, 2 * width)):
            small_ref[i:i + 1, :] = column_sum(d_ref[:, pl.ds(base, width)])
        small.begin()
        tick()
        late[3].wait()

        def input_part(t, carry):
            cols = pl.ds(pl.multiple_of(t * step, step), step)
            rows_ref[:, cols] = (base_ref[:, cols] + nt(d_ref[...], w_ref[cols, :])).astype(low)
            return carry

        lax.fori_loop(0, width // step, input_part, 0)

    pl.run_scoped(
        attend, lows(rows, 3 * width), lows(rows, 2 * width), lows(rows, width), lows(width, rows), lows(width, 3 * width),
        lows(rows, 3 * width), full(2, 2 * rows, 128), full(2, 2 * rows, 128), *backward_work(rows),
    )
    moves[1].start()
    for i, now in enumerate(clock):
        for call in steps[now - first]:
            call()
        if i % 2 and i < 8:
            small.advance(i // 2)
    small.finish()
    share = width // dp_size
    turned = pltpu.roll(small_out[0:8, :], lax.rem(width - place.dp * share, width), 1)
    for i in range(8):
        vec_outs[i][...] = turned[i:i + 1, 0:share]
    wide = small_out[pl.ds(8 + place.z, 1), :]
    vec_outs[8][...] = jnp.where(place.y == 0, wide[:, :width // 2], wide[:, width // 2:])
    for move in moves:
        move.wait()


def decode(dp_size, lengths, ins, out_shapes, part_shapes, plan, rows_shape):
    x = ins[4]
    rows, width = x.shape
    z, loads = dp_size // 2, sum(1 for p in plan if p[0] < len(part_shapes))
    slabs, dma = width // 128, pltpu.SemaphoreType.DMA
    anywhere, vmem = pl.BlockSpec(memory_space=pl.ANY), pl.BlockSpec(memory_space=pltpu.VMEM)
    low = lambda *shape: pltpu.VMEM(shape, jnp.bfloat16)
    full = lambda *shape: pltpu.VMEM(shape, jnp.float32)
    sds = lambda shape, dtype: jax.ShapeDtypeStruct(shape, dtype)
    return pl.pallas_call(
        functools.partial(decode_kernel, dp_size, plan, loads, min(512, rows)),
        out_shape=[sds(s, jnp.float32) for s in out_shapes] + [sds((1, width // dp_size), jnp.float32)] * 8
        + [sds((1, width // 2), jnp.float32)] + [sds(rows_shape, jnp.bfloat16)] * 2 + [sds(s, jnp.bfloat16) for s in part_shapes],
        in_specs=[pl.BlockSpec(memory_space=pltpu.SMEM)] + [anywhere] * len(ins),
        out_specs=[anywhere] * 6 + [vmem] * 9 + [anywhere] * (2 + len(part_shapes)),
        scratch_shapes=[
            full(slabs, 2, rows, 128), dma((slabs, 2)), dma((slabs, 2)), low(rows, width), low(rows, width), full(rows, width),
            low(rows, width), full(rows, 128), low(rows, width), full(8, width), full(8, width),
            full(16, width), full(16, width), dma((2, 3)), dma((6,)), dma((4,)), dma((5, 2)), low(z, 2, plan[0][2], 3 * width),
            full(4, 16, width), full(z + 2, 16, width), dma((z + 2,)), dma((z + 2,)),
        ] + reduce_scratch(dp_size, len(plan), loads, plan[0][2], plan[0][4]),
        compiler_params=pltpu.CompilerParams(collective_id=3, has_side_effects=True, vmem_limit_bytes=62 << 20),
        name="decode",
    )(lengths, *ins)


def settle_kernel(count, *refs):
    srcs, dsts, bufs, sem = refs[:count], refs[count:2 * count], refs[2 * count:3 * count], refs[3 * count]
    gets = [pltpu.make_async_copy(a, b, sem.at[0, i]) for i, (a, b) in enumerate(zip(srcs, bufs))]
    puts = [pltpu.make_async_copy(a.at[0] if len(a.shape) > len(b.shape) else a, b, sem.at[1, i])
            for i, (a, b) in enumerate(zip(bufs, dsts))]
    for get in gets:
        get.start()
    for get, put in zip(gets, puts):
        get.wait()
        put.start()
    for put in puts:
        put.wait()


def settle(arrays):
    count = len(arrays)
    anywhere = pl.BlockSpec(memory_space=pl.ANY)
    shape = lambda a: a.shape[1:] if a.shape[0] == 1 else a.shape
    return pl.pallas_call(
        functools.partial(settle_kernel, count),
        out_shape=[jax.ShapeDtypeStruct(shape(a), a.dtype) for a in arrays],
        in_specs=[anywhere] * count,
        out_specs=[anywhere] * count,
        scratch_shapes=[pltpu.VMEM(a.shape, a.dtype) for a in arrays] + [pltpu.SemaphoreType.DMA((2, count))],
        compiler_params=pltpu.CompilerParams(vmem_limit_bytes=61 << 20),
        name="settle",
    )(*arrays)


def matmul(a, b):
    return jnp.dot(a, b, preferred_element_type=jnp.float32)


def inner_rows(a, b):
    return lax.dot_general(a, b, (((0,), (0,)), ((), ())), preferred_element_type=jnp.float32)


def times_transposed(a, b):
    return lax.dot_general(a, b, (((1,), (1,)), ((), ())), preferred_element_type=jnp.float32)


def swap_rows(rows):
    side = lax.div(lax.axis_index("seq"), 2)
    size = lax.axis_size("seq")
    got = lax.ppermute(lax.dynamic_index_in_dim(rows, 1 - side, 0, False), "seq", [(i, i ^ 2) for i in range(size)])
    kept = lax.dynamic_index_in_dim(rows, side, 0, False)
    first = jnp.where(side == 0, kept, got)
    second = jnp.where(side == 0, got, kept)
    return jnp.concatenate([first, second], axis=0)


def swap_rows_back(rows):
    side = lax.div(lax.axis_index("seq"), 2)
    size = lax.axis_size("seq")
    blocks = rows.reshape(2, rows.shape[0] // 2, rows.shape[1])
    got = lax.ppermute(lax.dynamic_index_in_dim(blocks, 1 - side, 0, False), "seq", [(i, i ^ 2) for i in range(size)])
    kept = lax.dynamic_index_in_dim(blocks, side, 0, False)
    return jnp.stack([jnp.where(side == 0, kept, got), jnp.where(side == 0, got, kept)])


def pack_vectors(narrow, wide):
    rows = jnp.stack([v.astype(jnp.float32) for v in narrow])
    rows = jnp.pad(rows, ((0, 0), (0, 128 - rows.shape[1])))
    more = wide.astype(jnp.float32).reshape(-1, 128)
    both = jnp.concatenate([rows, more], axis=0)
    return jnp.pad(both, ((0, 16 - both.shape[0]), (0, 0)))


def norm_stats(hidden):
    row_mean = jnp.mean(hidden, axis=-1, keepdims=True)
    centred = hidden - row_mean
    row_var = jnp.mean(centred * centred, axis=-1, keepdims=True)
    scale = lax.rsqrt(row_var + eps_norm)
    return centred * scale, scale


def norm_backward(grad, gain, unit, scale):
    e = grad * gain
    first = jnp.mean(e, axis=-1, keepdims=True)
    second = jnp.mean(e * unit, axis=-1, keepdims=True)
    return scale * (e - first - unit * second)


def col_sum(value):
    return jnp.sum(value, axis=0)


def local(
    inputs, lengths, query_weight, key_weight, value_weight, output_weight, up_weight, down_weight,
    query_bias, value_bias, output_bias, up_bias, down_bias, first_gain, first_shift, second_gain, second_shift, cotangent,
):
    dp_size = lax.axis_size("dp")
    groups, length, width = inputs.shape
    shard = query_weight.shape[0]
    fast = dp_size == 8 and shard == 96 and groups == 2
    rows = groups * length
    seq = lax.axis_index("seq")
    core, side = lax.rem(seq, 2), lax.div(seq, 2)
    narrow = [query_bias, value_bias, output_bias, down_bias, first_gain, first_shift, second_gain, second_shift]
    hidden_width = up_weight.shape[1]
    if fast:
        u = shard
        half = width // 2
        cuts = [(i, 0, 0, 0, width * i) for i in (1, 2, 0)] + [(3, 1, 0, 0, 0)]
        cuts += [(4, 2, 0, width * j, width * j) for j in range(hidden_width // width)]
        plan = [(s, d, row, u, col + half * h, half, to + half * h) for s, d, row, col, to in cuts for h in range(2)]
        plan += [(5, 3, u * j, u, half * h, half, half * h) for h in range(2) for j in range(down_weight.shape[0] // u)]
        plan = [(*p, i < len(plan) - 9) for i, p in enumerate(plan)]
        weights = [query_weight, key_weight, value_weight, output_weight, up_weight, down_weight]
        shapes = [(u, 3 * width), (u, width), (u, hidden_width), (down_weight.shape[0], width)]
        (qkv_w, out_w, up_w, down_w, flat_in, qkv, context, lse, other, first_norm, unit_1, scale_1, hidden_act, slope,
         second_sum_grad, layer_rows, sums, flat_vec) = encode(
            dp_size, lengths, weights, shapes, plan, pack_vectors(narrow, up_bias), inputs, cotangent
        )
        qkv_w, out_w = qkv_w.reshape(width, 3 * width), out_w.reshape(width, width)
        up_w, down_w = up_w.reshape(width, hidden_width), down_w.reshape(hidden_width, width)
    else:
        gather = lambda a: lax.all_gather(a, "dp", axis=0, tiled=True)
        qkv_w = gather(jnp.concatenate([query_weight, key_weight, value_weight], axis=1))
        out_w, up_w, down_w = gather(output_weight), gather(up_weight), gather(down_weight)
        flat_vec = jnp.stack([gather(v.astype(jnp.float32)) for v in narrow])
        bias_up = gather(up_bias.astype(jnp.float32))
        flat_in, flat_cot = swap_rows(inputs), swap_rows(cotangent)
    bias_q, bias_v, bias_out, bias_down, gain_1, shift_1, gain_2, shift_2 = [flat_vec[i] for i in range(8)]
    if not fast:
        bias_qkv = jnp.concatenate([bias_q, jnp.zeros_like(bias_q), bias_v])
        qkv = (matmul(flat_in, qkv_w) + bias_qkv).astype(jnp.bfloat16)
        context, lse, other = attend_forward(lengths, qkv)
        first_sum = flat_in.astype(jnp.float32) + (matmul(context, out_w) + bias_out)
        unit_1, scale_1 = norm_stats(first_sum)
        first_norm = (unit_1 * gain_1 + shift_1).astype(jnp.bfloat16)
        up_pre = matmul(first_norm, up_w) + bias_up
        below = 0.5 + 0.5 * lax.erf(up_pre * (0.5 ** 0.5))
        hidden_act = (up_pre * below).astype(jnp.bfloat16)
        slope = (below + up_pre * jnp.exp(-0.5 * up_pre * up_pre) * 0.3989422804014327).astype(jnp.bfloat16)
        down_out = matmul(hidden_act, down_w) + bias_down
        second_sum = first_norm.astype(jnp.float32) + down_out
        unit_2, scale_2 = norm_stats(second_sum)
        layer_rows = (unit_2 * gain_2 + shift_2).astype(jnp.bfloat16)

        row = jnp.arange(rows)
        position = lax.rem(row, length) + (core + 2 * lax.div(row, length)) * length
        live = (position < lengths[side]).astype(jnp.float32)
        grad_out = flat_cot.astype(jnp.float32) * live[:, None]
        second_gain_grad, second_shift_grad = col_sum(grad_out * unit_2), col_sum(grad_out)
        second_sum_grad = norm_backward(grad_out, gain_2, unit_2, scale_2)
        down_bias_grad = col_sum(second_sum_grad.astype(jnp.bfloat16).astype(jnp.float32))
    low = jnp.bfloat16
    if not fast:
        down_low = second_sum_grad.astype(jnp.bfloat16)
        down_w_grad = inner_rows(hidden_act, down_low).astype(low)
        up_low = (times_transposed(down_low, down_w) * slope.astype(jnp.float32)).astype(low)
        up_w_grad = inner_rows(first_norm, up_low).astype(low)
        up_bias_grad = col_sum(up_low.astype(jnp.float32))
        norm_grad = second_sum_grad + times_transposed(up_low, up_w)
        first_gain_grad, first_shift_grad = col_sum(norm_grad * unit_1), col_sum(norm_grad)
        first_sum_grad = norm_backward(norm_grad, gain_1, unit_1, scale_1)
        attended_low = first_sum_grad.astype(low)
        out_w_grad = inner_rows(context, attended_low).astype(low)
        out_bias_grad = col_sum(attended_low.astype(jnp.float32))
        context_grad = times_transposed(attended_low, out_w).astype(low)
        qkv_low = attend_backward(lengths, qkv, other, context, context_grad, lse)
        qkv_w_grad = inner_rows(flat_in, qkv_low)
        qkv_bias_grad = col_sum(qkv_low.astype(jnp.float32))
        input_rows = (first_sum_grad + times_transposed(qkv_low, qkv_w)).astype(low)
        small = jnp.concatenate([
            jnp.stack([qkv_bias_grad[:width], qkv_bias_grad[2 * width:], out_bias_grad, down_bias_grad, first_gain_grad,
                       first_shift_grad, second_gain_grad, second_shift_grad]),
            up_bias_grad.reshape(-1, width),
        ], axis=0)
    me = lax.axis_index("dp")
    if fast:
        plan = [(0, u * j, u, half * h, half, u * j, [(0, half, 5, half * h)]) for j in range(down_weight.shape[0] // u) for h in range(2)]
        plan += [(1, 0, u, half * i, half, 0, [(0, half, 4, half * i)]) for i in range(hidden_width // half)]
        plan += [(2, 0, u, half * h, half, 0, [(0, half, 3, half * h)]) for h in range(2)]
        for p in range(width // 256):
            plan.append((3, 0, u, width * p, half, 0, [(0, 256, 0, 256 * p), (256, 128, 1, 256 * p)]))
            plan.append((3, 0, u, width * p + half, half, 0, [(0, 128, 1, 256 * p + 128), (128, 256, 2, 256 * p)]))
        plan = [(*p, 1 <= i < len(plan) - 5) for i, p in enumerate(plan)]
        shapes = [(u, width)] * 4 + [up_weight.shape, down_weight.shape]
        halves_of = lambda shape: (dp_size // 2, 2, *shape)
        part_shapes = [halves_of(down_weight.shape), halves_of(up_weight.shape), halves_of(output_weight.shape)]
        ins = (qkv, other, context, lse, flat_in, qkv_w, out_w, up_w, down_w, first_norm, unit_1, scale_1, hidden_act, slope,
               second_sum_grad, layer_rows, sums, flat_vec)
        results = decode(dp_size, lengths, ins, shapes, part_shapes, plan, (groups, length, width))
        mine, layer_out, input_grad = results[:15], results[15], results[16]
        layer_out, input_grad, *mine = settle((layer_out, input_grad, *mine))
        weight_grads, mine = mine[:6], mine[6:]
        up_mine = mine.pop()
    else:
        scatter = lambda a: lax.psum(lax.psum_scatter(a.astype(jnp.float32), "dp", scatter_dimension=0, tiled=True), "seq")
        qkv_g = scatter(qkv_w_grad)
        weight_grads = [qkv_g[:, :width], qkv_g[:, width:2 * width], qkv_g[:, 2 * width:]]
        weight_grads += [scatter(out_w_grad), scatter(up_w_grad), scatter(down_w_grad)]
        small = lax.psum(small, ("dp", "seq"))
        layer_out, input_grad = swap_rows_back(layer_rows), swap_rows_back(input_rows)
        part = query_bias.shape[0]
        mine = list(lax.dynamic_slice(small, (0, me * part), (8, part)))
        up_part = up_bias.shape[0]
        up_mine = lax.dynamic_slice(small[8:8 + hidden_width // width].reshape(hidden_width), (me * up_part,), (up_part,))
    return (layer_out, input_grad, *weight_grads, mine[0], mine[1], mine[2], up_mine, *mine[3:8])


def solution(mesh):
    rows, matrix, vector = P("dp", "seq", None), P("dp", None), P("dp")
    return jax.shard_map(
        local,
        mesh=mesh,
        in_specs=(rows, vector, *[matrix] * 6, *[vector] * 9, rows),
        out_specs=(rows, rows, *[matrix] * 6, *[vector] * 9),
        check_vma=False,
    )
```
